128 devices in a mesh: dp: 4 (over x_lo, core), expert: 32 (over y, x_hi, z).
Axes of the slice: x: 4 (x_hi: 2, x_lo: 2; x = x_hi * 2 + x_lo), y: 4, z: 4, core: 2. Of those that a mesh axis runs over, the one named last changes fastest.
Arguments:
- hidden_in: bfloat16 [16384, 2048], P(('dp', 'expert')), may hold values from -6 to 6
- attn_gain: float32 [2048], replicated, may hold values from 0.1 to 1.9
- query_key_value_weight: bfloat16 [2048, 2560], P('expert'), may hold values from -0.125 to 0.125
- q_gain: float32 [128], replicated, may hold values from 0.1 to 1.9
- key_norm_gain: float32 [128], replicated, may hold values from 0.1 to 1.9
- w_out: bfloat16 [2048, 2048], P('expert'), may hold values from -0.125 to 0.125
- moe_gain: float32 [2048], replicated, may hold values from 0.1 to 1.9
- w_gate_up: bfloat16 [128, 2048, 1536], P(('dp', 'expert')), may hold values from -0.125 to 0.125
- w_down: bfloat16 [128, 768, 2048], P(('dp', 'expert')), may hold values from -0.21875 to 0.21875
- kv_pool: bfloat16 [32, 2, 128, 2, 128], P('dp'), may hold values from -160 to 160
- page_table: int32 [32], replicated, may hold values from 0 to 31, each once
- suffix_lengths: int32 [4, 4], replicated, may hold values from 1 to 2560, 4096 in all within a row
- request_group: int32 [4, 4], replicated, may hold values from 0 to 1
- expert_ids: int32 [16384, 8], P(('dp', 'expert')), may hold values from 0 to 127, all different within a row; in each aligned block of 128 rows (0 to 127, 128 to 255, ...) at most 12 rows name the same one
- gate_weights: float32 [16384, 8], P(('dp', 'expert')), may hold values from 0.05 to 0.3
Outputs:
- hidden_out: bfloat16 [16384, 2048], P(('dp', 'expert'))
- suffix_cache: bfloat16 [16384, 512], P(('dp', 'expert'))
The draws below stay inside these ranges and needn't reach their ends.
Inputs may be any that keep to these rules, and one draw needn't show every extreme that they name: page_table holds each pool page once. `suffix_lengths`: each row sums to 4096; the largest of each row is exactly 2560. `expert_ids`: a token's 8 experts differ; among the 128 rows of one device no expert is named more than 12 times, and that many times in some device.
All inputs are finite; a program needn't handle non-finite values.
Results may differ from the reference program's by a relative error of at most 0.01.
The reference program's roundings to bfloat16 on the way count: a program that leaves them out, or rounds other values in their place, can miss the bound.
Values may be sent and summed in bfloat16 or wider, within the bound.
A program may use at most 256 MiB of HBM per device.

```python
import math
import jax
import jax.numpy as jnp
import numpy as np
from jax import lax

MODEL_WIDTH = 2048
FF = 768
QUERY_HEADS = 16
KEY_VALUE_HEADS = 2
HEAD_SIZE = 128
TOPK = 8
TOK_DEV = 128
PREFIX_TOKENS = 2048
PAGE_TOKENS = 128
PREFIX_GROUPS = 2
REQ_ROW = 4
SUFFIX_TOKENS = 4096
TOKENS = 16384
SUFFIX_MOST = 2560
POOL_PAGES = 32
EXPERTS = 128
CAP = 12
N_DP = 4
N_EXPERT = 32


def draw_kv_pool(key, part):
    first = jax.random.fold_in(jax.random.fold_in(key, 11), 0)
    array_shape = (POOL_PAGES, 2, PAGE_TOKENS, KEY_VALUE_HEADS, HEAD_SIZE)
    base = jnp.clip(jax.random.normal(first, array_shape, jnp.float32), -4.0, 4.0)
    return base.astype(jnp.bfloat16)


def set_ends(drawn, rng, smallest, largest):
    spot = [jax.random.randint(jax.random.fold_in(rng, axis), (), 0, length) for axis, length in enumerate(drawn.shape)]
    main_axis = drawn.shape.index(max(drawn.shape))
    next_to = spot[:main_axis] + [(spot[main_axis] + 1) % drawn.shape[main_axis]] + spot[main_axis + 1:]
    return drawn.at[tuple(spot)].set(smallest).at[tuple(next_to)].set(largest)


def block_levels(own_key, shape, shards, low, high):
    def one(dim, blocks):
        draws = jax.random.uniform(jax.random.fold_in(jax.random.fold_in(own_key, 6), dim), (blocks,), jnp.float32, low / len(shards), high / len(shards))
        return jnp.repeat(jnp.exp(draws), shape[dim] // blocks).reshape((-1,) + (1,) * (len(shape) - dim - 1))

    factor_of = one(*shards[0])
    for cut in shards[1:]:
        factor_of = factor_of * one(*cut)
    return factor_of


def profile(count, total, most, slope):
    weights = [(1 << 20) // math.isqrt(rank ** slope) + 1 for rank in range(2, count + 1)]
    spare, given = total - most - (count - 1), [1] * (count - 1)
    while spare > 0:
        movable = [i for i in range(count - 1) if given[i] < most]
        whole, budget = sum([weights[i] for i in movable]), spare
        for i in movable:
            more = min(most - given[i], max(1, budget * weights[i] // whole), spare)
            given[i] = given[i] + more
            spare = spare - more
    return np.array([most] + given)


def uneven(stream_key, amount, total, most, slope):
    if amount == 2:
        one = jax.random.randint(stream_key, (), max(1, total - most), min(most, total - 1) + 1)
        return jnp.stack([one, total - one])
    tallies = jnp.asarray(profile(amount, total, most, slope), jnp.int32)
    pairs = (amount - 1) // 2
    source_of, taker = tallies[1:1 + 2 * pairs:2], tallies[2:2 + 2 * pairs:2]
    slack = jnp.minimum(source_of - 1, most - taker)
    moved = jax.random.randint(jax.random.fold_in(stream_key, 1), (pairs,), 0, 1 << 20) % (slack + 1)
    tallies = tallies.at[1:1 + 2 * pairs:2].set(source_of - moved).at[2:2 + 2 * pairs:2].set(taker + moved)
    return tallies[jax.random.permutation(jax.random.fold_in(stream_key, 2), amount)]


def routed_block(key, own, number, rows, amount, top, reach, lean):
    order = jax.random.permutation(key, amount)
    crowded, common = load_shares(amount, rows * top, reach, lean, True), load_shares(amount, rows * top, reach, lean, False)
    places = jnp.arange(amount)

    def named(tallies, turn):
        used = int((tallies > 0).sum())
        fixed = max(1, used // 4)
        shifted = fixed + (places - fixed + turn * (used - fixed)) % max(1, amount - fixed)
        return jnp.zeros((amount,), jnp.int32).at[order[jnp.where(places < fixed, places, shifted)]].set(jnp.asarray(tallies, jnp.int32))

    tallies = jnp.where(number % 4 == 0, named(crowded, number // 4), named(common, number - number // 4 - 1))
    mixed = jax.random.permutation(jax.random.fold_in(own, 3), amount)
    giver, taker = mixed[0:amount // 2 * 2:2], mixed[1:amount // 2 * 2:2]
    margin = jnp.minimum(tallies[giver] - 1, reach - tallies[taker]) // 2
    margin = jnp.where((giver == order[0]) | (taker == order[0]) | (tallies[taker] == 0), 0, jnp.maximum(margin, 0))
    shifted = jax.random.randint(jax.random.fold_in(own, 4), (amount // 2,), 0, 1 << 20) % (margin + 1)
    tallies = tallies.at[giver].add(-shifted).at[taker].add(shifted)
    labels = jnp.searchsorted(jnp.cumsum(tallies), jnp.arange(rows * top), side="right").astype(jnp.int32)
    table = labels.reshape(top, rows).T
    table = table[jax.random.permutation(jax.random.fold_in(own, 1), rows)]
    turn = jax.random.randint(jax.random.fold_in(own, 2), (rows, 1), 0, top)
    return jnp.take_along_axis(table, (jnp.arange(top)[None, :] + turn) % top, axis=1)


def load_shares(count, total, bound, slope, full):
    weights = [(1 << 20) // math.isqrt(rank ** slope) + 1 for rank in range(1, count + 1)]
    largest = bound if full else min(bound, max(-(-total // count), total * weights[0] // sum(weights)))
    least = 1 if total - largest >= count - 1 else 0
    holding, surplus = [largest] + [least] * (count - 1), total - largest - least * (count - 1)
    while surplus > 0:
        movable = [i for i in range(1, count) if holding[i] < largest] or [i for i in range(1, count) if holding[i] < bound]
        mass, left = sum([weights[i] for i in movable]), surplus
        for i in movable:
            addition = min(bound - holding[i], max(1, left * weights[i] // mass), surplus)
            holding[i] = holding[i] + addition
            surplus = surplus - addition
    return np.array(holding)


def gaussian(stream_key, shape, spread, reach, pieces=(), kind=jnp.bfloat16):
    drawn = jax.random.normal(stream_key, shape, jnp.float32) * spread
    if len(pieces) > 0:
        drawn = block_levels(stream_key, shape, pieces, -0.22, 0.18) * drawn
    return jnp.clip(drawn, min=-reach, max=reach).astype(kind)


def setup_inputs(seed: int = 0) -> dict:
    key_list = jax.random.split(jax.random.key(seed), 16)
    hidden_in = gaussian(key_list[0], (TOKENS, MODEL_WIDTH), 1.0, 6.0, ((0, 128),))
    attn_gain = jnp.clip(1.0 + 0.18 * jax.random.normal(key_list[1], (MODEL_WIDTH,), jnp.float32), 0.1, 1.9)
    query_key_value_weight = gaussian(key_list[2], (MODEL_WIDTH, (QUERY_HEADS + 2 * KEY_VALUE_HEADS) * HEAD_SIZE), MODEL_WIDTH ** -0.5, 0.125, ((0, 32),))
    q_gain = jnp.clip(1.0 + 0.18 * jax.random.normal(key_list[3], (HEAD_SIZE,), jnp.float32), 0.1, 1.9)
    key_norm_gain = jnp.clip(1.0 + 0.18 * jax.random.normal(key_list[4], (HEAD_SIZE,), jnp.float32), 0.1, 1.9)
    w_out = gaussian(key_list[5], (QUERY_HEADS * HEAD_SIZE, MODEL_WIDTH), (QUERY_HEADS * HEAD_SIZE) ** -0.5, 0.125, ((0, 32),))
    moe_gain = jnp.clip(1.0 + 0.18 * jax.random.normal(key_list[6], (MODEL_WIDTH,), jnp.float32), 0.1, 1.9)
    w_gate_up = gaussian(key_list[7], (EXPERTS, MODEL_WIDTH, 2 * FF), MODEL_WIDTH ** -0.5, 0.125, ((0, 128),))
    w_down = gaussian(key_list[8], (EXPERTS, FF, MODEL_WIDTH), FF ** -0.5, 0.21875, ((0, 128),))
    kv_pool = draw_kv_pool(jax.random.fold_in(key_list[15], 71), 0)
    page_table = jax.random.permutation(key_list[10], POOL_PAGES).astype(jnp.int32)
    suffix_lengths = jax.vmap(lambda own: uneven(own, REQ_ROW, SUFFIX_TOKENS, SUFFIX_MOST, 2))(jax.random.split(key_list[11], N_DP)).reshape((N_DP, REQ_ROW)).astype(jnp.int32)
    request_group = set_ends(jax.random.randint(key_list[12], (N_DP, REQ_ROW), 0, PREFIX_GROUPS), jax.random.fold_in(key_list[12], 1), 0, PREFIX_GROUPS - 1).astype(jnp.int32)
    expert_ids_keys = jax.random.split(jax.random.fold_in(key_list[13], 1), TOKENS // TOK_DEV)
    expert_ids_turns = jax.random.permutation(jax.random.fold_in(key_list[13], 3), TOKENS // TOK_DEV)
    expert_ids = jax.vmap(lambda own, number: routed_block(jax.random.fold_in(key_list[13], 2), own, number, TOK_DEV, EXPERTS, TOPK, CAP, 2))(expert_ids_keys, expert_ids_turns).reshape((TOKENS, TOPK))
    gate_weights = jnp.clip(0.05 + 0.25 * jax.random.uniform(key_list[14], (TOKENS, TOPK), jnp.float32) ** block_levels(key_list[14], (TOKENS, TOPK), ((0, 128),), -0.2, 0.2), 0.05, 0.3)
    return {"hidden_in": hidden_in, "attn_gain": attn_gain, "query_key_value_weight": query_key_value_weight, "q_gain": q_gain, "key_norm_gain": key_norm_gain, "w_out": w_out, "moe_gain": moe_gain, "w_gate_up": w_gate_up, "w_down": w_down, "kv_pool": kv_pool, "page_table": page_table, "suffix_lengths": suffix_lengths, "request_group": request_group, "expert_ids": expert_ids, "gate_weights": gate_weights}


eps = 1e-06
theta = 1000000.0

def root_mean_scale(value_rows, gain):
    value_rows = value_rows.astype(jnp.float32)
    return value_rows * lax.rsqrt(lax.optimization_barrier(jnp.mean(value_rows * value_rows, axis=-1, keepdims=True)) + eps) * gain

def rotary_apply(value_rows, token_positions):
    half = value_rows.shape[-1] // 2
    freqs = theta ** (-jnp.arange(half, dtype=jnp.float32) / half)
    angles = token_positions.astype(jnp.float32)[:, None] * freqs[None, :]
    cosine = jnp.cos(angles)[:, None, :]
    sine = jnp.sin(angles)[:, None, :]
    first = value_rows[..., :half]
    second_split = value_rows[..., half:]
    return jnp.concatenate([first * cosine - second_split * sine, second_split * cosine + first * sine], axis=-1)

def layout(lengths_row, index):
    ends = jnp.cumsum(lengths_row).astype(jnp.int32)
    starts = (ends - lengths_row).astype(jnp.int32)
    request = lax.optimization_barrier(jnp.sum((index[:, None] >= ends[None, :]).astype(jnp.int32), axis=1)).astype(jnp.int32)
    chosen = request[:, None] == jnp.arange(lengths_row.shape[0], dtype=jnp.int32)[None, :]
    offset = (index - lax.optimization_barrier(jnp.sum(jnp.where(chosen, starts[None, :], 0), axis=1))).astype(jnp.int32)
    return (request, offset, chosen)

def expert_rows(rows, gate_up, down):
    both = jnp.dot(rows, gate_up, preferred_element_type=jnp.float32)
    half = both.shape[1] // 2
    act = (jax.nn.silu(both[:, :half]) * both[:, half:]).astype(jnp.bfloat16)
    return jnp.dot(act, down, preferred_element_type=jnp.float32).astype(jnp.bfloat16)

def reference(hidden_in, attn_gain, query_key_value_weight, q_gain, key_norm_gain, w_out, moe_gain, w_gate_up, w_down, kv_pool, page_table, suffix_lengths, request_group, expert_ids, gate_weights):
    head_split = QUERY_HEADS // KEY_VALUE_HEADS
    scale = 1.0 / math.sqrt(HEAD_SIZE)
    normed = root_mean_scale(hidden_in, attn_gain).astype(jnp.bfloat16)
    qkv = jnp.dot(normed, query_key_value_weight, preferred_element_type=jnp.float32)
    query_width = QUERY_HEADS * HEAD_SIZE
    key_value_width = KEY_VALUE_HEADS * HEAD_SIZE
    page_list = kv_pool[page_table]
    cached_prefix_key = page_list[:, 0].reshape(PREFIX_GROUPS * PREFIX_TOKENS, KEY_VALUE_HEADS, HEAD_SIZE)
    cached_prefix_value = page_list[:, 1].reshape(PREFIX_GROUPS * PREFIX_TOKENS, KEY_VALUE_HEADS, HEAD_SIZE)
    prefix_group = (jnp.arange(PREFIX_GROUPS * PREFIX_TOKENS, dtype=jnp.int32) // PREFIX_TOKENS).astype(jnp.int32)
    index = jnp.arange(SUFFIX_TOKENS, dtype=jnp.int32)
    block_slice = math.gcd(SUFFIX_TOKENS, 512)
    blocks = SUFFIX_TOKENS // block_slice
    mixed_rows = []
    cache_rows = []
    for row in range(N_DP):
        request, offset, chosen = layout(suffix_lengths[row], index)
        qgroup = lax.optimization_barrier(jnp.sum(jnp.where(chosen, request_group[row][None, :], 0), axis=1)).astype(jnp.int32)
        token_positions = PREFIX_TOKENS + offset
        part = qkv[row * SUFFIX_TOKENS:(row + 1) * SUFFIX_TOKENS]
        queries = rotary_apply(root_mean_scale(part[:, :query_width].reshape(SUFFIX_TOKENS, QUERY_HEADS, HEAD_SIZE), q_gain), token_positions).astype(jnp.bfloat16)
        key_rows = rotary_apply(root_mean_scale(part[:, query_width:query_width + key_value_width].reshape(SUFFIX_TOKENS, KEY_VALUE_HEADS, HEAD_SIZE), key_norm_gain), token_positions).astype(jnp.bfloat16)
        value_rows = part[:, query_width + key_value_width:].reshape(SUFFIX_TOKENS, KEY_VALUE_HEADS, HEAD_SIZE).astype(jnp.bfloat16)
        cache_rows.append(jnp.concatenate([key_rows.reshape(SUFFIX_TOKENS, key_value_width), value_rows.reshape(SUFFIX_TOKENS, key_value_width)], axis=1))
        key_all = lax.optimization_barrier(jnp.concatenate([cached_prefix_key, key_rows], axis=0)).astype(jnp.float32)
        value_all = lax.optimization_barrier(jnp.concatenate([cached_prefix_value, value_rows], axis=0)).astype(jnp.float32)
        key_group = jnp.concatenate([prefix_group, jnp.full((SUFFIX_TOKENS,), -1, jnp.int32)])
        key_request = jnp.concatenate([jnp.full((PREFIX_GROUPS * PREFIX_TOKENS,), -1, jnp.int32), request])
        key_index = jnp.concatenate([jnp.zeros((PREFIX_GROUPS * PREFIX_TOKENS,), jnp.int32), index])

        def attend_block(args):
            query_block, req_block, idx_block, grp_block = args
            query_float = lax.optimization_barrier(query_block).astype(jnp.float32).reshape(block_slice, KEY_VALUE_HEADS, head_split, HEAD_SIZE)
            scores = jnp.einsum('qkgd,skd->kgqs', query_float, key_all) * scale
            mask = (key_group[None, :] == grp_block[:, None]) | (key_request[None, :] == req_block[:, None]) & (key_index[None, :] <= idx_block[:, None])
            scores = jnp.where(mask[None, None], scores, -jnp.inf)
            top = lax.optimization_barrier(jnp.max(scores, axis=-1, keepdims=True))
            weights = jnp.exp(scores - top)
            total = lax.optimization_barrier(jnp.sum(weights, axis=-1))
            rounded = lax.optimization_barrier(weights.astype(jnp.bfloat16)).astype(jnp.float32)
            mixed = jnp.einsum('kgqs,skd->qkgd', rounded, value_all) / jnp.transpose(total, (2, 0, 1))[..., None]
            return mixed.reshape(block_slice, query_width).astype(jnp.bfloat16)
        mixed = lax.map(attend_block, (queries.reshape(blocks, block_slice, QUERY_HEADS, HEAD_SIZE), request.reshape(blocks, block_slice), index.reshape(blocks, block_slice), qgroup.reshape(blocks, block_slice)))
        mixed_rows.append(mixed.reshape(SUFFIX_TOKENS, query_width))
    attended = jnp.concatenate(mixed_rows, axis=0)
    suffix_cache = jnp.concatenate(cache_rows, axis=0)
    mid = (hidden_in.astype(jnp.float32) + jnp.dot(attended, w_out, preferred_element_type=jnp.float32)).astype(jnp.bfloat16)
    moe_in = root_mean_scale(mid, moe_gain).astype(jnp.bfloat16)
    flat = expert_ids.reshape(-1)
    routes = flat.shape[0]
    owner = (jnp.arange(routes, dtype=jnp.int32) // TOPK).astype(jnp.int32)
    order = jnp.argsort(flat, stable=True).astype(jnp.int32)
    counts = jax.ops.segment_sum(jnp.ones((routes,), jnp.int32), flat, num_segments=EXPERTS).astype(jnp.int32)
    starts = (jnp.cumsum(counts) - counts).astype(jnp.int32)
    most = CAP * N_DP * N_EXPERT
    padded = jnp.concatenate([order, jnp.zeros((most,), jnp.int32)])
    gates_flat = gate_weights.reshape(-1)

    def one_expert(acc, expert):
        take = lax.dynamic_slice_in_dim(padded, starts[expert], most)
        live = jnp.arange(most, dtype=jnp.int32) < counts[expert]
        rows = moe_in[owner[take]]
        out = lax.optimization_barrier(expert_rows(rows, w_gate_up[expert], w_down[expert])).astype(jnp.float32)
        weight = jnp.where(live, gates_flat[take], 0.0)
        return (acc.at[owner[take]].add(out * weight[:, None]), None)
    moe, _ = lax.scan(one_expert, jnp.zeros((TOKENS, MODEL_WIDTH), jnp.float32), jnp.arange(EXPERTS, dtype=jnp.int32))
    hidden_out = (lax.optimization_barrier(mid).astype(jnp.float32) + moe).astype(jnp.bfloat16)
    return (hidden_out, suffix_cache)
```

```python
import math

import jax
import jax.numpy as jnp
from jax import lax
from jax.experimental import pallas as pl
from jax.experimental.pallas import tpu as pltpu
from jax.sharding import PartitionSpec as P

PREFIX_TOKENS = 2048
PAGE_TOKENS = 128


eps = 1e-06
theta = 1000000.0
floor_value = -1e30


def root_mean_scale(value_rows, gain):
    value_rows = value_rows.astype(jnp.float32)
    return (
        value_rows
        * lax.rsqrt(jnp.mean(value_rows * value_rows, axis=-1, keepdims=True) + eps)
        * gain
    )


def rotary_apply(value_rows, token_positions):
    half = value_rows.shape[-1] // 2
    freqs = theta ** (-jnp.arange(half, dtype=jnp.float32) / half)
    angles = token_positions.astype(jnp.float32)[:, None] * freqs[None, :]
    cosine = jnp.cos(angles)[:, None, :]
    sine = jnp.sin(angles)[:, None, :]
    first = value_rows[..., :half]
    second_split = value_rows[..., half:]
    return jnp.concatenate(
        [first * cosine - second_split * sine, second_split * cosine + first * sine], axis=-1
    )


def layout(lengths_row, index):
    ends = jnp.cumsum(lengths_row)
    starts = ends - lengths_row
    request = jnp.sum((index[:, None] >= ends[None, :]).astype(jnp.int32), axis=1)
    chosen = request[:, None] == jnp.arange(lengths_row.shape[0], dtype=jnp.int32)[None, :]
    offset = index - jnp.sum(jnp.where(chosen, starts[None, :], 0), axis=1)
    return (request, offset, chosen)


def attend(carry, queries, key_rows, value_rows, mask, scale):
    high, total, acc = carry
    scores = (
        jnp.einsum("qkgd,skd->kgqs", queries, key_rows, preferred_element_type=jnp.float32) * scale
    )
    scores = jnp.where(mask[None, None], scores, -jnp.inf)
    new_high = jnp.maximum(high, jnp.max(scores, axis=-1))
    weights = jnp.exp(scores - new_high[..., None])
    scale_factor = jnp.exp(high - new_high)
    total = total * scale_factor + jnp.sum(weights, axis=-1)
    acc = acc * scale_factor[..., None] + jnp.einsum(
        "kgqs,skd->kgqd",
        weights.astype(jnp.bfloat16),
        value_rows,
        preferred_element_type=jnp.float32,
    )
    return (new_high, total, acc)


MESH_ID = pl.DeviceIdType.MESH
STEP = 45
CHUNK = 16


def place():
    dp = lax.axis_index("dp")
    ex = lax.axis_index("expert")
    x = lax.rem(lax.div(ex, 4), 2) * 2 + lax.div(dp, 2)
    return (x, lax.div(ex, 8), lax.rem(ex, 4), lax.rem(dp, 2))


def device(x, y, z, c):
    return {"dp": lax.rem(x, 2) * 2 + c, "expert": y * 8 + lax.div(x, 2) * 4 + z}


def number(x, y, z, c):
    return (lax.rem(x, 2) * 2 + c) * 32 + y * 8 + lax.div(x, 2) * 4 + z


def shift(k):
    o = lax.rem(k * STEP, 128)
    return (lax.div(o, 32), lax.rem(lax.div(o, 8), 4), lax.rem(lax.div(o, 2), 4), lax.rem(o, 2))


def target(here, k):
    x, y, z, c = here
    dx, dy, dz, dc = shift(k)
    sign = 1 - 2 * c
    return (
        lax.rem(x + sign * dx + 4, 4),
        lax.rem(y + sign * dy + 4, 4),
        lax.rem(z + sign * dz + 4, 4),
        lax.rem(c + dc, 2),
    )


def origin(here, k):
    x, y, z, c = here
    dx, dy, dz, dc = shift(k)
    source_core = lax.rem(c + dc, 2)
    sign = 1 - 2 * source_core
    return (
        lax.rem(x - sign * dx + 4, 4),
        lax.rem(y - sign * dy + 4, 4),
        lax.rem(z - sign * dz + 4, 4),
        source_core,
    )


def greet_all(here):
    barrier = pltpu.get_barrier_semaphore()

    def tell(k, _):
        pl.semaphore_signal(
            barrier, inc=1, device_id=device(*target(here, k)), device_id_type=MESH_ID
        )
        return 0

    lax.fori_loop(1, 128, tell, 0)
    return barrier


def send(src, dst, send_sem, recv_sem, where):
    return pltpu.make_async_remote_copy(
        src_ref=src,
        dst_ref=dst,
        send_sem=send_sem,
        recv_sem=recv_sem,
        device_id=device(*where),
        device_id_type=MESH_ID,
    )


def moe_kernel(
    x_ref,
    ids_ref,
    gates_ref,
    gate_up_hbm,
    down_hbm,
    out_ref,
    send_a,
    send_b,
    recv_a,
    recv_b,
    back_a,
    back_b,
    home_a,
    home_b,
    gate_up,
    down,
    rows,
    acts,
    result,
    rank_ref,
    gate_ref,
    weight_sem,
    out_sem,
    in_a_sem,
    in_b_sem,
    back_sem,
    home_sem,
):
    f32, bf16 = jnp.float32, jnp.bfloat16
    width = x_ref.shape[1]
    half = width // 2
    ff = down.shape[0]
    here = place()
    me = number(*here)
    load_gate_up = pltpu.make_async_copy(gate_up_hbm, gate_up, weight_sem.at[0])
    load_down = pltpu.make_async_copy(down_hbm, down, weight_sem.at[1])
    load_gate_up.start()
    load_down.start()
    barrier = greet_all(here)

    expert = lax.broadcasted_iota(jnp.int32, (128, 128), 0)
    token = lax.broadcasted_iota(jnp.int32, (128, 128), 1)
    named = jnp.zeros((128, 128), f32)
    gates = jnp.zeros((128, 128), f32)
    for k in range(ids_ref.shape[0]):
        hit = ids_ref[k : k + 1, :] == expert
        named += jnp.where(hit, 1.0, 0.0)
        gates += jnp.where(hit, gates_ref[k : k + 1, :], 0.0)
    before = jnp.where(expert < token, 1.0, 0.0).astype(bf16)
    rank = jnp.dot(named.astype(bf16), before, preferred_element_type=f32)
    rank_ref[...] = jnp.where(named > 0.5, rank, -1.0)
    gate_ref[...] = gates

    slot = lax.broadcasted_iota(jnp.int32, (32, 8, 128), 1)

    def choice(part, wanted):
        ranks = rank_ref[pl.ds(part * 32, 32), :]
        return jnp.where(ranks[:, None, :] == wanted.astype(f32), 1.0, 0.0)

    def pack(part, _):
        first = choice(part, slot).reshape(256, 128).astype(bf16)
        send_a[pl.ds(part * 256, 256), :] = jnp.dot(
            first, x_ref[...], preferred_element_type=f32
        ).astype(bf16)
        low = choice(part, jnp.where(slot < 4, slot + 8, 99)).reshape(256, 128).astype(bf16)
        high = choice(part, jnp.where(slot >= 4, slot + 4, 99)).reshape(256, 128).astype(bf16)
        mixed = jnp.dot(low, x_ref[:, :half], preferred_element_type=f32)
        mixed += jnp.dot(high, x_ref[:, half:], preferred_element_type=f32)
        send_b[pl.ds(part * 256, 256), :] = mixed.astype(bf16)
        return 0

    lax.fori_loop(0, 4, pack, 0)
    pl.semaphore_wait(barrier, 127)

    def piece(ref, index):
        return ref.at[pl.ds(index * 8, 8), :]

    def dispatch(k, _):
        there = target(here, k)
        to = number(*there)
        group = lax.div(k, CHUNK)
        send(piece(send_a, to), piece(recv_a, k), out_sem.at[0], in_a_sem.at[group], there).start()
        send(piece(send_b, to), piece(recv_b, k), out_sem.at[1], in_b_sem.at[group], there).start()
        return 0

    own_a = pltpu.make_async_copy(piece(send_a, me), piece(recv_a, 0), in_a_sem.at[0])
    own_b = pltpu.make_async_copy(piece(send_b, me), piece(recv_b, 0), in_b_sem.at[0])
    own_a.start()
    own_b.start()
    lax.fori_loop(1, 128, dispatch, 0)
    load_gate_up.wait()
    load_down.wait()

    tall, short = CHUNK * 8, CHUNK * 4
    row = lax.broadcasted_iota(jnp.int32, (short, tall), 0)
    column = lax.broadcasted_iota(jnp.int32, (short, tall), 1)
    at_low = lax.div(row, 4) * 8 + lax.rem(row, 4)
    take_low = jnp.where(column == at_low, 1.0, 0.0).astype(bf16)
    take_high = jnp.where(column == at_low + 4, 1.0, 0.0).astype(bf16)
    row_t = lax.broadcasted_iota(jnp.int32, (tall, short), 0)
    column_t = lax.broadcasted_iota(jnp.int32, (tall, short), 1)
    at_low_t = lax.div(column_t, 4) * 8 + lax.rem(column_t, 4)
    give_low = jnp.where(row_t == at_low_t, 1.0, 0.0).astype(bf16)
    give_high = jnp.where(row_t == at_low_t + 4, 1.0, 0.0).astype(bf16)

    def work(group, _):
        a_rows = recv_a.at[pl.ds(group * tall, tall), :]
        b_rows = recv_b.at[pl.ds(group * tall, tall), :]
        pltpu.make_async_copy(a_rows, a_rows, in_a_sem.at[group]).wait()
        pltpu.make_async_copy(b_rows, b_rows, in_b_sem.at[group]).wait()
        rows[:tall, :] = a_rows[...]
        rows[tall:, :half] = jnp.dot(
            take_low, b_rows[...], preferred_element_type=f32
        ).astype(bf16)
        rows[tall:, half:] = jnp.dot(
            take_high, b_rows[...], preferred_element_type=f32
        ).astype(bf16)

        def up(tile, _):
            at = pl.multiple_of(tile * 256, 256)
            first = jnp.dot(rows[...], gate_up[:, pl.ds(at, 256)], preferred_element_type=f32)
            second = jnp.dot(
                rows[...], gate_up[:, pl.ds(ff + at, 256)], preferred_element_type=f32
            )
            acts[:, pl.ds(at, 256)] = (jax.nn.silu(first) * second).astype(bf16)
            return 0

        lax.fori_loop(0, ff // 256, up, 0)

        def lower(tile, _):
            at = pl.multiple_of(tile * 512, 512)
            result[:, pl.ds(at, 512)] = jnp.dot(
                acts[...], down[:, pl.ds(at, 512)], preferred_element_type=f32
            ).astype(bf16)
            return 0

        lax.fori_loop(0, width // 512, lower, 0)
        back_a[pl.ds(group * tall, tall), :] = result[:tall, :]
        mixed = jnp.dot(give_low, result[tall:, :half], preferred_element_type=f32)
        mixed += jnp.dot(give_high, result[tall:, half:], preferred_element_type=f32)
        back_b[pl.ds(group * tall, tall), :] = mixed.astype(bf16)

        def give(k, _):
            there = origin(here, k)
            send(piece(back_a, k), piece(home_a, me), back_sem.at[0], home_sem.at[0], there).start()
            send(piece(back_b, k), piece(home_b, me), back_sem.at[1], home_sem.at[1], there).start()
            return 0

        lax.fori_loop(jnp.where(group == 0, 1, group * CHUNK), (group + 1) * CHUNK, give, 0)
        return 0

    lax.fori_loop(0, 128 // CHUNK, work, 0)
    own_c = pltpu.make_async_copy(piece(back_a, 0), piece(home_a, me), home_sem.at[0])
    own_d = pltpu.make_async_copy(piece(back_b, 0), piece(home_b, me), home_sem.at[1])
    own_c.start()
    own_d.start()
    pltpu.make_async_copy(home_a, home_a, home_sem.at[0]).wait()
    pltpu.make_async_copy(home_b, home_b, home_sem.at[1]).wait()

    out_ref[...] = jnp.zeros_like(out_ref)
    over_rows = (((0,), (0,)), ((), ()))

    def combine(part, _):
        weight = gate_ref[pl.ds(part * 32, 32), :][:, None, :]

        def add(wanted, values, columns):
            exact = (choice(part, wanted) * weight).reshape(256, 128)
            coarse = exact.astype(bf16)
            fine = (exact - coarse.astype(f32)).astype(bf16)
            out_ref[:, columns] += lax.dot_general(
                coarse, values, over_rows, preferred_element_type=f32
            ) + lax.dot_general(fine, values, over_rows, preferred_element_type=f32)

        add(slot, home_a[pl.ds(part * 256, 256), :], slice(None))
        values = home_b[pl.ds(part * 256, 256), :]
        add(jnp.where(slot < 4, slot + 8, 99), values, slice(0, half))
        add(jnp.where(slot >= 4, slot + 4, 99), values, slice(half, width))
        return 0

    lax.fori_loop(0, 4, combine, 0)
    others = pl.ds(0, 127 * 8)
    pltpu.make_async_copy(send_a.at[others], send_a.at[others], out_sem.at[0]).wait()
    pltpu.make_async_copy(send_b.at[others], send_b.at[others], out_sem.at[1]).wait()
    pltpu.make_async_copy(back_a.at[others], back_a.at[others], back_sem.at[0]).wait()
    pltpu.make_async_copy(back_b.at[others], back_b.at[others], back_sem.at[1]).wait()


def experts(moe_in, ids, gates, gate_up, down):
    tokens, width = moe_in.shape
    ff = down.shape[0]
    groups = 128 // CHUNK
    vmem = pl.BlockSpec(memory_space=pltpu.VMEM)
    hbm = pl.BlockSpec(memory_space=pl.ANY)
    a_shape = pltpu.VMEM((1024, width), jnp.bfloat16)
    b_shape = pltpu.VMEM((1024, width // 2), jnp.bfloat16)
    return pl.pallas_call(
        moe_kernel,
        out_shape=jax.ShapeDtypeStruct((tokens, width), jnp.float32),
        in_specs=[vmem, vmem, vmem, hbm, hbm],
        out_specs=vmem,
        scratch_shapes=[
            a_shape,
            b_shape,
            a_shape,
            b_shape,
            a_shape,
            b_shape,
            a_shape,
            b_shape,
            pltpu.VMEM((width, 2 * ff), jnp.bfloat16),
            pltpu.VMEM((ff, width), jnp.bfloat16),
            pltpu.VMEM((CHUNK * 12, width), jnp.bfloat16),
            pltpu.VMEM((CHUNK * 12, ff), jnp.bfloat16),
            pltpu.VMEM((CHUNK * 12, width), jnp.bfloat16),
            pltpu.VMEM((128, 128), jnp.float32),
            pltpu.VMEM((128, 128), jnp.float32),
            pltpu.SemaphoreType.DMA((2,)),
            pltpu.SemaphoreType.DMA((2,)),
            pltpu.SemaphoreType.DMA((groups,)),
            pltpu.SemaphoreType.DMA((groups,)),
            pltpu.SemaphoreType.DMA((2,)),
            pltpu.SemaphoreType.DMA((2,)),
        ],
        compiler_params=pltpu.CompilerParams(
            collective_id=3, has_side_effects=True, vmem_limit_bytes=60 * 1024 * 1024
        ),
        cost_estimate=pl.CostEstimate(
            flops=20_000_000_000, bytes_accessed=400_000_000, transcendentals=1_000_000
        ),
    )(moe_in, ids.T, gates.T, gate_up, down)


def local(
    hidden_in,
    attn_gain,
    query_key_value_weight,
    q_gain,
    key_norm_gain,
    w_out,
    moe_gain,
    w_gate_up,
    w_down,
    kv_pool,
    page_table,
    suffix_lengths,
    request_group,
    expert_ids,
    gate_weights,
):
    tokens_here, width = hidden_in.shape
    page_rows = kv_pool.shape[2]
    kv_heads = kv_pool.shape[3]
    head_dim = kv_pool.shape[4]
    key_value_width = kv_heads * head_dim
    query_width = query_key_value_weight.shape[1] - 2 * key_value_width
    q_heads = query_width // head_dim
    head_split = q_heads // kv_heads
    scale = 1.0 / math.sqrt(head_dim)
    row = lax.axis_index("dp")
    col = lax.axis_index("expert")
    normed = root_mean_scale(hidden_in, attn_gain).astype(jnp.bfloat16)
    part = normed
    qkv = jnp.dot(
        part,
        lax.all_gather(query_key_value_weight, "expert", axis=0, tiled=True),
        preferred_element_type=jnp.float32,
    )
    index = col * tokens_here + jnp.arange(tokens_here, dtype=jnp.int32)
    lengths_row = lax.dynamic_index_in_dim(suffix_lengths, row, 0, keepdims=False)
    groups_row = lax.dynamic_index_in_dim(request_group, row, 0, keepdims=False)
    request, offset, chosen = layout(lengths_row, index)
    qgroup = jnp.sum(jnp.where(chosen, groups_row[None, :], 0), axis=1)
    token_positions = PREFIX_TOKENS + offset
    queries = rotary_apply(
        root_mean_scale(qkv[:, :query_width].reshape(tokens_here, q_heads, head_dim), q_gain),
        token_positions,
    ).astype(jnp.bfloat16)
    key_rows = rotary_apply(
        root_mean_scale(
            qkv[:, query_width : query_width + key_value_width].reshape(
                tokens_here, kv_heads, head_dim
            ),
            key_norm_gain,
        ),
        token_positions,
    ).astype(jnp.bfloat16)
    value_rows = (
        qkv[:, query_width + key_value_width :]
        .reshape(tokens_here, kv_heads, head_dim)
        .astype(jnp.bfloat16)
    )
    suffix_cache = jnp.concatenate(
        [
            key_rows.reshape(tokens_here, key_value_width),
            value_rows.reshape(tokens_here, key_value_width),
        ],
        axis=1,
    )
    grouped = queries.reshape(tokens_here, kv_heads, head_split, head_dim)
    carry = (
        jnp.full((kv_heads, head_split, tokens_here), floor_value, jnp.float32),
        jnp.zeros((kv_heads, head_split, tokens_here), jnp.float32),
        jnp.zeros((kv_heads, head_split, tokens_here, head_dim), jnp.float32),
    )
    piece_keys = lax.all_gather(key_rows, "expert", axis=0, tiled=True)
    piece_values = lax.all_gather(value_rows, "expert", axis=0, tiled=True)
    key_index = jnp.arange(piece_keys.shape[0], dtype=jnp.int32)
    key_request, _, _ = layout(lengths_row, key_index)
    mask = (key_request[None, :] == request[:, None]) & (key_index[None, :] <= index[:, None])
    carry = attend(carry, grouped, piece_keys, piece_values, mask, scale)
    per_group = PREFIX_TOKENS // PAGE_TOKENS
    slot_ids = jnp.arange(page_table.shape[0], dtype=jnp.int32)
    piece = lax.all_gather(kv_pool, "dp", axis=0, tiled=True)
    count = piece.shape[0]
    hit = page_table[None, :] == jnp.arange(count, dtype=jnp.int32)[:, None]
    key_group = jnp.repeat(
        jnp.sum(jnp.where(hit, slot_ids[None, :] // per_group, 0), axis=1), page_rows
    )
    mask = key_group[None, :] == qgroup[:, None]
    carry = attend(
        carry,
        grouped,
        piece[:, 0].reshape(count * page_rows, kv_heads, head_dim),
        piece[:, 1].reshape(count * page_rows, kv_heads, head_dim),
        mask,
        scale,
    )
    mixed = (
        (carry[2] / carry[1][..., None])
        .transpose(2, 0, 1, 3)
        .reshape(tokens_here, query_width)
        .astype(jnp.bfloat16)
    )
    part = mixed
    projected = jnp.dot(
        part,
        lax.all_gather(w_out, "expert", axis=0, tiled=True),
        preferred_element_type=jnp.float32,
    )
    mid = (hidden_in.astype(jnp.float32) + projected).astype(jnp.bfloat16)
    moe_in = root_mean_scale(mid, moe_gain).astype(jnp.bfloat16)
    moe = experts(moe_in, expert_ids, gate_weights, w_gate_up[0], w_down[0])
    hidden_out = (mid.astype(jnp.float32) + moe).astype(jnp.bfloat16)
    return (hidden_out, suffix_cache)


def solution(mesh):
    return jax.shard_map(
        local,
        mesh=mesh,
        in_specs=(
            P(("dp", "expert"), None),
            P(),
            P("expert", None),
            P(),
            P(),
            P("expert", None),
            P(),
            P(("dp", "expert"), None, None),
            P(("dp", "expert"), None, None),
            P("dp", None, None, None, None),
            P(),
            P(),
            P(),
            P(("dp", "expert"), None),
            P(("dp", "expert"), None),
        ),
        out_specs=(P(("dp", "expert"), None), P(("dp", "expert"), None)),
        check_vma=False,
    )
```

```python
import math

import jax
import jax.numpy as jnp
from jax import lax
from jax.experimental import pallas as pl
from jax.experimental.pallas import tpu as pltpu
from jax.sharding import PartitionSpec as P

PREFIX_TOKENS = 2048


eps = 1e-06
theta = 1000000.0
floor_value = -1e30


def root_mean_scale(value_rows, gain):
    value_rows = value_rows.astype(jnp.float32)
    return (
        value_rows
        * lax.rsqrt(jnp.mean(value_rows * value_rows, axis=-1, keepdims=True) + eps)
        * gain
    )


MESH_ID = pl.DeviceIdType.MESH
STEP = 45
CHUNK = 16


def place():
    dp = lax.axis_index("dp")
    ex = lax.axis_index("expert")
    x = lax.rem(lax.div(ex, 4), 2) * 2 + lax.div(dp, 2)
    return (x, lax.div(ex, 8), lax.rem(ex, 4), lax.rem(dp, 2))


def device(x, y, z, c):
    return {"dp": lax.rem(x, 2) * 2 + c, "expert": y * 8 + lax.div(x, 2) * 4 + z}


def number(x, y, z, c):
    return (lax.rem(x, 2) * 2 + c) * 32 + y * 8 + lax.div(x, 2) * 4 + z


def shift(k):
    o = lax.rem(k * STEP, 128)
    return (lax.div(o, 32), lax.rem(lax.div(o, 8), 4), lax.rem(lax.div(o, 2), 4), lax.rem(o, 2))


def target(here, k):
    x, y, z, c = here
    dx, dy, dz, dc = shift(k)
    sign = 1 - 2 * c
    return (
        lax.rem(x + sign * dx + 4, 4),
        lax.rem(y + sign * dy + 4, 4),
        lax.rem(z + sign * dz + 4, 4),
        lax.rem(c + dc, 2),
    )


def origin(here, k):
    x, y, z, c = here
    dx, dy, dz, dc = shift(k)
    source_core = lax.rem(c + dc, 2)
    sign = 1 - 2 * source_core
    return (
        lax.rem(x - sign * dx + 4, 4),
        lax.rem(y - sign * dy + 4, 4),
        lax.rem(z - sign * dz + 4, 4),
        source_core,
    )


def greet_all(here):
    barrier = pltpu.get_barrier_semaphore()

    def tell(k, _):
        pl.semaphore_signal(
            barrier, inc=1, device_id=device(*target(here, k)), device_id_type=MESH_ID
        )
        return 0

    lax.fori_loop(1, 128, tell, 0)
    return barrier


def send(src, dst, send_sem, recv_sem, where):
    return pltpu.make_async_remote_copy(
        src_ref=src,
        dst_ref=dst,
        send_sem=send_sem,
        recv_sem=recv_sem,
        device_id=device(*where),
        device_id_type=MESH_ID,
    )


def moe_kernel(
    x_ref,
    ids_ref,
    gates_ref,
    gate_up_hbm,
    down_hbm,
    out_ref,
    send_a,
    send_b,
    recv_a,
    recv_b,
    back_a,
    back_b,
    home_a,
    home_b,
    gate_up,
    down,
    rows,
    acts,
    result,
    rank_ref,
    gate_ref,
    weight_sem,
    out_sem,
    in_a_sem,
    in_b_sem,
    back_sem,
    home_sem,
):
    f32, bf16 = jnp.float32, jnp.bfloat16
    width = x_ref.shape[1]
    half = width // 2
    ff = down.shape[0]
    here = place()
    me = number(*here)
    load_gate_up = pltpu.make_async_copy(gate_up_hbm, gate_up, weight_sem.at[0])
    load_down = pltpu.make_async_copy(down_hbm, down, weight_sem.at[1])
    load_gate_up.start()
    load_down.start()
    barrier = greet_all(here)

    expert = lax.broadcasted_iota(jnp.int32, (128, 128), 0)
    token = lax.broadcasted_iota(jnp.int32, (128, 128), 1)
    named = jnp.zeros((128, 128), f32)
    gates = jnp.zeros((128, 128), f32)
    for k in range(ids_ref.shape[0]):
        hit = ids_ref[k : k + 1, :] == expert
        named += jnp.where(hit, 1.0, 0.0)
        gates += jnp.where(hit, gates_ref[k : k + 1, :], 0.0)
    before = jnp.where(expert < token, 1.0, 0.0).astype(bf16)
    rank = jnp.dot(named.astype(bf16), before, preferred_element_type=f32)
    rank_ref[...] = jnp.where(named > 0.5, rank, -1.0)
    gate_ref[...] = gates

    slot = lax.broadcasted_iota(jnp.int32, (32, 8, 128), 1)

    def choice(part, wanted):
        ranks = rank_ref[pl.ds(part * 32, 32), :]
        return jnp.where(ranks[:, None, :] == wanted.astype(f32), 1.0, 0.0)

    def pack(part, _):
        first = choice(part, slot).reshape(256, 128).astype(bf16)
        send_a[pl.ds(part * 256, 256), :] = jnp.dot(
            first, x_ref[...], preferred_element_type=f32
        ).astype(bf16)
        low = choice(part, jnp.where(slot < 4, slot + 8, 99)).reshape(256, 128).astype(bf16)
        high = choice(part, jnp.where(slot >= 4, slot + 4, 99)).reshape(256, 128).astype(bf16)
        mixed = jnp.dot(low, x_ref[:, :half], preferred_element_type=f32)
        mixed += jnp.dot(high, x_ref[:, half:], preferred_element_type=f32)
        send_b[pl.ds(part * 256, 256), :] = mixed.astype(bf16)
        return 0

    lax.fori_loop(0, 4, pack, 0)
    pl.semaphore_wait(barrier, 127)

    def piece(ref, index):
        return ref.at[pl.ds(index * 8, 8), :]

    def dispatch(k, _):
        there = target(here, k)
        to = number(*there)
        group = lax.div(k, CHUNK)
        send(piece(send_a, to), piece(recv_a, k), out_sem.at[0], in_a_sem.at[group], there).start()
        send(piece(send_b, to), piece(recv_b, k), out_sem.at[1], in_b_sem.at[group], there).start()
        return 0

    own_a = pltpu.make_async_copy(piece(send_a, me), piece(recv_a, 0), in_a_sem.at[0])
    own_b = pltpu.make_async_copy(piece(send_b, me), piece(recv_b, 0), in_b_sem.at[0])
    own_a.start()
    own_b.start()
    lax.fori_loop(1, 128, dispatch, 0)
    load_gate_up.wait()
    load_down.wait()

    tall, short = CHUNK * 8, CHUNK * 4
    row = lax.broadcasted_iota(jnp.int32, (short, tall), 0)
    column = lax.broadcasted_iota(jnp.int32, (short, tall), 1)
    at_low = lax.div(row, 4) * 8 + lax.rem(row, 4)
    take_low = jnp.where(column == at_low, 1.0, 0.0).astype(bf16)
    take_high = jnp.where(column == at_low + 4, 1.0, 0.0).astype(bf16)
    row_t = lax.broadcasted_iota(jnp.int32, (tall, short), 0)
    column_t = lax.broadcasted_iota(jnp.int32, (tall, short), 1)
    at_low_t = lax.div(column_t, 4) * 8 + lax.rem(column_t, 4)
    give_low = jnp.where(row_t == at_low_t, 1.0, 0.0).astype(bf16)
    give_high = jnp.where(row_t == at_low_t + 4, 1.0, 0.0).astype(bf16)

    def work(group, _):
        a_rows = recv_a.at[pl.ds(group * tall, tall), :]
        b_rows = recv_b.at[pl.ds(group * tall, tall), :]
        pltpu.make_async_copy(a_rows, a_rows, in_a_sem.at[group]).wait()
        pltpu.make_async_copy(b_rows, b_rows, in_b_sem.at[group]).wait()
        rows[:tall, :] = a_rows[...]
        rows[tall:, :half] = jnp.dot(
            take_low, b_rows[...], preferred_element_type=f32
        ).astype(bf16)
        rows[tall:, half:] = jnp.dot(
            take_high, b_rows[...], preferred_element_type=f32
        ).astype(bf16)

        def up(tile, _):
            at = pl.multiple_of(tile * 256, 256)
            first = jnp.dot(rows[...], gate_up[:, pl.ds(at, 256)], preferred_element_type=f32)
            second = jnp.dot(
                rows[...], gate_up[:, pl.ds(ff + at, 256)], preferred_element_type=f32
            )
            acts[:, pl.ds(at, 256)] = (jax.nn.silu(first) * second).astype(bf16)
            return 0

        lax.fori_loop(0, ff // 256, up, 0)

        def lower(tile, _):
            at = pl.multiple_of(tile * 512, 512)
            result[:, pl.ds(at, 512)] = jnp.dot(
                acts[...], down[:, pl.ds(at, 512)], preferred_element_type=f32
            ).astype(bf16)
            return 0

        lax.fori_loop(0, width // 512, lower, 0)
        back_a[pl.ds(group * tall, tall), :] = result[:tall, :]
        mixed = jnp.dot(give_low, result[tall:, :half], preferred_element_type=f32)
        mixed += jnp.dot(give_high, result[tall:, half:], preferred_element_type=f32)
        back_b[pl.ds(group * tall, tall), :] = mixed.astype(bf16)

        def give(k, _):
            there = origin(here, k)
            send(piece(back_a, k), piece(home_a, me), back_sem.at[0], home_sem.at[0], there).start()
            send(piece(back_b, k), piece(home_b, me), back_sem.at[1], home_sem.at[1], there).start()
            return 0

        lax.fori_loop(jnp.where(group == 0, 1, group * CHUNK), (group + 1) * CHUNK, give, 0)
        return 0

    lax.fori_loop(0, 128 // CHUNK, work, 0)
    own_c = pltpu.make_async_copy(piece(back_a, 0), piece(home_a, me), home_sem.at[0])
    own_d = pltpu.make_async_copy(piece(back_b, 0), piece(home_b, me), home_sem.at[1])
    own_c.start()
    own_d.start()
    pltpu.make_async_copy(home_a, home_a, home_sem.at[0]).wait()
    pltpu.make_async_copy(home_b, home_b, home_sem.at[1]).wait()

    out_ref[...] = jnp.zeros_like(out_ref)
    over_rows = (((0,), (0,)), ((), ()))

    def combine(part, _):
        weight = gate_ref[pl.ds(part * 32, 32), :][:, None, :]

        def add(wanted, values, columns):
            exact = (choice(part, wanted) * weight).reshape(256, 128)
            coarse = exact.astype(bf16)
            fine = (exact - coarse.astype(f32)).astype(bf16)
            out_ref[:, columns] += lax.dot_general(
                coarse, values, over_rows, preferred_element_type=f32
            ) + lax.dot_general(fine, values, over_rows, preferred_element_type=f32)

        add(slot, home_a[pl.ds(part * 256, 256), :], slice(None))
        values = home_b[pl.ds(part * 256, 256), :]
        add(jnp.where(slot < 4, slot + 8, 99), values, slice(0, half))
        add(jnp.where(slot >= 4, slot + 4, 99), values, slice(half, width))
        return 0

    lax.fori_loop(0, 4, combine, 0)
    others = pl.ds(0, 127 * 8)
    pltpu.make_async_copy(send_a.at[others], send_a.at[others], out_sem.at[0]).wait()
    pltpu.make_async_copy(send_b.at[others], send_b.at[others], out_sem.at[1]).wait()
    pltpu.make_async_copy(back_a.at[others], back_a.at[others], back_sem.at[0]).wait()
    pltpu.make_async_copy(back_b.at[others], back_b.at[others], back_sem.at[1]).wait()


def experts(moe_in, ids, gates, gate_up, down):
    tokens, width = moe_in.shape
    ff = down.shape[0]
    groups = 128 // CHUNK
    vmem = pl.BlockSpec(memory_space=pltpu.VMEM)
    hbm = pl.BlockSpec(memory_space=pl.ANY)
    a_shape = pltpu.VMEM((1024, width), jnp.bfloat16)
    b_shape = pltpu.VMEM((1024, width // 2), jnp.bfloat16)
    return pl.pallas_call(
        moe_kernel,
        out_shape=jax.ShapeDtypeStruct((tokens, width), jnp.float32),
        in_specs=[vmem, vmem, vmem, hbm, hbm],
        out_specs=vmem,
        scratch_shapes=[
            a_shape,
            b_shape,
            a_shape,
            b_shape,
            a_shape,
            b_shape,
            a_shape,
            b_shape,
            pltpu.VMEM((width, 2 * ff), jnp.bfloat16),
            pltpu.VMEM((ff, width), jnp.bfloat16),
            pltpu.VMEM((CHUNK * 12, width), jnp.bfloat16),
            pltpu.VMEM((CHUNK * 12, ff), jnp.bfloat16),
            pltpu.VMEM((CHUNK * 12, width), jnp.bfloat16),
            pltpu.VMEM((128, 128), jnp.float32),
            pltpu.VMEM((128, 128), jnp.float32),
            pltpu.SemaphoreType.DMA((2,)),
            pltpu.SemaphoreType.DMA((2,)),
            pltpu.SemaphoreType.DMA((groups,)),
            pltpu.SemaphoreType.DMA((groups,)),
            pltpu.SemaphoreType.DMA((2,)),
            pltpu.SemaphoreType.DMA((2,)),
        ],
        compiler_params=pltpu.CompilerParams(
            collective_id=3, has_side_effects=True, vmem_limit_bytes=60 * 1024 * 1024
        ),
        cost_estimate=pl.CostEstimate(
            flops=20_000_000_000, bytes_accessed=400_000_000, transcendentals=1_000_000
        ),
    )(moe_in, ids.T, gates.T, gate_up, down)


def arrived(ref, sem):
    pltpu.make_async_copy(ref, ref, sem).wait()


class Gather:
    def __init__(self, buf, here, cross, columns, sems):
        self.buf, self.here, self.cross, self.columns = buf, here, cross, columns
        self.send_sem, self.recv_sem, self.cross_sem = sems

    def cut(self, r):
        start, size = self.columns[r]
        return pl.ds(pl.multiple_of(start, 128), size)

    def whole(self, h):
        x, y, z, c = self.here
        start, size = self.columns[0]
        return self.buf.at[y, h, z, :, pl.ds(pl.multiple_of(start, 128), size + self.columns[1][1])]

    def near(self, r):
        x, y, z, c = self.here
        cut = self.cut(r)
        if r == 0:
            return lambda p, h: self.buf.at[y, h, p, :, cut]
        return lambda p, h: self.buf.at[p, h, z, :, cut]

    def far(self, r):
        cut = self.cut(r)
        if r == 0:
            return lambda p, h: self.buf.at[p, h, :, :, cut]
        return lambda p, h: self.buf.at[:, h, p, :, cut]

    def ring(self, r, phase):
        x, y, z, c = self.here
        if (r + phase) % 2 == 0:
            return z, (x, y, lax.rem(z + 1, 4), c), (x, y, lax.rem(z + 3, 4), c)
        return y, (x, lax.rem(y + 1, 4), z, c), (x, lax.rem(y + 3, 4), z, c)

    def start(self):
        own = lax.div(self.here[0], 2)
        send(
            self.whole(own), self.whole(own), self.cross_sem.at[0], self.cross_sem.at[1], self.cross
        ).start()
        self.push(0, own)

    def push(self, phase, h):
        for r in range(2):
            pick = (self.near if phase == 0 else self.far)(r)
            pos, right, left = self.ring(r, phase)
            piece = pick(pos, h)
            for d, there in enumerate((right, left)):
                send(
                    piece,
                    piece,
                    self.send_sem.at[r, phase, d, h],
                    self.recv_sem.at[r, phase, d, h],
                    there,
                ).start()

    def first(self):
        own = lax.div(self.here[0], 2)
        arrived(self.whole(1 - own), self.cross_sem.at[1])
        self.push(0, 1 - own)
        self.forward(0)
        self.rest(0, None)

    def forward(self, phase):
        for d in range(2):
            for r in range(2):
                pick = (self.near if phase == 0 else self.far)(r)
                pos, right, left = self.ring(r, phase)
                arrived(pick(pos, d), self.recv_sem.at[r, phase, d, d])
                piece = pick(lax.rem(pos + (3 if d == 0 else 1), 4), d)
                send(
                    piece,
                    piece,
                    self.send_sem.at[r, phase, 2, d],
                    self.recv_sem.at[r, phase, 2, d],
                    right if d == 0 else left,
                ).start()

    def rest(self, phase, seen):
        for d, h in ((0, 1), (1, 0), (2, 0), (2, 1)):
            for r in range(2):
                pick = (self.near if phase == 0 else self.far)(r)
                pos, _, _ = self.ring(r, phase)
                arrived(pick(pos, h), self.recv_sem.at[r, phase, d, h])
                if seen is not None:
                    seen(r, d, h, pick(lax.rem(pos + (3, 1, 2)[d], 4), h))

    def second(self, seen=None):
        self.push(1, 0)
        self.push(1, 1)
        self.forward(1)
        if seen is not None:
            for d in range(2):
                for r in range(2):
                    pos, _, _ = self.ring(r, 1)
                    seen(r, d, d, self.far(r)(lax.rem(pos + (3, 1)[d], 4), d))
        self.rest(1, seen)

    def drain(self):
        arrived(self.whole(0), self.cross_sem.at[0])
        for r in range(2):
            for phase in range(2):
                pick = (self.near if phase == 0 else self.far)(r)
                for d in range(3):
                    for h in range(2):
                        arrived(pick(0, h), self.send_sem.at[r, phase, d, h])


def front_kernel(
    hidden_ref,
    gain_ref,
    shard_ref,
    q_gain_ref,
    k_gain_ref,
    cos_ref,
    sin_ref,
    q_ref,
    kv_ref,
    cache_ref,
    weight,
    qkv,
    normed_ref,
    w_send,
    w_recv,
    w_cross,
    k_send,
    k_recv,
    k_cross,
    swap_send,
    swap_recv,
    local_sem,
):
    f32, bf16 = jnp.float32, jnp.bfloat16
    here = place()
    x, y, z, c = here
    own = lax.div(x, 2)
    columns = weight.shape[-1]
    side = columns // 2
    turn = side // 2
    partner = (x, y, z, 1 - c)
    even = 1 - lax.rem(x, 2)
    across = (lax.rem(x + 1 + 2 * even, 4), y, z, c)
    opposite = (lax.rem(x + 2, 4), y, z, c)
    barrier = pltpu.get_barrier_semaphore()
    peers = (
        partner,
        across,
        opposite,
        (x, lax.rem(y + 1, 4), z, c),
        (x, lax.rem(y + 3, 4), z, c),
        (x, y, lax.rem(z + 1, 4), c),
        (x, y, lax.rem(z + 3, 4), c),
    )
    for peer in peers:
        pl.semaphore_signal(barrier, inc=1, device_id=device(*peer), device_id_type=MESH_ID)
    mine = pl.ds(pl.multiple_of(c * side, 128), side)
    seed = pltpu.make_async_copy(
        shard_ref.at[:, mine], weight.at[y, own, z, :, mine], local_sem
    )
    seed.start()
    seed.wait()
    pl.semaphore_wait(barrier, len(peers))

    gather = Gather(
        weight,
        here,
        across,
        ((c * side, turn), (c * side + turn, side - turn)),
        (w_send, w_recv, w_cross),
    )
    gather.start()

    value = hidden_ref[...].astype(f32)
    mean = jnp.mean(value * value, axis=-1, keepdims=True)
    normed_ref[...] = (value * lax.rsqrt(mean + eps) * gain_ref[...]).astype(bf16)

    gather.first()
    swaps = []

    def swap(r, slot, piece):
        copy = send(piece, piece, swap_send.at[r, slot], swap_recv.at[r, slot], partner)
        copy.start()
        swaps.append(copy)

    gather.push(1, 0)
    gather.push(1, 1)
    for r in range(2):
        pos, _, _ = gather.ring(r, 1)
        cut = gather.cut(r)
        whole = weight.at[pos, :, :, :, cut] if r == 0 else weight.at[:, :, pos, :, cut]
        swap(r, 6, whole)
    gather.forward(1)
    for d in range(2):
        for r in range(2):
            pos, _, _ = gather.ring(r, 1)
            swap(r, d * 2 + d, gather.far(r)(lax.rem(pos + (3, 1)[d], 4), d))
    gather.rest(1, lambda r, d, h, piece: swap(r, d * 2 + h, piece))
    for copy in swaps:
        copy.wait_recv()

    span = 2 * 4 * weight.shape[3]

    def project(tile, _):
        at = pl.multiple_of(tile * 512, 512)
        total = jnp.zeros((normed_ref.shape[0], 512), f32)
        for plane in range(4):
            block = weight[plane, :, :, :, pl.ds(at, 512)].reshape(span, 512)
            total += jnp.dot(
                normed_ref[:, plane * span : (plane + 1) * span],
                block,
                preferred_element_type=f32,
            )
        qkv[:, pl.ds(at, 512)] = total
        return 0

    lax.fori_loop(0, columns // 512, project, 0)

    cosine = cos_ref[...]
    sine = sin_ref[...]
    heads = columns // 128

    def turned(head, gain):
        rows = qkv[:, pl.ds(pl.multiple_of(head * 128, 128), 128)]
        mean = jnp.mean(rows * rows, axis=-1, keepdims=True)
        rows = rows * lax.rsqrt(mean + eps) * gain
        return (rows * cosine + pltpu.roll(rows, 64, 1) * sine).astype(bf16)

    for h in range(2):
        cache_ref[:, h * 128 : (h + 1) * 128] = turned(heads - 4 + h, k_gain_ref[...])
    cache_ref[:, 256:512] = qkv[:, columns - 256 :].astype(bf16)
    seed = pltpu.make_async_copy(cache_ref, kv_ref.at[y, own, z], local_sem)
    seed.start()
    seed.wait()
    spread = Gather(kv_ref, here, opposite, ((0, 256), (256, 256)), (k_send, k_recv, k_cross))
    spread.start()

    def query(head, _):
        at = pl.multiple_of(lax.rem(head, 8) * 128, 128)
        q_ref[lax.div(head, 8), pl.ds(at, 128), :] = turned(head, q_gain_ref[...])
        return 0

    lax.fori_loop(0, heads - 4, query, 0)
    spread.first()
    spread.second()
    gather.drain()
    spread.drain()
    for copy in swaps:
        copy.wait_send()


def front(hidden, gain, shard, q_gain, k_gain, cosine, sine):
    tokens, width = hidden.shape
    rows, columns = shard.shape
    vmem = pl.BlockSpec(memory_space=pltpu.VMEM)
    ring = pltpu.SemaphoreType.DMA((2, 2, 3, 2))
    two = pltpu.SemaphoreType.DMA((2,))
    swap = pltpu.SemaphoreType.DMA((2, 7))
    return pl.pallas_call(
        front_kernel,
        out_shape=(
            jax.ShapeDtypeStruct((2, 8 * tokens, 128), jnp.bfloat16),
            jax.ShapeDtypeStruct((4, 2, 4, tokens, 512), jnp.bfloat16),
            jax.ShapeDtypeStruct((tokens, 512), jnp.bfloat16),
        ),
        in_specs=[vmem] * 7,
        out_specs=(vmem, vmem, vmem),
        scratch_shapes=[
            pltpu.VMEM((4, 2, 4, rows, columns), jnp.bfloat16),
            pltpu.VMEM((tokens, columns), jnp.float32),
            pltpu.VMEM((tokens, width), jnp.bfloat16),
            ring,
            ring,
            two,
            ring,
            ring,
            two,
            swap,
            swap,
            pltpu.SemaphoreType.DMA,
        ],
        compiler_params=pltpu.CompilerParams(
            collective_id=1, has_side_effects=True, vmem_limit_bytes=56 * 1024 * 1024
        ),
        cost_estimate=pl.CostEstimate(
            flops=1_400_000_000, bytes_accessed=200_000_000, transcendentals=1_000_000
        ),
    )(hidden, gain, shard, q_gain, k_gain, cosine, sine)


def attention_kernel(
    facts, table, q_ref, kv_ref, pool_ref, start_ref, index_ref, group_ref, out_ref, high, total, acc
):
    f32, bf16 = jnp.float32, jnp.bfloat16
    factor = math.log2(math.e) / math.sqrt(128)
    high[...] = jnp.full_like(high, floor_value)
    total[...] = jnp.zeros_like(total)
    acc[...] = jnp.zeros_like(acc)

    def step(h, keys, values, seen):
        scores = lax.dot_general(
            keys, q_ref[h], (((1,), (1,)), ((), ())), preferred_element_type=f32
        )
        if seen is not None:
            scores = jnp.where(jnp.concatenate([seen] * 8, axis=1), scores, -jnp.inf)
        old = high[h]
        new = jnp.maximum(old, jnp.max(scores, axis=0, keepdims=True))
        weights = jnp.exp2((scores - new) * factor)
        shrink = jnp.exp2((old - new) * factor)
        high[h] = new
        total[h] = total[h] * shrink + jnp.sum(weights, axis=0, keepdims=True)
        acc[h] = acc[h] * shrink + lax.dot_general(
            values, weights.astype(bf16), (((0,), (0,)), ((), ())), preferred_element_type=f32
        )

    span = 4
    for group in range(2):

        def pages(seen, group=group):
            def body(j, _):
                picked = [table[group * 16 + j * span + i] for i in range(span)]
                for h in range(2):
                    keys = jnp.concatenate([pool_ref[p, 0, h] for p in picked], axis=0)
                    values = jnp.concatenate([pool_ref[p, 1, h] for p in picked], axis=0)
                    step(h, keys, values, seen)
                return 0

            lax.fori_loop(0, 16 // span, body, 0)

        @pl.when(facts[group] == 2)
        def _():
            pages(None)

        @pl.when(facts[group] == 1)
        def _():
            pages(jnp.broadcast_to(group_ref[...] == group, (span * 128, 128)))

    size = 256

    def suffix(tile, masked):
        at = pl.multiple_of(tile * size, size)
        seen = None
        if masked:
            place_of = at + lax.broadcasted_iota(jnp.int32, (size, 128), 0)
            seen = (place_of >= start_ref[...]) & (place_of <= index_ref[...])
        for h in range(2):
            keys = kv_ref[pl.ds(at, size), h * 128 : (h + 1) * 128]
            values = kv_ref[pl.ds(at, size), 256 + h * 128 : 256 + (h + 1) * 128]
            step(h, keys, values, seen)

    def tiles(tile, _):
        clear = (tile * size >= facts[3]) & (tile * size + size <= facts[4] + 1)

        @pl.when(clear)
        def _():
            suffix(tile, False)

        @pl.when(jnp.logical_not(clear))
        def _():
            suffix(tile, True)

        return 0

    lax.fori_loop(lax.div(facts[2], size), lax.div(facts[5], size) + 1, tiles, 0)
    for h in range(2):
        done = acc[h] / total[h]
        for g in range(8):
            head = h * 8 + g
            out_ref[:, head * 128 : (head + 1) * 128] = (
                done[:, g * 128 : (g + 1) * 128].T.astype(bf16)
            )


def attention(facts, table, q, kv, pool, start, index, group):
    vmem = pl.BlockSpec(memory_space=pltpu.VMEM)
    smem = pl.BlockSpec(memory_space=pltpu.SMEM)
    tokens = start.shape[1]
    return pl.pallas_call(
        attention_kernel,
        out_shape=jax.ShapeDtypeStruct((tokens, 16 * 128), jnp.bfloat16),
        in_specs=[smem, smem] + [vmem] * 6,
        out_specs=vmem,
        scratch_shapes=[
            pltpu.VMEM((2, 1, 8 * tokens), jnp.float32),
            pltpu.VMEM((2, 1, 8 * tokens), jnp.float32),
            pltpu.VMEM((2, 128, 8 * tokens), jnp.float32),
        ],
        compiler_params=pltpu.CompilerParams(vmem_limit_bytes=56 * 1024 * 1024),
        cost_estimate=pl.CostEstimate(
            flops=5_000_000_000, bytes_accessed=10_000_000, transcendentals=10_000_000
        ),
    )(facts, table, q, kv, pool, start, index, group)


def local(
    hidden_in,
    attn_gain,
    query_key_value_weight,
    q_gain,
    key_norm_gain,
    w_out,
    moe_gain,
    w_gate_up,
    w_down,
    kv_pool,
    page_table,
    suffix_lengths,
    request_group,
    expert_ids,
    gate_weights,
):
    tokens_here, width = hidden_in.shape
    row = lax.axis_index("dp")
    col = lax.axis_index("expert")
    pool = lax.all_gather(kv_pool.transpose(0, 1, 3, 2, 4), "dp", axis=0, tiled=True)
    w_out_all = lax.all_gather(w_out, "expert", axis=0, tiled=True)
    index = col * tokens_here + jnp.arange(tokens_here, dtype=jnp.int32)
    lengths_row = lax.dynamic_index_in_dim(suffix_lengths, row, 0, keepdims=False)
    groups_row = lax.dynamic_index_in_dim(request_group, row, 0, keepdims=False)
    ends = [lengths_row[0]]
    for r in range(1, 4):
        ends.append(ends[-1] + lengths_row[r])
    start = jnp.zeros_like(index)
    group = jnp.full_like(index, 0) + groups_row[0]
    for r in range(3):
        later = index >= ends[r]
        start = jnp.where(later, ends[r], start)
        group = jnp.where(later, groups_row[r + 1], group)
    offset = index - start
    half = 64
    freqs = theta ** (-jnp.arange(half, dtype=jnp.float32) / half)
    angles = (PREFIX_TOKENS + offset).astype(jnp.float32)[:, None] * freqs[None, :]
    cosine, sine = jnp.cos(angles), jnp.sin(angles)
    q, kv, suffix_cache = front(
        hidden_in,
        attn_gain[None],
        query_key_value_weight,
        q_gain[None],
        key_norm_gain[None],
        jnp.concatenate([cosine, cosine], axis=1),
        jnp.concatenate([-sine, sine], axis=1),
    )
    ones = jnp.sum(group)
    facts = jnp.stack(
        [
            jnp.where(ones == 0, 2, jnp.where(ones == tokens_here, 0, 1)),
            jnp.where(ones == tokens_here, 2, jnp.where(ones == 0, 0, 1)),
            jnp.min(start),
            jnp.max(start),
            col * tokens_here,
            col * tokens_here + tokens_here - 1,
        ]
    ).astype(jnp.int32)
    mixed = attention(
        facts,
        page_table,
        q,
        kv.reshape(32 * tokens_here, 512),
        pool,
        start[None],
        index[None],
        group[None],
    )
    projected = jnp.dot(mixed, w_out_all, preferred_element_type=jnp.float32)
    mid = (hidden_in.astype(jnp.float32) + projected).astype(jnp.bfloat16)
    moe_in = root_mean_scale(mid, moe_gain).astype(jnp.bfloat16)
    moe = experts(moe_in, expert_ids, gate_weights, w_gate_up[0], w_down[0])
    hidden_out = (mid.astype(jnp.float32) + moe).astype(jnp.bfloat16)
    return (hidden_out, suffix_cache)


def solution(mesh):
    return jax.shard_map(
        local,
        mesh=mesh,
        in_specs=(
            P(("dp", "expert"), None),
            P(),
            P("expert", None),
            P(),
            P(),
            P("expert", None),
            P(),
            P(("dp", "expert"), None, None),
            P(("dp", "expert"), None, None),
            P("dp", None, None, None, None),
            P(),
            P(),
            P(),
            P(("dp", "expert"), None),
            P(("dp", "expert"), None),
        ),
        out_specs=(P(("dp", "expert"), None), P(("dp", "expert"), None)),
        check_vma=False,
    )
```

```python
import math

import jax
import jax.numpy as jnp
from jax import lax
from jax.experimental import pallas as pl
from jax.experimental.pallas import tpu as pltpu
from jax.sharding import PartitionSpec as P

PREFIX_TOKENS = 2048


eps = 1e-06
theta = 1000000.0
floor_value = -1e30


MESH_ID = pl.DeviceIdType.MESH
STEP = 45
CHUNK = 16


def place():
    dp = lax.axis_index("dp")
    ex = lax.axis_index("expert")
    x = lax.rem(lax.div(ex, 4), 2) * 2 + lax.div(dp, 2)
    return (x, lax.div(ex, 8), lax.rem(ex, 4), lax.rem(dp, 2))


def device(x, y, z, c):
    return {"dp": lax.rem(x, 2) * 2 + c, "expert": y * 8 + lax.div(x, 2) * 4 + z}


def number(x, y, z, c):
    return (lax.rem(x, 2) * 2 + c) * 32 + y * 8 + lax.div(x, 2) * 4 + z


def shift(k):
    o = lax.rem(k * STEP, 128)
    return (lax.div(o, 32), lax.rem(lax.div(o, 8), 4), lax.rem(lax.div(o, 2), 4), lax.rem(o, 2))


def target(here, k):
    x, y, z, c = here
    dx, dy, dz, dc = shift(k)
    sign = 1 - 2 * c
    return (
        lax.rem(x + sign * dx + 4, 4),
        lax.rem(y + sign * dy + 4, 4),
        lax.rem(z + sign * dz + 4, 4),
        lax.rem(c + dc, 2),
    )


def origin(here, k):
    x, y, z, c = here
    dx, dy, dz, dc = shift(k)
    source_core = lax.rem(c + dc, 2)
    sign = 1 - 2 * source_core
    return (
        lax.rem(x - sign * dx + 4, 4),
        lax.rem(y - sign * dy + 4, 4),
        lax.rem(z - sign * dz + 4, 4),
        source_core,
    )


def greet_all(here):
    barrier = pltpu.get_barrier_semaphore()

    def tell(k, _):
        pl.semaphore_signal(
            barrier, inc=1, device_id=device(*target(here, k)), device_id_type=MESH_ID
        )
        return 0

    lax.fori_loop(1, 128, tell, 0)
    return barrier


def send(src, dst, send_sem, recv_sem, where):
    return pltpu.make_async_remote_copy(
        src_ref=src,
        dst_ref=dst,
        send_sem=send_sem,
        recv_sem=recv_sem,
        device_id=device(*where),
        device_id_type=MESH_ID,
    )


def moe_kernel(
    x_ref,
    mid_ref,
    ids_ref,
    gates_ref,
    gate_up_hbm,
    down_hbm,
    out_ref,
    send_a,
    send_b,
    recv_a,
    recv_b,
    back_a,
    back_b,
    home_a,
    home_b,
    moe_sum,
    gate_up,
    down,
    rows,
    acts,
    result,
    rank_ref,
    gate_ref,
    weight_sem,
    out_sem,
    in_a_sem,
    in_b_sem,
    back_sem,
    home_sem,
):
    f32, bf16 = jnp.float32, jnp.bfloat16
    width = x_ref.shape[1]
    half = width // 2
    ff = down.shape[0]
    here = place()
    me = number(*here)
    load_gate_up = pltpu.make_async_copy(gate_up_hbm, gate_up, weight_sem.at[0])
    load_down = pltpu.make_async_copy(down_hbm, down, weight_sem.at[1])
    load_gate_up.start()
    load_down.start()
    barrier = greet_all(here)

    expert = lax.broadcasted_iota(jnp.int32, (128, 128), 0)
    token = lax.broadcasted_iota(jnp.int32, (128, 128), 1)
    named = jnp.zeros((128, 128), f32)
    gates = jnp.zeros((128, 128), f32)
    for k in range(ids_ref.shape[0]):
        hit = ids_ref[k : k + 1, :] == expert
        named += jnp.where(hit, 1.0, 0.0)
        gates += jnp.where(hit, gates_ref[k : k + 1, :], 0.0)
    before = jnp.where(expert < token, 1.0, 0.0).astype(bf16)
    rank = jnp.dot(named.astype(bf16), before, preferred_element_type=f32)
    rank_ref[...] = jnp.where(named > 0.5, rank, -1.0)
    gate_ref[...] = gates

    slot = lax.broadcasted_iota(jnp.int32, (32, 8, 128), 1)

    def choice(part, wanted):
        ranks = rank_ref[pl.ds(part * 32, 32), :]
        return jnp.where(ranks[:, None, :] == wanted.astype(f32), 1.0, 0.0)

    def pack(part, _):
        first = choice(part, slot).reshape(256, 128).astype(bf16)
        send_a[pl.ds(part * 256, 256), :] = jnp.dot(
            first, x_ref[...], preferred_element_type=f32
        ).astype(bf16)
        low = choice(part, jnp.where(slot < 4, slot + 8, 99)).reshape(256, 128).astype(bf16)
        high = choice(part, jnp.where(slot >= 4, slot + 4, 99)).reshape(256, 128).astype(bf16)
        mixed = jnp.dot(low, x_ref[:, :half], preferred_element_type=f32)
        mixed += jnp.dot(high, x_ref[:, half:], preferred_element_type=f32)
        send_b[pl.ds(part * 256, 256), :] = mixed.astype(bf16)
        return 0

    lax.fori_loop(0, 4, pack, 0)
    pl.semaphore_wait(barrier, 127)

    def piece(ref, index):
        return ref.at[pl.ds(index * 8, 8), :]

    def dispatch(k, _):
        there = target(here, k)
        to = number(*there)
        group = lax.div(k, CHUNK)
        send(piece(send_a, to), piece(recv_a, k), out_sem.at[0], in_a_sem.at[group], there).start()
        send(piece(send_b, to), piece(recv_b, k), out_sem.at[1], in_b_sem.at[group], there).start()
        return 0

    own_a = pltpu.make_async_copy(piece(send_a, me), piece(recv_a, 0), in_a_sem.at[0])
    own_b = pltpu.make_async_copy(piece(send_b, me), piece(recv_b, 0), in_b_sem.at[0])
    own_a.start()
    own_b.start()
    lax.fori_loop(1, 128, dispatch, 0)
    load_gate_up.wait()
    load_down.wait()

    tall, short = CHUNK * 8, CHUNK * 4
    row = lax.broadcasted_iota(jnp.int32, (short, tall), 0)
    column = lax.broadcasted_iota(jnp.int32, (short, tall), 1)
    at_low = lax.div(row, 4) * 8 + lax.rem(row, 4)
    take_low = jnp.where(column == at_low, 1.0, 0.0).astype(bf16)
    take_high = jnp.where(column == at_low + 4, 1.0, 0.0).astype(bf16)
    row_t = lax.broadcasted_iota(jnp.int32, (tall, short), 0)
    column_t = lax.broadcasted_iota(jnp.int32, (tall, short), 1)
    at_low_t = lax.div(column_t, 4) * 8 + lax.rem(column_t, 4)
    give_low = jnp.where(row_t == at_low_t, 1.0, 0.0).astype(bf16)
    give_high = jnp.where(row_t == at_low_t + 4, 1.0, 0.0).astype(bf16)

    def work(group, _):
        a_rows = recv_a.at[pl.ds(group * tall, tall), :]
        b_rows = recv_b.at[pl.ds(group * tall, tall), :]
        pltpu.make_async_copy(a_rows, a_rows, in_a_sem.at[group]).wait()
        pltpu.make_async_copy(b_rows, b_rows, in_b_sem.at[group]).wait()
        rows[:tall, :] = a_rows[...]
        rows[tall:, :half] = jnp.dot(
            take_low, b_rows[...], preferred_element_type=f32
        ).astype(bf16)
        rows[tall:, half:] = jnp.dot(
            take_high, b_rows[...], preferred_element_type=f32
        ).astype(bf16)

        def up(tile, _):
            at = pl.multiple_of(tile * 256, 256)
            first = jnp.dot(rows[...], gate_up[:, pl.ds(at, 256)], preferred_element_type=f32)
            second = jnp.dot(
                rows[...], gate_up[:, pl.ds(ff + at, 256)], preferred_element_type=f32
            )
            acts[:, pl.ds(at, 256)] = (jax.nn.silu(first) * second).astype(bf16)
            return 0

        lax.fori_loop(0, ff // 256, up, 0)

        def lower(tile, _):
            at = pl.multiple_of(tile * 512, 512)
            result[:, pl.ds(at, 512)] = jnp.dot(
                acts[...], down[:, pl.ds(at, 512)], preferred_element_type=f32
            ).astype(bf16)
            return 0

        lax.fori_loop(0, width // 512, lower, 0)
        back_a[pl.ds(group * tall, tall), :] = result[:tall, :]
        mixed = jnp.dot(give_low, result[tall:, :half], preferred_element_type=f32)
        mixed += jnp.dot(give_high, result[tall:, half:], preferred_element_type=f32)
        back_b[pl.ds(group * tall, tall), :] = mixed.astype(bf16)

        def give(k, _):
            there = origin(here, k)
            send(piece(back_a, k), piece(home_a, me), back_sem.at[0], home_sem.at[0], there).start()
            send(piece(back_b, k), piece(home_b, me), back_sem.at[1], home_sem.at[1], there).start()
            return 0

        lax.fori_loop(jnp.where(group == 0, 1, group * CHUNK), (group + 1) * CHUNK, give, 0)
        return 0

    lax.fori_loop(0, 128 // CHUNK, work, 0)
    own_c = pltpu.make_async_copy(piece(back_a, 0), piece(home_a, me), home_sem.at[0])
    own_d = pltpu.make_async_copy(piece(back_b, 0), piece(home_b, me), home_sem.at[1])
    own_c.start()
    own_d.start()
    pltpu.make_async_copy(home_a, home_a, home_sem.at[0]).wait()
    pltpu.make_async_copy(home_b, home_b, home_sem.at[1]).wait()

    moe_sum[...] = jnp.zeros_like(moe_sum)
    over_rows = (((0,), (0,)), ((), ()))

    def combine(part, _):
        weight = gate_ref[pl.ds(part * 32, 32), :][:, None, :]

        def add(wanted, values, columns):
            exact = (choice(part, wanted) * weight).reshape(256, 128)
            coarse = exact.astype(bf16)
            fine = (exact - coarse.astype(f32)).astype(bf16)
            moe_sum[:, columns] += lax.dot_general(
                coarse, values, over_rows, preferred_element_type=f32
            ) + lax.dot_general(fine, values, over_rows, preferred_element_type=f32)

        add(slot, home_a[pl.ds(part * 256, 256), :], slice(None))
        values = home_b[pl.ds(part * 256, 256), :]
        add(jnp.where(slot < 4, slot + 8, 99), values, slice(0, half))
        add(jnp.where(slot >= 4, slot + 4, 99), values, slice(half, width))
        return 0

    lax.fori_loop(0, 4, combine, 0)
    out_ref[...] = (mid_ref[...].astype(f32) + moe_sum[...]).astype(bf16)
    others = pl.ds(0, 127 * 8)
    pltpu.make_async_copy(send_a.at[others], send_a.at[others], out_sem.at[0]).wait()
    pltpu.make_async_copy(send_b.at[others], send_b.at[others], out_sem.at[1]).wait()
    pltpu.make_async_copy(back_a.at[others], back_a.at[others], back_sem.at[0]).wait()
    pltpu.make_async_copy(back_b.at[others], back_b.at[others], back_sem.at[1]).wait()


def experts(moe_in, mid, ids, gates, gate_up, down):
    tokens, width = moe_in.shape
    ff = down.shape[0]
    groups = 128 // CHUNK
    vmem = pl.BlockSpec(memory_space=pltpu.VMEM)
    hbm = pl.BlockSpec(memory_space=pl.ANY)
    a_shape = pltpu.VMEM((1024, width), jnp.bfloat16)
    b_shape = pltpu.VMEM((1024, width // 2), jnp.bfloat16)
    return pl.pallas_call(
        moe_kernel,
        out_shape=jax.ShapeDtypeStruct((tokens, width), jnp.bfloat16),
        in_specs=[vmem] * 4 + [hbm] * 2,
        out_specs=vmem,
        scratch_shapes=[
            a_shape,
            b_shape,
            a_shape,
            b_shape,
            a_shape,
            b_shape,
            a_shape,
            b_shape,
            pltpu.VMEM((tokens, width), jnp.float32),
            pltpu.VMEM((width, 2 * ff), jnp.bfloat16),
            pltpu.VMEM((ff, width), jnp.bfloat16),
            pltpu.VMEM((CHUNK * 12, width), jnp.bfloat16),
            pltpu.VMEM((CHUNK * 12, ff), jnp.bfloat16),
            pltpu.VMEM((CHUNK * 12, width), jnp.bfloat16),
            pltpu.VMEM((128, 128), jnp.float32),
            pltpu.VMEM((128, 128), jnp.float32),
            pltpu.SemaphoreType.DMA((2,)),
            pltpu.SemaphoreType.DMA((2,)),
            pltpu.SemaphoreType.DMA((groups,)),
            pltpu.SemaphoreType.DMA((groups,)),
            pltpu.SemaphoreType.DMA((2,)),
            pltpu.SemaphoreType.DMA((2,)),
        ],
        compiler_params=pltpu.CompilerParams(
            collective_id=3, has_side_effects=True, vmem_limit_bytes=60 * 1024 * 1024
        ),
        cost_estimate=pl.CostEstimate(
            flops=20_000_000_000, bytes_accessed=400_000_000, transcendentals=1_000_000
        ),
    )(moe_in, mid, ids.T, gates.T, gate_up, down)


def arrived(ref, sem):
    pltpu.make_async_copy(ref, ref, sem).wait()


class Gather:
    def __init__(self, buf, here, cross, columns, sems):
        self.buf, self.here, self.cross, self.columns = buf, here, cross, columns
        self.send_sem, self.recv_sem, self.cross_sem = sems

    def cut(self, r):
        start, size = self.columns[r]
        return pl.ds(pl.multiple_of(start, 128), size)

    def whole(self, h):
        x, y, z, c = self.here
        start, size = self.columns[0]
        return self.buf.at[y, h, z, :, pl.ds(pl.multiple_of(start, 128), size + self.columns[1][1])]

    def near(self, r):
        x, y, z, c = self.here
        cut = self.cut(r)
        if r == 0:
            return lambda p, h: self.buf.at[y, h, p, :, cut]
        return lambda p, h: self.buf.at[p, h, z, :, cut]

    def far(self, r):
        cut = self.cut(r)
        if r == 0:
            return lambda p, h: self.buf.at[p, h, :, :, cut]
        return lambda p, h: self.buf.at[:, h, p, :, cut]

    def ring(self, r, phase):
        x, y, z, c = self.here
        if (r + phase) % 2 == 0:
            return z, (x, y, lax.rem(z + 1, 4), c), (x, y, lax.rem(z + 3, 4), c)
        return y, (x, lax.rem(y + 1, 4), z, c), (x, lax.rem(y + 3, 4), z, c)

    def start(self):
        own = lax.div(self.here[0], 2)
        send(
            self.whole(own), self.whole(own), self.cross_sem.at[0], self.cross_sem.at[1], self.cross
        ).start()
        self.push(0, own)

    def push(self, phase, h):
        for r in range(2):
            pick = (self.near if phase == 0 else self.far)(r)
            pos, right, left = self.ring(r, phase)
            piece = pick(pos, h)
            for d, there in enumerate((right, left)):
                send(
                    piece,
                    piece,
                    self.send_sem.at[r, phase, d, h],
                    self.recv_sem.at[r, phase, d, h],
                    there,
                ).start()

    def first(self):
        own = lax.div(self.here[0], 2)
        arrived(self.whole(1 - own), self.cross_sem.at[1])
        self.push(0, 1 - own)
        self.forward(0)
        self.rest(0, None)

    def forward(self, phase):
        for d in range(2):
            for r in range(2):
                pick = (self.near if phase == 0 else self.far)(r)
                pos, right, left = self.ring(r, phase)
                arrived(pick(pos, d), self.recv_sem.at[r, phase, d, d])
                piece = pick(lax.rem(pos + (3 if d == 0 else 1), 4), d)
                send(
                    piece,
                    piece,
                    self.send_sem.at[r, phase, 2, d],
                    self.recv_sem.at[r, phase, 2, d],
                    right if d == 0 else left,
                ).start()

    def rest(self, phase, seen):
        for d, h in ((0, 1), (1, 0), (2, 0), (2, 1)):
            for r in range(2):
                pick = (self.near if phase == 0 else self.far)(r)
                pos, _, _ = self.ring(r, phase)
                arrived(pick(pos, h), self.recv_sem.at[r, phase, d, h])
                if seen is not None:
                    seen(r, d, h, pick(lax.rem(pos + (3, 1, 2)[d], 4), h))

    def second(self, seen=None):
        self.push(1, 0)
        self.push(1, 1)
        self.forward(1)
        if seen is not None:
            for d in range(2):
                for r in range(2):
                    pos, _, _ = self.ring(r, 1)
                    seen(r, d, d, self.far(r)(lax.rem(pos + (3, 1)[d], 4), d))
        self.rest(1, seen)

    def drain(self):
        arrived(self.whole(0), self.cross_sem.at[0])
        for r in range(2):
            for phase in range(2):
                pick = (self.near if phase == 0 else self.far)(r)
                for d in range(3):
                    for h in range(2):
                        arrived(pick(0, h), self.send_sem.at[r, phase, d, h])


def request_bounds(lengths_ref, row):
    ends = [lengths_ref[row, 0]]
    for r in range(1, 3):
        ends.append(ends[-1] + lengths_ref[row, r])
    return ends


def front_kernel(
    lengths_ref,
    hidden_ref,
    gain_ref,
    shard_ref,
    out_shard_ref,
    pool_ref,
    q_gain_ref,
    k_gain_ref,
    freq_ref,
    q_ref,
    kv_ref,
    cache_ref,
    w_out_ref,
    pages_ref,
    weight,
    qkv,
    normed_ref,
    w_sems,
    k_sems,
    o_sems,
    cross_sems,
    w_swap,
    o_swap,
    pool_sems,
    local_sem,
):
    f32, bf16 = jnp.float32, jnp.bfloat16
    here = place()
    x, y, z, c = here
    own = lax.div(x, 2)
    columns = weight.shape[-1]
    side = columns // 2
    partner = (x, y, z, 1 - c)
    even = 1 - lax.rem(x, 2)
    across = (lax.rem(x + 1 + 2 * even, 4), y, z, c)
    opposite = (lax.rem(x + 2, 4), y, z, c)
    upper = (lax.rem(x + 1, 4), y, z, c)
    lower = (lax.rem(x + 3, 4), y, z, c)
    barrier = pltpu.get_barrier_semaphore()
    peers = (
        partner,
        opposite,
        upper,
        lower,
        (x, lax.rem(y + 1, 4), z, c),
        (x, lax.rem(y + 3, 4), z, c),
        (x, y, lax.rem(z + 1, 4), c),
        (x, y, lax.rem(z + 3, 4), c),
    )
    for peer in peers:
        pl.semaphore_signal(barrier, inc=1, device_id=device(*peer), device_id_type=MESH_ID)
    out_side = w_out_ref.shape[-1] // 2
    mine = pl.ds(pl.multiple_of(c * side, 128), side)
    mine_out = pl.ds(pl.multiple_of(c * out_side, 128), out_side)
    held = pool_ref.shape[0]
    row = lax.rem(x, 2) * 2 + c
    seeds = (
        pltpu.make_async_copy(
            shard_ref.at[:, mine], weight.at[y, own, z, :, mine], local_sem.at[0]
        ),
        pltpu.make_async_copy(
            out_shard_ref.at[:, mine_out], w_out_ref.at[y, own, z, :, mine_out], local_sem.at[1]
        ),
        pltpu.make_async_copy(pool_ref, pages_ref.at[pl.ds(row * held, held)], local_sem.at[2]),
    )
    for seed in seeds:
        seed.start()
    seeds[0].wait()
    pl.semaphore_wait(barrier, len(peers))

    gather = Gather(
        weight,
        here,
        across,
        ((c * side, side // 2), (c * side + side // 2, side // 2)),
        (w_sems.at[0], w_sems.at[1], cross_sems.at[0]),
    )
    gather.start()
    seeds[1].wait()
    seeds[2].wait()
    project_out = Gather(
        w_out_ref,
        here,
        across,
        ((c * out_side, out_side // 2), (c * out_side + out_side // 2, out_side // 2)),
        (o_sems.at[0], o_sems.at[1], cross_sems.at[1]),
    )

    def pool_send(slot, first, count, there):
        piece = pages_ref.at[pl.ds(first, count)]
        copy = send(piece, piece, pool_sems.at[0, slot], pool_sems.at[1, slot], there)
        copy.start()
        return copy

    few = held // 2
    far_row = (1 - lax.rem(x, 2)) * 2 + c
    pool_copies = [
        pool_send(0, row * held, few, upper),
        pool_send(1, row * held + few, few, lower),
        pool_send(2, row * held, held, partner),
    ]

    value = hidden_ref[...].astype(f32)
    mean = jnp.mean(value * value, axis=-1, keepdims=True)
    normed_ref[...] = (value * lax.rsqrt(mean + eps) * gain_ref[...]).astype(bf16)

    gather.first()

    def swapper(sems, kept):
        def swap(r, slot, piece):
            copy = send(piece, piece, sems.at[0, r, slot], sems.at[1, r, slot], partner)
            copy.start()
            kept.append(copy)

        return swap

    def swap_near(target, ref, swap):
        for r in range(2):
            pos, _, _ = target.ring(r, 1)
            cut = target.cut(r)
            swap(r, 6, ref.at[pos, :, :, :, cut] if r == 0 else ref.at[:, :, pos, :, cut])

    def swap_forwarded(target, swap):
        for d in range(2):
            for r in range(2):
                pos, _, _ = target.ring(r, 1)
                swap(r, d * 2 + d, target.far(r)(lax.rem(pos + (3, 1)[d], 4), d))

    w_kept, o_kept = [], []
    w_pair = swapper(w_swap, w_kept)
    o_pair = swapper(o_swap, o_kept)
    gather.push(1, 0)
    gather.push(1, 1)
    swap_near(gather, weight, w_pair)
    project_out.start()
    gather.forward(1)
    swap_forwarded(gather, w_pair)
    gather.rest(1, lambda r, d, h, piece: w_pair(r, d * 2 + h, piece))
    project_out.first()
    project_out.push(1, 0)
    project_out.push(1, 1)
    for copy in w_kept:
        copy.wait_recv()
    swap_near(project_out, w_out_ref, o_pair)

    span = 2 * 4 * weight.shape[3]

    def project(tile, _):
        at = pl.multiple_of(tile * 512, 512)
        total = jnp.zeros((normed_ref.shape[0], 512), f32)
        for plane in range(4):
            block = weight[plane, :, :, :, pl.ds(at, 512)].reshape(span, 512)
            total += jnp.dot(
                normed_ref[:, plane * span : (plane + 1) * span],
                block,
                preferred_element_type=f32,
            )
        qkv[:, pl.ds(at, 512)] = total
        return 0

    tokens = hidden_ref.shape[0]
    index = (y * 8 + own * 4 + z) * tokens + lax.broadcasted_iota(jnp.int32, (tokens, 128), 0)
    start = jnp.zeros_like(index)
    for end in request_bounds(lengths_ref, row):
        start = jnp.where(index >= end, end, start)
    angles = (PREFIX_TOKENS + index - start).astype(f32) * freq_ref[...]
    cosine = jnp.cos(angles)
    sine = jnp.sin(angles)
    lane = lax.broadcasted_iota(jnp.int32, (tokens, 128), 1)
    sine = jnp.where(lane < 64, -sine, sine)
    heads = columns // 128

    def turned(head, gain):
        rows = qkv[:, pl.ds(pl.multiple_of(head * 128, 128), 128)]
        mean = jnp.mean(rows * rows, axis=-1, keepdims=True)
        rows = rows * lax.rsqrt(mean + eps) * gain
        return (rows * cosine + pltpu.roll(rows, 64, 1) * sine).astype(bf16)

    project(columns // 512 - 1, 0)
    for h in range(2):
        cache_ref[:, h * 128 : (h + 1) * 128] = turned(heads - 4 + h, k_gain_ref[...])
    cache_ref[:, 256:512] = qkv[:, columns - 256 :].astype(bf16)
    seed = pltpu.make_async_copy(cache_ref, kv_ref.at[y, own, z], local_sem.at[0])
    seed.start()
    seed.wait()
    spread = Gather(
        kv_ref,
        here,
        opposite,
        ((0, 256), (256, 256)),
        (k_sems.at[0], k_sems.at[1], cross_sems.at[2]),
    )
    spread.start()
    lax.fori_loop(0, columns // 512 - 1, project, 0)

    def query(head, _):
        at = pl.multiple_of(lax.rem(head, 8) * 128, 128)
        q_ref[lax.div(head, 8), pl.ds(at, 128), :] = turned(head, q_gain_ref[...])
        return 0

    spread.first()
    spread.push(1, 0)
    spread.push(1, 1)
    arrived(pages_ref.at[pl.ds(0, few)], pool_sems.at[1, 0])
    arrived(pages_ref.at[pl.ds(0, few)], pool_sems.at[1, 1])
    pool_copies.append(pool_send(3, far_row * held, held, partner))
    lax.fori_loop(0, heads - 4, query, 0)
    spread.forward(1)
    project_out.forward(1)
    swap_forwarded(project_out, o_pair)
    spread.rest(1, None)
    project_out.rest(1, lambda r, d, h, piece: o_pair(r, d * 2 + h, piece))
    for copy in o_kept:
        copy.wait_recv()
    for copy in pool_copies[2:]:
        copy.wait_recv()
    gather.drain()
    spread.drain()
    project_out.drain()
    for copy in w_kept + o_kept + pool_copies:
        copy.wait_send()


def front(lengths, hidden, gain, shard, out_shard, pool, q_gain, k_gain, freqs):
    tokens, width = hidden.shape
    rows, columns = shard.shape
    vmem = pl.BlockSpec(memory_space=pltpu.VMEM)
    smem = pl.BlockSpec(memory_space=pltpu.SMEM)
    hbm = pl.BlockSpec(memory_space=pl.ANY)
    ring = pltpu.SemaphoreType.DMA((2, 2, 2, 3, 2))
    swap = pltpu.SemaphoreType.DMA((2, 2, 7))
    return pl.pallas_call(
        front_kernel,
        out_shape=(
            jax.ShapeDtypeStruct((2, 8 * tokens, 128), jnp.bfloat16),
            jax.ShapeDtypeStruct((4, 2, 4, tokens, 512), jnp.bfloat16),
            jax.ShapeDtypeStruct((tokens, 512), jnp.bfloat16),
            jax.ShapeDtypeStruct((4, 2, 4) + out_shard.shape, jnp.bfloat16),
            jax.ShapeDtypeStruct((4 * pool.shape[0],) + pool.shape[1:], jnp.bfloat16),
        ),
        in_specs=[smem] + [vmem] * 8,
        out_specs=(vmem, hbm, vmem, hbm, hbm),
        scratch_shapes=[
            pltpu.VMEM((4, 2, 4, rows, columns), jnp.bfloat16),
            pltpu.VMEM((tokens, columns), jnp.float32),
            pltpu.VMEM((tokens, width), jnp.bfloat16),
            ring,
            ring,
            ring,
            pltpu.SemaphoreType.DMA((3, 2)),
            swap,
            swap,
            pltpu.SemaphoreType.DMA((2, 4)),
            pltpu.SemaphoreType.DMA((3,)),
        ],
        compiler_params=pltpu.CompilerParams(
            collective_id=1, has_side_effects=True, vmem_limit_bytes=56 * 1024 * 1024
        ),
        cost_estimate=pl.CostEstimate(
            flops=1_400_000_000, bytes_accessed=200_000_000, transcendentals=1_000_000
        ),
    )(lengths, hidden, gain, shard, out_shard, pool, q_gain, k_gain, freqs)


def attention_kernel(
    table,
    lengths_ref,
    groups_ref,
    q_ref,
    hidden_ref,
    gain_ref,
    kv_hbm,
    pool_hbm,
    w_out_hbm,
    mid_ref,
    moe_ref,
    kv_ref,
    pool_ref,
    w_out_ref,
    mixed,
    high,
    total,
    acc,
    sems,
):
    f32, bf16 = jnp.float32, jnp.bfloat16
    loads = (
        pltpu.make_async_copy(pool_hbm, pool_ref, sems.at[0]),
        pltpu.make_async_copy(kv_hbm, kv_ref, sems.at[1]),
        pltpu.make_async_copy(w_out_hbm, w_out_ref, sems.at[2]),
    )
    for load in loads:
        load.start()
    row = lax.axis_index("dp")
    first = lax.axis_index("expert") * hidden_ref.shape[0]
    last = first + hidden_ref.shape[0] - 1
    index = first + lax.broadcasted_iota(jnp.int32, (1, 128), 1)
    start = jnp.zeros_like(index)
    group_of = jnp.zeros_like(index) + groups_ref[row, 0]
    earliest, latest = jnp.int32(0), jnp.int32(0)
    begin = jnp.int32(0)
    counts = [jnp.int32(0), jnp.int32(0)]
    for r in range(4):
        end = begin + lengths_ref[row, r]
        of = groups_ref[row, r]
        if r > 0:
            start = jnp.where(index >= begin, begin, start)
            group_of = jnp.where(index >= begin, of, group_of)
            earliest = jnp.where(first >= begin, begin, earliest)
            latest = jnp.where(last >= begin, begin, latest)
        inside = jnp.maximum(jnp.minimum(end, last + 1) - jnp.maximum(begin, first), 0)
        counts[0] += jnp.where(of == 0, inside, 0)
        counts[1] += jnp.where(of == 1, inside, 0)
        begin = end
    everyone = last - first + 1
    factor = math.log2(math.e) / math.sqrt(128)
    high[...] = jnp.full_like(high, floor_value)
    total[...] = jnp.zeros_like(total)
    acc[...] = jnp.zeros_like(acc)

    def step(h, keys, values, seen):
        scores = lax.dot_general(
            keys, q_ref[h], (((1,), (1,)), ((), ())), preferred_element_type=f32
        )
        if seen is not None:
            scores = jnp.where(jnp.concatenate([seen] * 8, axis=1), scores, -jnp.inf)
        old = high[h]
        new = jnp.maximum(old, jnp.max(scores, axis=0, keepdims=True))
        weights = jnp.exp2((scores - new) * factor)
        shrink = jnp.exp2((old - new) * factor)
        high[h] = new
        total[h] = total[h] * shrink + jnp.sum(weights, axis=0, keepdims=True)
        acc[h] = acc[h] * shrink + lax.dot_general(
            values, weights.astype(bf16), (((0,), (0,)), ((), ())), preferred_element_type=f32
        )

    span = 4
    loads[0].wait()
    for group in range(2):

        def pages(seen, group=group):
            def body(j, _):
                picked = [table[group * 16 + j * span + i] for i in range(span)]
                for h in range(2):
                    keys = jnp.concatenate([pool_ref[p, 0, h] for p in picked], axis=0)
                    values = jnp.concatenate([pool_ref[p, 1, h] for p in picked], axis=0)
                    step(h, keys, values, seen)
                return 0

            lax.fori_loop(0, 16 // span, body, 0)

        @pl.when(counts[group] == everyone)
        def _():
            pages(None)

        @pl.when((counts[group] > 0) & (counts[group] < everyone))
        def _():
            pages(jnp.broadcast_to(group_of == group, (span * 128, 128)))

    loads[1].wait()
    size = 256

    def suffix(tile, masked):
        at = pl.multiple_of(tile * size, size)
        seen = None
        if masked:
            place_of = at + lax.broadcasted_iota(jnp.int32, (size, 128), 0)
            seen = (place_of >= start) & (place_of <= index)
        for h in range(2):
            keys = kv_ref[pl.ds(at, size), h * 128 : (h + 1) * 128]
            values = kv_ref[pl.ds(at, size), 256 + h * 128 : 256 + (h + 1) * 128]
            step(h, keys, values, seen)

    def tiles(tile, _):
        clear = (tile * size >= latest) & (tile * size + size <= first + 1)

        @pl.when(clear)
        def _():
            suffix(tile, False)

        @pl.when(jnp.logical_not(clear))
        def _():
            suffix(tile, True)

        return 0

    lax.fori_loop(lax.div(earliest, size), lax.div(last, size) + 1, tiles, 0)
    for h in range(2):
        done = acc[h] / total[h]
        for g in range(8):
            head = h * 8 + g
            mixed[:, head * 128 : (head + 1) * 128] = (
                done[:, g * 128 : (g + 1) * 128].T.astype(bf16)
            )


    loads[2].wait()

    def project(tile, square):
        at = pl.multiple_of(tile * 512, 512)
        part = jnp.dot(mixed[...], w_out_ref[:, pl.ds(at, 512)], preferred_element_type=f32)
        mid = (hidden_ref[:, pl.ds(at, 512)].astype(f32) + part).astype(bf16)
        mid_ref[:, pl.ds(at, 512)] = mid
        mid = mid.astype(f32)
        return square + jnp.sum(mid * mid, axis=-1, keepdims=True)

    width = hidden_ref.shape[1]
    square = lax.fori_loop(0, width // 512, project, jnp.zeros((hidden_ref.shape[0], 1), f32))
    factor_of = lax.rsqrt(square / width + eps)
    moe_ref[...] = (mid_ref[...].astype(f32) * factor_of * gain_ref[...]).astype(bf16)


def attention(table, lengths, groups, q, hidden, gain, kv, pool, w_out):
    vmem = pl.BlockSpec(memory_space=pltpu.VMEM)
    smem = pl.BlockSpec(memory_space=pltpu.SMEM)
    hbm = pl.BlockSpec(memory_space=pl.ANY)
    tokens, width = hidden.shape
    row = jax.ShapeDtypeStruct((tokens, width), jnp.bfloat16)
    return pl.pallas_call(
        attention_kernel,
        out_shape=(row, row),
        in_specs=[smem] * 3 + [vmem] * 3 + [hbm] * 3,
        out_specs=(vmem, vmem),
        scratch_shapes=[
            pltpu.VMEM(kv.shape, jnp.bfloat16),
            pltpu.VMEM(pool.shape, jnp.bfloat16),
            pltpu.VMEM(w_out.shape, jnp.bfloat16),
            pltpu.VMEM((tokens, width), jnp.bfloat16),
            pltpu.VMEM((2, 1, 8 * tokens), jnp.float32),
            pltpu.VMEM((2, 1, 8 * tokens), jnp.float32),
            pltpu.VMEM((2, 128, 8 * tokens), jnp.float32),
            pltpu.SemaphoreType.DMA((3,)),
        ],
        compiler_params=pltpu.CompilerParams(vmem_limit_bytes=56 * 1024 * 1024),
        cost_estimate=pl.CostEstimate(
            flops=5_000_000_000, bytes_accessed=10_000_000, transcendentals=10_000_000
        ),
    )(table, lengths, groups, q, hidden, gain, kv, pool, w_out)


def local(
    hidden_in,
    attn_gain,
    query_key_value_weight,
    q_gain,
    key_norm_gain,
    w_out,
    moe_gain,
    w_gate_up,
    w_down,
    kv_pool,
    page_table,
    suffix_lengths,
    request_group,
    expert_ids,
    gate_weights,
):
    tokens_here, width = hidden_in.shape
    half = q_gain.shape[0] // 2
    freqs = theta ** (-jnp.arange(half, dtype=jnp.float32) / half)
    q, kv, suffix_cache, w_out_all, pool = front(
        suffix_lengths,
        hidden_in,
        attn_gain[None],
        query_key_value_weight,
        w_out,
        kv_pool.transpose(0, 1, 3, 2, 4),
        q_gain[None],
        key_norm_gain[None],
        jnp.concatenate([freqs, freqs])[None],
    )
    mid, moe_in = attention(
        page_table,
        suffix_lengths,
        request_group,
        q,
        hidden_in,
        moe_gain[None],
        kv.reshape(32 * tokens_here, 512),
        pool,
        w_out_all.reshape(32 * w_out.shape[0], width),
    )
    hidden_out = experts(moe_in, mid, expert_ids, gate_weights, w_gate_up[0], w_down[0])
    return (hidden_out, suffix_cache)


def solution(mesh):
    return jax.shard_map(
        local,
        mesh=mesh,
        in_specs=(
            P(("dp", "expert"), None),
            P(),
            P("expert", None),
            P(),
            P(),
            P("expert", None),
            P(),
            P(("dp", "expert"), None, None),
            P(("dp", "expert"), None, None),
            P("dp", None, None, None, None),
            P(),
            P(),
            P(),
            P(("dp", "expert"), None),
            P(("dp", "expert"), None),
        ),
        out_specs=(P(("dp", "expert"), None), P(("dp", "expert"), None)),
        check_vma=False,
    )
```

```python
import math

import jax
import jax.numpy as jnp
from jax import lax
from jax.experimental import pallas as pl
from jax.experimental.pallas import tpu as pltpu
from jax.sharding import PartitionSpec as P

PREFIX_TOKENS = 2048


eps = 1e-06
theta = 1000000.0
floor_value = -1e30


MESH_ID = pl.DeviceIdType.MESH
STEP = 45
PARTS = (0, 640, 1280, 2048)


def place():
    dp = lax.axis_index("dp")
    ex = lax.axis_index("expert")
    x = lax.rem(lax.div(ex, 4), 2) * 2 + lax.div(dp, 2)
    return (x, lax.div(ex, 8), lax.rem(ex, 4), lax.rem(dp, 2))


def device(x, y, z, c):
    return {"dp": lax.rem(x, 2) * 2 + c, "expert": y * 8 + lax.div(x, 2) * 4 + z}


def number(x, y, z, c):
    return (lax.rem(x, 2) * 2 + c) * 32 + y * 8 + lax.div(x, 2) * 4 + z


def greet_all(here):
    barrier = pltpu.get_barrier_semaphore()
    x, y, z, c = here

    def tell(k, _):
        there = (
            lax.rem(x + lax.div(k, 32), 4),
            lax.rem(y + lax.rem(lax.div(k, 8), 4), 4),
            lax.rem(z + lax.rem(lax.div(k, 2), 4), 4),
            lax.rem(c + k, 2),
        )
        pl.semaphore_signal(barrier, inc=1, device_id=device(*there), device_id_type=MESH_ID)
        return 0

    lax.fori_loop(1, 128, tell, 0)
    return barrier


def send(src, dst, send_sem, recv_sem, where):
    return pltpu.make_async_remote_copy(
        src_ref=src,
        dst_ref=dst,
        send_sem=send_sem,
        recv_sem=recv_sem,
        device_id=device(*where),
        device_id_type=MESH_ID,
    )


def part_columns(p):
    return slice(PARTS[p], PARTS[p + 1])


def in_plane(p, here):
    x, y, z, c = here
    return ((y, z), (z, x), (y, x))[p]


def at_plane(p, here, a, b, c):
    x, y, z, _ = here
    return ((x, a, b, c), (b, y, a, c), (b, a, z, c))[p]


def on_line(p, here, d):
    moved = list(here)
    moved[p] = lax.rem(here[p] + d, 4)
    return tuple(moved)


def moe_kernel(
    x_ref,
    mid_ref,
    info_ref,
    gate_up_hbm,
    down_hbm,
    out_ref,
    line,
    infos,
    pack_a,
    pack_b,
    recv_a,
    recv_b,
    home_a,
    home_b,
    rows,
    acts,
    result,
    partial,
    inbox,
    ranks,
    gates,
    gate_up,
    down,
    weight_sem,
    line_send,
    line_recv,
    info_send,
    info_recv,
    out_sem,
    in_sem,
    back_sem,
    home_sem,
    sum_send,
    sum_recv,
):
    f32, bf16 = jnp.float32, jnp.bfloat16
    ff = down.shape[0]
    here = place()
    c = here[3]
    load_gate_up = pltpu.make_async_copy(gate_up_hbm, gate_up, weight_sem.at[0])
    load_down = pltpu.make_async_copy(down_hbm, down, weight_sem.at[1])
    load_gate_up.start()
    load_down.start()
    barrier = greet_all(here)
    pl.semaphore_wait(barrier, 127)

    for p in range(3):
        own = here[p]
        pltpu.make_async_copy(info_ref, infos.at[p, own], info_recv.at[p]).start()
        for d in (1, 3, 2):
            send(
                info_ref, infos.at[p, own], info_send.at[p], info_recv.at[p], on_line(p, here, d)
            ).start()
    for d in (1, 3, 2):
        for p in range(3):
            cut = part_columns(p)
            send(
                x_ref.at[:, cut],
                line.at[here[p], :, cut],
                line_send.at[p],
                line_recv.at[p],
                on_line(p, here, d),
            ).start()
    for p in range(3):
        cut = part_columns(p)
        pltpu.make_async_copy(
            x_ref.at[:, cut], line.at[here[p], :, cut], line_recv.at[p]
        ).start()

    local = lax.broadcasted_iota(jnp.int32, (32, 128), 0)
    before = jnp.where(
        lax.broadcasted_iota(jnp.int32, (128, 128), 0)
        < lax.broadcasted_iota(jnp.int32, (128, 128), 1),
        1.0,
        0.0,
    ).astype(bf16)
    for p in range(3):
        arrived(infos.at[p], info_recv.at[p])
        expert = number(
            *at_plane(
                p,
                here,
                lax.rem(lax.div(local, 4), 4),
                lax.rem(local, 4),
                lax.div(local, 16),
            )
        ).astype(f32)
        for q in range(4):
            named = jnp.zeros((32, 128), f32)
            gate = jnp.zeros((32, 128), f32)
            for k in range(8):
                hit = infos[p, q, k : k + 1, :] == expert
                named += jnp.where(hit, 1.0, 0.0)
                gate += jnp.where(hit, infos[p, q, 8 + k : 9 + k, :], 0.0)
            rank = jnp.dot(named.astype(bf16), before, preferred_element_type=f32)
            ranks[p, :, q * 128 : (q + 1) * 128] = jnp.where(named > 0.5, rank, 99.0)
            gates[p, :, q * 128 : (q + 1) * 128] = gate

    quarter = lax.div(lax.broadcasted_iota(jnp.int32, (1, 512), 1), 128).astype(f32)

    def choice(p, group, low, count):
        many = 256 // (4 * count)
        rank = ranks[p, pl.ds(group * many, many), :]
        rank = jnp.where(
            (rank >= low) & (rank < low + count), rank - low + count * quarter, -1.0
        )
        wanted = lax.broadcasted_iota(jnp.int32, (many, 4 * count, 512), 1).astype(f32)
        return jnp.where(rank[:, None, :] == wanted, 1.0, 0.0)

    halves = ((0, 8, pack_a, recv_a, home_a), (8, 4, pack_b, recv_b, home_b))

    def pack(half):
        low, count, packed, _, _ = halves[half]

        def body(group, _):
            for p in range(3):
                cut = part_columns(p)
                chosen = choice(p, group, low, count).reshape(256, 512).astype(bf16)
                values = line[:, :, cut].reshape(512, cut.stop - cut.start)
                packed[pl.ds(group * 256, 256), cut] = jnp.dot(
                    chosen, values, preferred_element_type=f32
                ).astype(bf16)
            return 0

        lax.fori_loop(0, count // 2, body, 0)

    def block(ref, index, size, p):
        return ref.at[pl.ds(index * size, size), part_columns(p)]

    def exchange(src, dst, size, send_sem, recv_sem):
        sign = 1 - 2 * c

        def body(k, _):
            o = lax.rem(k * STEP, 32)
            for p in range(3):
                a, b = in_plane(p, here)
                to_a = lax.rem(a + sign * lax.rem(lax.div(o, 4), 4) + 4, 4)
                to_b = lax.rem(b + sign * lax.rem(o, 4) + 4, 4)
                to_c = lax.rem(c + lax.div(o, 16), 2)
                send(
                    block(src, to_c * 16 + to_a * 4 + to_b, size, p),
                    block(dst, c * 16 + a * 4 + b, size, p),
                    send_sem.at[p],
                    recv_sem.at[p],
                    at_plane(p, here, to_a, to_b, to_c),
                ).start()
            return 0

        lax.fori_loop(1, 32, body, 0)
        for p in range(3):
            a, b = in_plane(p, here)
            index = c * 16 + a * 4 + b
            pltpu.make_async_copy(
                block(src, index, size, p), block(dst, index, size, p), recv_sem.at[p]
            ).start()

    for p in range(3):
        cut = part_columns(p)
        arrived(line.at[:, :, cut], line_recv.at[p])
    for half in range(2):
        low, count, packed, received, _ = halves[half]
        pack(half)
        exchange(packed, received, 4 * count, out_sem.at[half], in_sem.at[half])
    load_gate_up.wait()
    load_down.wait()

    def swapped(count):
        size = 16 * count
        row = lax.broadcasted_iota(jnp.int32, (size, size), 0)
        column = lax.broadcasted_iota(jnp.int32, (size, size), 1)
        source = (
            lax.rem(lax.div(row, count), 4) * 4 * count
            + lax.div(row, 4 * count) * count
            + lax.rem(row, count)
        )
        return jnp.where(column == source, 1.0, 0.0).astype(bf16)

    def others(ref, size, p):
        return ref.at[pl.ds(0, 31 * size), part_columns(p)]

    for half in range(2):
        low, count, packed, received, home = halves[half]
        size = 4 * count
        total = 32 * size
        for p in range(3):
            arrived(received.at[:, part_columns(p)], in_sem.at[half, p])
        turn = swapped(count)
        rows[:total, part_columns(0)] = received[:, part_columns(0)]

        def unpack(group, _):
            core, a = lax.div(group, 4), lax.rem(group, 4)
            cut = part_columns(1)
            block_y = jnp.dot(
                turn, received[pl.ds(group * 4 * size, 4 * size), cut], preferred_element_type=f32
            ).astype(bf16)
            for y in range(4):
                at = (core * 16 + y * 4 + a) * size
                rows[pl.ds(pl.multiple_of(at, size), size), cut] = block_y[
                    y * size : (y + 1) * size
                ]
            cut = part_columns(2)
            rows[pl.ds(group * 4 * size, 4 * size), cut] = jnp.dot(
                turn, received[pl.ds(group * 4 * size, 4 * size), cut], preferred_element_type=f32
            ).astype(bf16)
            return 0

        lax.fori_loop(0, 8, unpack, 0)

        def up(tile, _):
            at = pl.multiple_of(tile * 256, 256)
            values = rows[:total, :]
            first = jnp.dot(values, gate_up[:, pl.ds(at, 256)], preferred_element_type=f32)
            second = jnp.dot(values, gate_up[:, pl.ds(ff + at, 256)], preferred_element_type=f32)
            acts[:total, pl.ds(at, 256)] = (jax.nn.silu(first) * second).astype(bf16)
            return 0

        lax.fori_loop(0, ff // 256, up, 0)
        for p in range(3):
            arrived(others(packed, size, p), out_sem.at[half, p])

        def lower(group, _):
            at = pl.multiple_of(group * 256, 256)
            for p in range(3):
                cut = part_columns(p)
                value = jnp.dot(
                    acts[pl.ds(at, 256), :], down[:, cut], preferred_element_type=f32
                ).astype(bf16)
                if p == 0:
                    packed[pl.ds(at, 256), cut] = value
                else:
                    result[pl.ds(at, 256), cut.start - PARTS[1] : cut.stop - PARTS[1]] = value
            return 0

        lax.fori_loop(0, total // 256, lower, 0)

        def repack(group, _):
            core, a = lax.div(group, 4), lax.rem(group, 4)
            cut = slice(0, PARTS[2] - PARTS[1])
            pieces = []
            for y in range(4):
                at = (core * 16 + y * 4 + a) * size
                pieces.append(result[pl.ds(pl.multiple_of(at, size), size), cut])
            packed[pl.ds(group * 4 * size, 4 * size), part_columns(1)] = jnp.dot(
                turn, jnp.concatenate(pieces, axis=0), preferred_element_type=f32
            ).astype(bf16)
            cut = slice(PARTS[2] - PARTS[1], PARTS[3] - PARTS[1])
            packed[pl.ds(group * 4 * size, 4 * size), part_columns(2)] = jnp.dot(
                turn, result[pl.ds(group * 4 * size, 4 * size), cut], preferred_element_type=f32
            ).astype(bf16)
            return 0

        lax.fori_loop(0, 8, repack, 0)
        exchange(packed, home, size, back_sem.at[half], home_sem.at[half])

    partial[...] = jnp.zeros_like(partial)
    over_rows = (((0,), (0,)), ((), ()))
    for half in range(2):
        low, count, packed, received, home = halves[half]
        many = 256 // (4 * count)
        for p in range(3):
            arrived(home.at[:, part_columns(p)], home_sem.at[half, p])

        def combine(group, _):
            for p in range(3):
                cut = part_columns(p)
                gate = gates[p, pl.ds(group * many, many), :]
                exact = (choice(p, group, low, count) * gate[:, None, :]).reshape(256, 512)
                coarse = exact.astype(bf16)
                fine = (exact - coarse.astype(f32)).astype(bf16)
                values = home[pl.ds(group * 256, 256), cut]
                partial[:, cut] += lax.dot_general(
                    coarse, values, over_rows, preferred_element_type=f32
                ) + lax.dot_general(fine, values, over_rows, preferred_element_type=f32)
            return 0

        lax.fori_loop(0, count // 2, combine, 0)

    rows[:512, :] = partial[...].astype(bf16)
    for d in (1, 3, 2):
        for p in range(3):
            cut = part_columns(p)
            there = on_line(p, here, d)
            send(
                rows.at[pl.ds(there[p] * 128, 128), cut],
                inbox.at[here[p], :, cut],
                sum_send.at[p],
                sum_recv.at[p],
                there,
            ).start()
    for p in range(3):
        cut = part_columns(p)
        arrived(inbox.at[pl.ds(0, 3), :, cut], sum_recv.at[p])
        total = partial[pl.ds(pl.multiple_of(here[p] * 128, 128), 128), cut]
        for d in range(1, 4):
            total += inbox[lax.rem(here[p] + d, 4), :, cut].astype(f32)
        out_ref[:, cut] = (mid_ref[:, cut].astype(f32) + total).astype(bf16)

    for p in range(3):
        cut = part_columns(p)
        arrived(infos.at[p, pl.ds(0, 3)], info_send.at[p])
        arrived(inbox.at[pl.ds(0, 3), :, cut], line_send.at[p])
        arrived(inbox.at[pl.ds(0, 3), :, cut], sum_send.at[p])
        for half in range(2):
            _, count, packed, _, _ = halves[half]
            arrived(others(packed, 4 * count, p), back_sem.at[half, p])


def experts(moe_in, mid, ids, gates, gate_up, down):
    tokens, width = moe_in.shape
    ff = down.shape[0]
    bf16 = jnp.bfloat16
    vmem = pl.BlockSpec(memory_space=pltpu.VMEM)
    hbm = pl.BlockSpec(memory_space=pl.ANY)
    a_shape = pltpu.VMEM((1024, width), bf16)
    b_shape = pltpu.VMEM((512, width), bf16)
    three = pltpu.SemaphoreType.DMA((3,))
    six = pltpu.SemaphoreType.DMA((2, 3))
    info = jnp.concatenate([ids.T.astype(jnp.float32), gates.T], axis=0)
    return pl.pallas_call(
        moe_kernel,
        out_shape=jax.ShapeDtypeStruct((tokens, width), bf16),
        in_specs=[vmem] * 3 + [hbm] * 2,
        out_specs=vmem,
        scratch_shapes=[
            pltpu.VMEM((4, tokens, width), bf16),
            pltpu.VMEM((3, 4, 16, tokens), jnp.float32),
            a_shape,
            b_shape,
            a_shape,
            b_shape,
            a_shape,
            b_shape,
            a_shape,
            pltpu.VMEM((1024, ff), bf16),
            pltpu.VMEM((1024, PARTS[3] - PARTS[1]), bf16),
            pltpu.VMEM((512, width), jnp.float32),
            pltpu.VMEM((4, tokens, width), bf16),
            pltpu.VMEM((3, 32, 512), jnp.float32),
            pltpu.VMEM((3, 32, 512), jnp.float32),
            pltpu.VMEM((width, 2 * ff), bf16),
            pltpu.VMEM((ff, width), bf16),
            pltpu.SemaphoreType.DMA((2,)),
            three,
            three,
            three,
            three,
            six,
            six,
            six,
            six,
            three,
            three,
        ],
        compiler_params=pltpu.CompilerParams(
            collective_id=3, has_side_effects=True, vmem_limit_bytes=63 * 1024 * 1024
        ),
        cost_estimate=pl.CostEstimate(
            flops=20_000_000_000, bytes_accessed=400_000_000, transcendentals=1_000_000
        ),
    )(moe_in, mid, info, gate_up, down)


def arrived(ref, sem):
    pltpu.make_async_copy(ref, ref, sem).wait()


class Gather:
    def __init__(self, buf, here, cross, columns, sems):
        self.buf, self.here, self.cross, self.columns = buf, here, cross, columns
        self.send_sem, self.recv_sem, self.cross_sem = sems

    def cut(self, r):
        start, size = self.columns[r]
        return pl.ds(pl.multiple_of(start, 128), size)

    def whole(self, h):
        x, y, z, c = self.here
        start, size = self.columns[0]
        return self.buf.at[y, h, z, :, pl.ds(pl.multiple_of(start, 128), size + self.columns[1][1])]

    def near(self, r):
        x, y, z, c = self.here
        cut = self.cut(r)
        if r == 0:
            return lambda p, h: self.buf.at[y, h, p, :, cut]
        return lambda p, h: self.buf.at[p, h, z, :, cut]

    def far(self, r):
        cut = self.cut(r)
        if r == 0:
            return lambda p, h: self.buf.at[p, h, :, :, cut]
        return lambda p, h: self.buf.at[:, h, p, :, cut]

    def ring(self, r, phase):
        x, y, z, c = self.here
        if (r + phase) % 2 == 0:
            return z, (x, y, lax.rem(z + 1, 4), c), (x, y, lax.rem(z + 3, 4), c)
        return y, (x, lax.rem(y + 1, 4), z, c), (x, lax.rem(y + 3, 4), z, c)

    def start(self):
        own = lax.div(self.here[0], 2)
        send(
            self.whole(own), self.whole(own), self.cross_sem.at[0], self.cross_sem.at[1], self.cross
        ).start()
        self.push(0, own)

    def push(self, phase, h):
        for r in range(2):
            pick = (self.near if phase == 0 else self.far)(r)
            pos, right, left = self.ring(r, phase)
            piece = pick(pos, h)
            for d, there in enumerate((right, left)):
                send(
                    piece,
                    piece,
                    self.send_sem.at[r, phase, d, h],
                    self.recv_sem.at[r, phase, d, h],
                    there,
                ).start()

    def first(self):
        own = lax.div(self.here[0], 2)
        arrived(self.whole(1 - own), self.cross_sem.at[1])
        self.push(0, 1 - own)
        self.forward(0)
        self.rest(0, None)

    def forward(self, phase):
        for d in range(2):
            for r in range(2):
                pick = (self.near if phase == 0 else self.far)(r)
                pos, right, left = self.ring(r, phase)
                arrived(pick(pos, d), self.recv_sem.at[r, phase, d, d])
                piece = pick(lax.rem(pos + (3 if d == 0 else 1), 4), d)
                send(
                    piece,
                    piece,
                    self.send_sem.at[r, phase, 2, d],
                    self.recv_sem.at[r, phase, 2, d],
                    right if d == 0 else left,
                ).start()

    def rest(self, phase, seen):
        for d, h in ((0, 1), (1, 0), (2, 0), (2, 1)):
            for r in range(2):
                pick = (self.near if phase == 0 else self.far)(r)
                pos, _, _ = self.ring(r, phase)
                arrived(pick(pos, h), self.recv_sem.at[r, phase, d, h])
                if seen is not None:
                    seen(r, d, h, pick(lax.rem(pos + (3, 1, 2)[d], 4), h))

    def second(self, seen=None):
        self.push(1, 0)
        self.push(1, 1)
        self.forward(1)
        if seen is not None:
            for d in range(2):
                for r in range(2):
                    pos, _, _ = self.ring(r, 1)
                    seen(r, d, d, self.far(r)(lax.rem(pos + (3, 1)[d], 4), d))
        self.rest(1, seen)

    def drain(self):
        arrived(self.whole(0), self.cross_sem.at[0])
        for r in range(2):
            for phase in range(2):
                pick = (self.near if phase == 0 else self.far)(r)
                for d in range(3):
                    for h in range(2):
                        arrived(pick(0, h), self.send_sem.at[r, phase, d, h])


def request_bounds(lengths_ref, row):
    ends = [lengths_ref[row, 0]]
    for r in range(1, 3):
        ends.append(ends[-1] + lengths_ref[row, r])
    return ends


def front_kernel(
    lengths_ref,
    hidden_ref,
    gain_ref,
    shard_ref,
    out_shard_ref,
    pool_ref,
    q_gain_ref,
    k_gain_ref,
    freq_ref,
    q_ref,
    kv_ref,
    cache_ref,
    w_out_ref,
    pages_ref,
    weight,
    qkv,
    normed_ref,
    w_sems,
    k_sems,
    o_sems,
    cross_sems,
    w_swap,
    o_swap,
    pool_sems,
    local_sem,
):
    f32, bf16 = jnp.float32, jnp.bfloat16
    here = place()
    x, y, z, c = here
    own = lax.div(x, 2)
    columns = weight.shape[-1]
    side = columns // 2
    partner = (x, y, z, 1 - c)
    even = 1 - lax.rem(x, 2)
    across = (lax.rem(x + 1 + 2 * even, 4), y, z, c)
    opposite = (lax.rem(x + 2, 4), y, z, c)
    upper = (lax.rem(x + 1, 4), y, z, c)
    lower = (lax.rem(x + 3, 4), y, z, c)
    barrier = pltpu.get_barrier_semaphore()
    peers = (
        partner,
        opposite,
        upper,
        lower,
        (x, lax.rem(y + 1, 4), z, c),
        (x, lax.rem(y + 3, 4), z, c),
        (x, y, lax.rem(z + 1, 4), c),
        (x, y, lax.rem(z + 3, 4), c),
    )
    for peer in peers:
        pl.semaphore_signal(barrier, inc=1, device_id=device(*peer), device_id_type=MESH_ID)
    out_side = w_out_ref.shape[-1] // 2
    mine = pl.ds(pl.multiple_of(c * side, 128), side)
    mine_out = pl.ds(pl.multiple_of(c * out_side, 128), out_side)
    held = pool_ref.shape[0]
    row = lax.rem(x, 2) * 2 + c
    seeds = (
        pltpu.make_async_copy(
            shard_ref.at[:, mine], weight.at[y, own, z, :, mine], local_sem.at[0]
        ),
        pltpu.make_async_copy(
            out_shard_ref.at[:, mine_out], w_out_ref.at[y, own, z, :, mine_out], local_sem.at[1]
        ),
        pltpu.make_async_copy(pool_ref, pages_ref.at[pl.ds(row * held, held)], local_sem.at[2]),
    )
    for seed in seeds:
        seed.start()
    seeds[0].wait()
    pl.semaphore_wait(barrier, len(peers))

    gather = Gather(
        weight,
        here,
        across,
        ((c * side, side // 2), (c * side + side // 2, side // 2)),
        (w_sems.at[0], w_sems.at[1], cross_sems.at[0]),
    )
    gather.start()
    seeds[1].wait()
    seeds[2].wait()
    project_out = Gather(
        w_out_ref,
        here,
        across,
        ((c * out_side, out_side // 2), (c * out_side + out_side // 2, out_side // 2)),
        (o_sems.at[0], o_sems.at[1], cross_sems.at[1]),
    )

    def pool_send(slot, first, count, there):
        piece = pages_ref.at[pl.ds(first, count)]
        copy = send(piece, piece, pool_sems.at[0, slot], pool_sems.at[1, slot], there)
        copy.start()
        return copy

    few = held // 2
    far_row = (1 - lax.rem(x, 2)) * 2 + c
    pool_copies = [
        pool_send(0, row * held, few, upper),
        pool_send(1, row * held + few, few, lower),
        pool_send(2, row * held, held, partner),
    ]

    value = hidden_ref[...].astype(f32)
    mean = jnp.mean(value * value, axis=-1, keepdims=True)
    normed_ref[...] = (value * lax.rsqrt(mean + eps) * gain_ref[...]).astype(bf16)

    gather.first()

    def swapper(sems, kept):
        def swap(r, slot, piece):
            copy = send(piece, piece, sems.at[0, r, slot], sems.at[1, r, slot], partner)
            copy.start()
            kept.append(copy)

        return swap

    def swap_near(target, ref, swap):
        for r in range(2):
            pos, _, _ = target.ring(r, 1)
            cut = target.cut(r)
            swap(r, 6, ref.at[pos, :, :, :, cut] if r == 0 else ref.at[:, :, pos, :, cut])

    def swap_forwarded(target, swap):
        for d in range(2):
            for r in range(2):
                pos, _, _ = target.ring(r, 1)
                swap(r, d * 2 + d, target.far(r)(lax.rem(pos + (3, 1)[d], 4), d))

    w_kept, o_kept = [], []
    w_pair = swapper(w_swap, w_kept)
    o_pair = swapper(o_swap, o_kept)
    gather.push(1, 0)
    gather.push(1, 1)
    swap_near(gather, weight, w_pair)
    project_out.start()
    gather.forward(1)
    swap_forwarded(gather, w_pair)
    gather.rest(1, lambda r, d, h, piece: w_pair(r, d * 2 + h, piece))
    project_out.first()
    project_out.push(1, 0)
    project_out.push(1, 1)
    for copy in w_kept:
        copy.wait_recv()
    swap_near(project_out, w_out_ref, o_pair)

    span = 2 * 4 * weight.shape[3]

    def project(tile, _):
        at = pl.multiple_of(tile * 512, 512)
        total = jnp.zeros((normed_ref.shape[0], 512), f32)
        for plane in range(4):
            block = weight[plane, :, :, :, pl.ds(at, 512)].reshape(span, 512)
            total += jnp.dot(
                normed_ref[:, plane * span : (plane + 1) * span],
                block,
                preferred_element_type=f32,
            )
        qkv[:, pl.ds(at, 512)] = total
        return 0

    tokens = hidden_ref.shape[0]
    index = (y * 8 + own * 4 + z) * tokens + lax.broadcasted_iota(jnp.int32, (tokens, 128), 0)
    start = jnp.zeros_like(index)
    for end in request_bounds(lengths_ref, row):
        start = jnp.where(index >= end, end, start)
    angles = (PREFIX_TOKENS + index - start).astype(f32) * freq_ref[...]
    cosine = jnp.cos(angles)
    sine = jnp.sin(angles)
    lane = lax.broadcasted_iota(jnp.int32, (tokens, 128), 1)
    sine = jnp.where(lane < 64, -sine, sine)
    heads = columns // 128

    def turned(head, gain):
        rows = qkv[:, pl.ds(pl.multiple_of(head * 128, 128), 128)]
        mean = jnp.mean(rows * rows, axis=-1, keepdims=True)
        rows = rows * lax.rsqrt(mean + eps) * gain
        return (rows * cosine + pltpu.roll(rows, 64, 1) * sine).astype(bf16)

    project(columns // 512 - 1, 0)
    for h in range(2):
        cache_ref[:, h * 128 : (h + 1) * 128] = turned(heads - 4 + h, k_gain_ref[...])
    cache_ref[:, 256:512] = qkv[:, columns - 256 :].astype(bf16)
    seed = pltpu.make_async_copy(cache_ref, kv_ref.at[y, own, z], local_sem.at[0])
    seed.start()
    seed.wait()
    spread = Gather(
        kv_ref,
        here,
        opposite,
        ((0, 256), (256, 256)),
        (k_sems.at[0], k_sems.at[1], cross_sems.at[2]),
    )
    spread.start()
    lax.fori_loop(0, columns // 512 - 1, project, 0)

    def query(head, _):
        at = pl.multiple_of(lax.rem(head, 8) * 128, 128)
        q_ref[lax.div(head, 8), pl.ds(at, 128), :] = turned(head, q_gain_ref[...])
        return 0

    spread.first()
    spread.push(1, 0)
    spread.push(1, 1)
    arrived(pages_ref.at[pl.ds(0, few)], pool_sems.at[1, 0])
    arrived(pages_ref.at[pl.ds(0, few)], pool_sems.at[1, 1])
    pool_copies.append(pool_send(3, far_row * held, held, partner))
    lax.fori_loop(0, heads - 4, query, 0)
    spread.forward(1)
    project_out.forward(1)
    swap_forwarded(project_out, o_pair)
    spread.rest(1, None)
    project_out.rest(1, lambda r, d, h, piece: o_pair(r, d * 2 + h, piece))
    for copy in o_kept:
        copy.wait_recv()
    for copy in pool_copies[2:]:
        copy.wait_recv()
    gather.drain()
    spread.drain()
    project_out.drain()
    for copy in w_kept + o_kept + pool_copies:
        copy.wait_send()


def front(lengths, hidden, gain, shard, out_shard, pool, q_gain, k_gain, freqs):
    tokens, width = hidden.shape
    rows, columns = shard.shape
    vmem = pl.BlockSpec(memory_space=pltpu.VMEM)
    smem = pl.BlockSpec(memory_space=pltpu.SMEM)
    hbm = pl.BlockSpec(memory_space=pl.ANY)
    ring = pltpu.SemaphoreType.DMA((2, 2, 2, 3, 2))
    swap = pltpu.SemaphoreType.DMA((2, 2, 7))
    return pl.pallas_call(
        front_kernel,
        out_shape=(
            jax.ShapeDtypeStruct((2, 8 * tokens, 128), jnp.bfloat16),
            jax.ShapeDtypeStruct((4, 2, 4, tokens, 512), jnp.bfloat16),
            jax.ShapeDtypeStruct((tokens, 512), jnp.bfloat16),
            jax.ShapeDtypeStruct((4, 2, 4) + out_shard.shape, jnp.bfloat16),
            jax.ShapeDtypeStruct((4 * pool.shape[0],) + pool.shape[1:], jnp.bfloat16),
        ),
        in_specs=[smem] + [vmem] * 8,
        out_specs=(vmem, hbm, vmem, hbm, hbm),
        scratch_shapes=[
            pltpu.VMEM((4, 2, 4, rows, columns), jnp.bfloat16),
            pltpu.VMEM((tokens, columns), jnp.float32),
            pltpu.VMEM((tokens, width), jnp.bfloat16),
            ring,
            ring,
            ring,
            pltpu.SemaphoreType.DMA((3, 2)),
            swap,
            swap,
            pltpu.SemaphoreType.DMA((2, 4)),
            pltpu.SemaphoreType.DMA((3,)),
        ],
        compiler_params=pltpu.CompilerParams(
            collective_id=1, has_side_effects=True, vmem_limit_bytes=56 * 1024 * 1024
        ),
        cost_estimate=pl.CostEstimate(
            flops=1_400_000_000, bytes_accessed=200_000_000, transcendentals=1_000_000
        ),
    )(lengths, hidden, gain, shard, out_shard, pool, q_gain, k_gain, freqs)


def attention_kernel(
    table,
    lengths_ref,
    groups_ref,
    q_ref,
    hidden_ref,
    gain_ref,
    kv_hbm,
    pool_hbm,
    w_out_hbm,
    mid_ref,
    moe_ref,
    kv_ref,
    pool_ref,
    w_out_ref,
    mixed,
    high,
    total,
    acc,
    sems,
):
    f32, bf16 = jnp.float32, jnp.bfloat16
    loads = (
        pltpu.make_async_copy(pool_hbm, pool_ref, sems.at[0]),
        pltpu.make_async_copy(kv_hbm, kv_ref, sems.at[1]),
        pltpu.make_async_copy(w_out_hbm, w_out_ref, sems.at[2]),
    )
    for load in loads:
        load.start()
    row = lax.axis_index("dp")
    first = lax.axis_index("expert") * hidden_ref.shape[0]
    last = first + hidden_ref.shape[0] - 1
    index = first + lax.broadcasted_iota(jnp.int32, (1, 128), 1)
    start = jnp.zeros_like(index)
    group_of = jnp.zeros_like(index) + groups_ref[row, 0]
    earliest, latest = jnp.int32(0), jnp.int32(0)
    begin = jnp.int32(0)
    counts = [jnp.int32(0), jnp.int32(0)]
    for r in range(4):
        end = begin + lengths_ref[row, r]
        of = groups_ref[row, r]
        if r > 0:
            start = jnp.where(index >= begin, begin, start)
            group_of = jnp.where(index >= begin, of, group_of)
            earliest = jnp.where(first >= begin, begin, earliest)
            latest = jnp.where(last >= begin, begin, latest)
        inside = jnp.maximum(jnp.minimum(end, last + 1) - jnp.maximum(begin, first), 0)
        counts[0] += jnp.where(of == 0, inside, 0)
        counts[1] += jnp.where(of == 1, inside, 0)
        begin = end
    everyone = last - first + 1
    factor = math.log2(math.e) / math.sqrt(128)
    high[...] = jnp.full_like(high, floor_value)
    total[...] = jnp.zeros_like(total)
    acc[...] = jnp.zeros_like(acc)

    def step(h, keys, values, seen):
        scores = lax.dot_general(
            keys, q_ref[h], (((1,), (1,)), ((), ())), preferred_element_type=f32
        )
        if seen is not None:
            scores = jnp.where(jnp.concatenate([seen] * 8, axis=1), scores, -jnp.inf)
        old = high[h]
        new = jnp.maximum(old, jnp.max(scores, axis=0, keepdims=True))
        weights = jnp.exp2((scores - new) * factor)
        shrink = jnp.exp2((old - new) * factor)
        high[h] = new
        total[h] = total[h] * shrink + jnp.sum(weights, axis=0, keepdims=True)
        acc[h] = acc[h] * shrink + lax.dot_general(
            values, weights.astype(bf16), (((0,), (0,)), ((), ())), preferred_element_type=f32
        )

    span = 4
    loads[0].wait()
    for group in range(2):

        def pages(seen, group=group):
            def body(j, _):
                picked = [table[group * 16 + j * span + i] for i in range(span)]
                for h in range(2):
                    keys = jnp.concatenate([pool_ref[p, 0, h] for p in picked], axis=0)
                    values = jnp.concatenate([pool_ref[p, 1, h] for p in picked], axis=0)
                    step(h, keys, values, seen)
                return 0

            lax.fori_loop(0, 16 // span, body, 0)

        @pl.when(counts[group] == everyone)
        def _():
            pages(None)

        @pl.when((counts[group] > 0) & (counts[group] < everyone))
        def _():
            pages(jnp.broadcast_to(group_of == group, (span * 128, 128)))

    loads[1].wait()
    size = 256

    def suffix(tile, masked):
        at = pl.multiple_of(tile * size, size)
        seen = None
        if masked:
            place_of = at + lax.broadcasted_iota(jnp.int32, (size, 128), 0)
            seen = (place_of >= start) & (place_of <= index)
        for h in range(2):
            keys = kv_ref[pl.ds(at, size), h * 128 : (h + 1) * 128]
            values = kv_ref[pl.ds(at, size), 256 + h * 128 : 256 + (h + 1) * 128]
            step(h, keys, values, seen)

    def tiles(tile, _):
        clear = (tile * size >= latest) & (tile * size + size <= first + 1)

        @pl.when(clear)
        def _():
            suffix(tile, False)

        @pl.when(jnp.logical_not(clear))
        def _():
            suffix(tile, True)

        return 0

    lax.fori_loop(lax.div(earliest, size), lax.div(last, size) + 1, tiles, 0)
    for h in range(2):
        done = acc[h] / total[h]
        for g in range(8):
            head = h * 8 + g
            mixed[:, head * 128 : (head + 1) * 128] = (
                done[:, g * 128 : (g + 1) * 128].T.astype(bf16)
            )


    loads[2].wait()

    def project(tile, square):
        at = pl.multiple_of(tile * 512, 512)
        part = jnp.dot(mixed[...], w_out_ref[:, pl.ds(at, 512)], preferred_element_type=f32)
        mid = (hidden_ref[:, pl.ds(at, 512)].astype(f32) + part).astype(bf16)
        mid_ref[:, pl.ds(at, 512)] = mid
        mid = mid.astype(f32)
        return square + jnp.sum(mid * mid, axis=-1, keepdims=True)

    width = hidden_ref.shape[1]
    square = lax.fori_loop(0, width // 512, project, jnp.zeros((hidden_ref.shape[0], 1), f32))
    factor_of = lax.rsqrt(square / width + eps)
    moe_ref[...] = (mid_ref[...].astype(f32) * factor_of * gain_ref[...]).astype(bf16)


def attention(table, lengths, groups, q, hidden, gain, kv, pool, w_out):
    vmem = pl.BlockSpec(memory_space=pltpu.VMEM)
    smem = pl.BlockSpec(memory_space=pltpu.SMEM)
    hbm = pl.BlockSpec(memory_space=pl.ANY)
    tokens, width = hidden.shape
    row = jax.ShapeDtypeStruct((tokens, width), jnp.bfloat16)
    return pl.pallas_call(
        attention_kernel,
        out_shape=(row, row),
        in_specs=[smem] * 3 + [vmem] * 3 + [hbm] * 3,
        out_specs=(vmem, vmem),
        scratch_shapes=[
            pltpu.VMEM(kv.shape, jnp.bfloat16),
            pltpu.VMEM(pool.shape, jnp.bfloat16),
            pltpu.VMEM(w_out.shape, jnp.bfloat16),
            pltpu.VMEM((tokens, width), jnp.bfloat16),
            pltpu.VMEM((2, 1, 8 * tokens), jnp.float32),
            pltpu.VMEM((2, 1, 8 * tokens), jnp.float32),
            pltpu.VMEM((2, 128, 8 * tokens), jnp.float32),
            pltpu.SemaphoreType.DMA((3,)),
        ],
        compiler_params=pltpu.CompilerParams(vmem_limit_bytes=56 * 1024 * 1024),
        cost_estimate=pl.CostEstimate(
            flops=5_000_000_000, bytes_accessed=10_000_000, transcendentals=10_000_000
        ),
    )(table, lengths, groups, q, hidden, gain, kv, pool, w_out)


def local(
    hidden_in,
    attn_gain,
    query_key_value_weight,
    q_gain,
    key_norm_gain,
    w_out,
    moe_gain,
    w_gate_up,
    w_down,
    kv_pool,
    page_table,
    suffix_lengths,
    request_group,
    expert_ids,
    gate_weights,
):
    tokens_here, width = hidden_in.shape
    half = q_gain.shape[0] // 2
    freqs = theta ** (-jnp.arange(half, dtype=jnp.float32) / half)
    q, kv, suffix_cache, w_out_all, pool = front(
        suffix_lengths,
        hidden_in,
        attn_gain[None],
        query_key_value_weight,
        w_out,
        kv_pool.transpose(0, 1, 3, 2, 4),
        q_gain[None],
        key_norm_gain[None],
        jnp.concatenate([freqs, freqs])[None],
    )
    mid, moe_in = attention(
        page_table,
        suffix_lengths,
        request_group,
        q,
        hidden_in,
        moe_gain[None],
        kv.reshape(32 * tokens_here, 512),
        pool,
        w_out_all.reshape(32 * w_out.shape[0], width),
    )
    hidden_out = experts(moe_in, mid, expert_ids, gate_weights, w_gate_up[0], w_down[0])
    return (hidden_out, suffix_cache)


def solution(mesh):
    return jax.shard_map(
        local,
        mesh=mesh,
        in_specs=(
            P(("dp", "expert"), None),
            P(),
            P("expert", None),
            P(),
            P(),
            P("expert", None),
            P(),
            P(("dp", "expert"), None, None),
            P(("dp", "expert"), None, None),
            P("dp", None, None, None, None),
            P(),
            P(),
            P(),
            P(("dp", "expert"), None),
            P(("dp", "expert"), None),
        ),
        out_specs=(P(("dp", "expert"), None), P(("dp", "expert"), None)),
        check_vma=False,
    )
```

```python
import math

import jax
import jax.numpy as jnp
from jax import lax
from jax.experimental import pallas as pl
from jax.experimental.pallas import tpu as pltpu
from jax.sharding import PartitionSpec as P

PREFIX_TOKENS = 2048


eps = 1e-06
theta = 1000000.0
floor_value = -1e30


MESH_ID = pl.DeviceIdType.MESH
STEP = 45
PARTS = (0, 640, 1280, 2048)


def place():
    dp = lax.axis_index("dp")
    ex = lax.axis_index("expert")
    x = lax.rem(lax.div(ex, 4), 2) * 2 + lax.div(dp, 2)
    return (x, lax.div(ex, 8), lax.rem(ex, 4), lax.rem(dp, 2))


def device(x, y, z, c):
    return {"dp": lax.rem(x, 2) * 2 + c, "expert": y * 8 + lax.div(x, 2) * 4 + z}


def number(x, y, z, c):
    return (lax.rem(x, 2) * 2 + c) * 32 + y * 8 + lax.div(x, 2) * 4 + z


def greet_all(here):
    barrier = pltpu.get_barrier_semaphore()
    x, y, z, c = here

    def tell(k, _):
        there = (
            lax.rem(x + lax.div(k, 32), 4),
            lax.rem(y + lax.rem(lax.div(k, 8), 4), 4),
            lax.rem(z + lax.rem(lax.div(k, 2), 4), 4),
            lax.rem(c + k, 2),
        )
        pl.semaphore_signal(barrier, inc=1, device_id=device(*there), device_id_type=MESH_ID)
        return 0

    lax.fori_loop(1, 128, tell, 0)
    return barrier


def send(src, dst, send_sem, recv_sem, where):
    return pltpu.make_async_remote_copy(
        src_ref=src,
        dst_ref=dst,
        send_sem=send_sem,
        recv_sem=recv_sem,
        device_id=device(*where),
        device_id_type=MESH_ID,
    )


def part_columns(p):
    return slice(PARTS[p], PARTS[p + 1])


def in_plane(p, here):
    x, y, z, c = here
    return ((y, z), (z, x), (y, x))[p]


def at_plane(p, here, a, b, c):
    x, y, z, _ = here
    return ((x, a, b, c), (b, y, a, c), (b, a, z, c))[p]


def on_line(p, here, d):
    moved = list(here)
    moved[p] = lax.rem(here[p] + d, 4)
    return tuple(moved)


def moe_kernel(
    x_ref,
    mid_ref,
    info_ref,
    gate_up_hbm,
    down_hbm,
    out_ref,
    line,
    infos,
    pack_a,
    pack_b,
    recv_a,
    recv_b,
    home_a,
    home_b,
    rows,
    acts,
    partial,
    inbox,
    ranks,
    gates,
    gate_up,
    down,
    weight_sem,
    line_send,
    line_recv,
    info_send,
    info_recv,
    out_sem,
    in_sem,
    back_sem,
    home_sem,
    sum_send,
    sum_recv,
):
    f32, bf16 = jnp.float32, jnp.bfloat16
    ff = down.shape[0]
    here = place()
    c = here[3]
    load_gate_up = pltpu.make_async_copy(gate_up_hbm, gate_up, weight_sem.at[0])
    load_down = pltpu.make_async_copy(down_hbm, down, weight_sem.at[1])
    load_gate_up.start()
    load_down.start()
    barrier = greet_all(here)
    pl.semaphore_wait(barrier, 127)

    for p in range(3):
        own = here[p]
        pltpu.make_async_copy(info_ref, infos.at[p, own], info_recv.at[p]).start()
        for d in (1, 3, 2):
            send(
                info_ref, infos.at[p, own], info_send.at[p], info_recv.at[p], on_line(p, here, d)
            ).start()
    for d in (1, 3, 2):
        for p in range(3):
            cut = part_columns(p)
            send(
                x_ref.at[:, cut],
                line.at[here[p], :, cut],
                line_send.at[p],
                line_recv.at[p],
                on_line(p, here, d),
            ).start()
    for p in range(3):
        cut = part_columns(p)
        pltpu.make_async_copy(
            x_ref.at[:, cut], line.at[here[p], :, cut], line_recv.at[p]
        ).start()

    local = lax.broadcasted_iota(jnp.int32, (32, 128), 0)
    before = jnp.where(
        lax.broadcasted_iota(jnp.int32, (128, 128), 0)
        < lax.broadcasted_iota(jnp.int32, (128, 128), 1),
        1.0,
        0.0,
    ).astype(bf16)
    for p in range(3):
        arrived(infos.at[p], info_recv.at[p])
        expert = number(
            *at_plane(
                p,
                here,
                lax.rem(lax.div(local, 4), 4),
                lax.rem(local, 4),
                lax.div(local, 16),
            )
        ).astype(f32)
        for q in range(4):
            named = jnp.zeros((32, 128), f32)
            gate = jnp.zeros((32, 128), f32)
            for k in range(8):
                hit = infos[p, q, k : k + 1, :] == expert
                named += jnp.where(hit, 1.0, 0.0)
                gate += jnp.where(hit, infos[p, q, 8 + k : 9 + k, :], 0.0)
            rank = jnp.dot(named.astype(bf16), before, preferred_element_type=f32)
            ranks[p, q] = jnp.where(named > 0.5, rank, 99.0)
            gates[p, q] = gate

    def choice(p, q, low, count):
        rank = ranks[p, q]
        wanted = (low + lax.broadcasted_iota(jnp.int32, (32, count, 128), 1)).astype(f32)
        return jnp.where(rank[:, None, :] == wanted, 1.0, 0.0)

    halves = ((0, 8, pack_a, recv_a, home_a), (8, 4, pack_b, recv_b, home_b))

    def pack(half):
        low, count, packed, _, _ = halves[half]

        def body(q, _):
            for p in range(3):
                cut = part_columns(p)
                chosen = choice(p, q, low, count).reshape(32 * count, 128).astype(bf16)
                value = jnp.dot(chosen, line[q, :, cut], preferred_element_type=f32)
                packed[q, :, :, cut] = value.astype(bf16).reshape(32, count, cut.stop - cut.start)
            return 0

        lax.fori_loop(0, 4, body, 0)

    def bundle(ref, a, b, core, p):
        return ref.at[:, core * 16 + a * 4 + b, :, part_columns(p)]

    def spread(ref, p, x, y, z, core):
        cut = part_columns(p)
        if p == 0:
            return ref.at[:, core, y, z, :, cut]
        if p == 1:
            return ref.at[x, core, :, z, :, cut]
        return ref.at[x, core, y, :, :, cut]

    def visit(step):
        sign = 1 - 2 * c

        def body(k, _):
            o = lax.rem(k * STEP, 32)
            for p in range(3):
                a, b = in_plane(p, here)
                to_a = lax.rem(a + sign * lax.rem(lax.div(o, 4), 4) + 4, 4)
                to_b = lax.rem(b + sign * lax.rem(o, 4) + 4, 4)
                to_c = lax.rem(c + lax.div(o, 16), 2)
                step(p, to_a, to_b, to_c)
            return 0

        lax.fori_loop(1, 32, body, 0)

    def dispatch(src, dst, send_sem, recv_sem):
        def step(p, a, b, core):
            send(
                bundle(src, a, b, core, p),
                spread(dst, p, *here),
                send_sem.at[p],
                recv_sem.at[p],
                at_plane(p, here, a, b, core),
            ).start()

        visit(step)
        for p in range(3):
            a, b = in_plane(p, here)
            pltpu.make_async_copy(
                bundle(src, a, b, c, p), spread(dst, p, *here), recv_sem.at[p]
            ).start()

    def give_back(src, dst, send_sem, recv_sem):
        def step(p, a, b, core):
            own_a, own_b = in_plane(p, here)
            there = at_plane(p, here, a, b, core)
            send(
                spread(src, p, *there),
                bundle(dst, own_a, own_b, c, p),
                send_sem.at[p],
                recv_sem.at[p],
                there,
            ).start()

        visit(step)
        for p in range(3):
            a, b = in_plane(p, here)
            pltpu.make_async_copy(
                spread(src, p, *here), bundle(dst, a, b, c, p), recv_sem.at[p]
            ).start()

    for p in range(3):
        cut = part_columns(p)
        arrived(line.at[:, :, cut], line_recv.at[p])
    for half in range(2):
        low, count, packed, received, _ = halves[half]
        pack(half)
        dispatch(packed, received, out_sem.at[half], in_sem.at[half])
    load_gate_up.wait()
    load_down.wait()

    def others(ref, p):
        return ref.at[:, pl.ds(0, 31), :, part_columns(p)]

    for half in range(2):
        low, count, packed, received, home = halves[half]
        total = 128 * count
        for p in range(3):
            whole = packed.at[:, :, :, part_columns(p)]
            arrived(whole, in_sem.at[half, p])
        rows[:total, :] = received[...].reshape(total, rows.shape[1])

        def up(tile, _):
            at = pl.multiple_of(tile * 256, 256)
            values = rows[:total, :]
            first = jnp.dot(values, gate_up[:, pl.ds(at, 256)], preferred_element_type=f32)
            second = jnp.dot(values, gate_up[:, pl.ds(ff + at, 256)], preferred_element_type=f32)
            acts[:total, pl.ds(at, 256)] = (jax.nn.silu(first) * second).astype(bf16)
            return 0

        lax.fori_loop(0, ff // 256, up, 0)

        def lower(tile, _):
            at = pl.multiple_of(tile * 256, 256)
            value = jnp.dot(
                acts[:total, :], down[:, pl.ds(at, 256)], preferred_element_type=f32
            ).astype(bf16)
            received[:, :, :, :, :, pl.ds(at, 256)] = value.reshape(4, 2, 4, 4, count, 256)
            return 0

        lax.fori_loop(0, rows.shape[1] // 256, lower, 0)
        give_back(received, home, back_sem.at[half], home_sem.at[half])

    over_rows = (((0,), (0,)), ((), ()))
    for half in range(2):
        low, count, packed, received, home = halves[half]
        for p in range(3):
            arrived(home.at[:, :, :, part_columns(p)], home_sem.at[half, p])

        def combine(q, _):
            at = pl.ds(pl.multiple_of(q * 128, 128), 128)
            for p in range(3):
                cut = part_columns(p)
                exact = choice(p, q, low, count) * gates[p, q][:, None, :]
                exact = exact.reshape(32 * count, 128)
                coarse = exact.astype(bf16)
                fine = (exact - coarse.astype(f32)).astype(bf16)
                values = home[q, :, :, cut].reshape(32 * count, cut.stop - cut.start)
                value = lax.dot_general(
                    coarse, values, over_rows, preferred_element_type=f32
                ) + lax.dot_general(fine, values, over_rows, preferred_element_type=f32)
                if half == 0:
                    partial[at, cut] = value
                else:
                    value += partial[at, cut]
                    partial[at, cut] = value
                    rows[at, cut] = value.astype(bf16)
            return 0

        lax.fori_loop(0, 4, combine, 0)

    for d in (1, 3, 2):
        for p in range(3):
            cut = part_columns(p)
            there = on_line(p, here, d)
            send(
                rows.at[pl.ds(there[p] * 128, 128), cut],
                inbox.at[here[p], :, cut],
                sum_send.at[p],
                sum_recv.at[p],
                there,
            ).start()
    for p in range(3):
        cut = part_columns(p)
        arrived(inbox.at[pl.ds(0, 3), :, cut], sum_recv.at[p])
        total = partial[pl.ds(pl.multiple_of(here[p] * 128, 128), 128), cut]
        for d in range(1, 4):
            total += inbox[lax.rem(here[p] + d, 4), :, cut].astype(f32)
        out_ref[:, cut] = (mid_ref[:, cut].astype(f32) + total).astype(bf16)

    for p in range(3):
        cut = part_columns(p)
        arrived(infos.at[p, pl.ds(0, 3)], info_send.at[p])
        arrived(inbox.at[pl.ds(0, 3), :, cut], line_send.at[p])
        arrived(inbox.at[pl.ds(0, 3), :, cut], sum_send.at[p])
        for half in range(2):
            arrived(others(halves[half][2], p), out_sem.at[half, p])
            arrived(others(halves[half][2], p), back_sem.at[half, p])


def experts(moe_in, mid, ids, gates, gate_up, down):
    tokens, width = moe_in.shape
    ff = down.shape[0]
    bf16 = jnp.bfloat16
    vmem = pl.BlockSpec(memory_space=pltpu.VMEM)
    hbm = pl.BlockSpec(memory_space=pl.ANY)
    flat_a, flat_b = (pltpu.VMEM((4, 32, n, width), bf16) for n in (8, 4))
    wide_a, wide_b = (pltpu.VMEM((4, 2, 4, 4, n, width), bf16) for n in (8, 4))
    three = pltpu.SemaphoreType.DMA((3,))
    six = pltpu.SemaphoreType.DMA((2, 3))
    info = jnp.concatenate([ids.T.astype(jnp.float32), gates.T], axis=0)
    return pl.pallas_call(
        moe_kernel,
        out_shape=jax.ShapeDtypeStruct((tokens, width), bf16),
        in_specs=[vmem] * 3 + [hbm] * 2,
        out_specs=vmem,
        scratch_shapes=[
            pltpu.VMEM((4, tokens, width), bf16),
            pltpu.VMEM((3, 4, 16, tokens), jnp.float32),
            flat_a,
            flat_b,
            wide_a,
            wide_b,
            flat_a,
            flat_b,
            pltpu.VMEM((1024, width), bf16),
            pltpu.VMEM((1024, ff), bf16),
            pltpu.VMEM((512, width), jnp.float32),
            pltpu.VMEM((4, tokens, width), bf16),
            pltpu.VMEM((3, 4, 32, tokens), jnp.float32),
            pltpu.VMEM((3, 4, 32, tokens), jnp.float32),
            pltpu.VMEM((width, 2 * ff), bf16),
            pltpu.VMEM((ff, width), bf16),
            pltpu.SemaphoreType.DMA((2,)),
            three,
            three,
            three,
            three,
            six,
            six,
            six,
            six,
            three,
            three,
        ],
        compiler_params=pltpu.CompilerParams(
            collective_id=3, has_side_effects=True, vmem_limit_bytes=63 * 1024 * 1024
        ),
        cost_estimate=pl.CostEstimate(
            flops=20_000_000_000, bytes_accessed=400_000_000, transcendentals=1_000_000
        ),
    )(moe_in, mid, info, gate_up, down)


def arrived(ref, sem):
    pltpu.make_async_copy(ref, ref, sem).wait()


class Gather:
    def __init__(self, buf, here, cross, columns, sems):
        self.buf, self.here, self.cross, self.columns = buf, here, cross, columns
        self.send_sem, self.recv_sem, self.cross_sem = sems

    def cut(self, r):
        start, size = self.columns[r]
        return pl.ds(pl.multiple_of(start, 128), size)

    def whole(self, h):
        x, y, z, c = self.here
        start, size = self.columns[0]
        return self.buf.at[y, h, z, :, pl.ds(pl.multiple_of(start, 128), size + self.columns[1][1])]

    def near(self, r):
        x, y, z, c = self.here
        cut = self.cut(r)
        if r == 0:
            return lambda p, h: self.buf.at[y, h, p, :, cut]
        return lambda p, h: self.buf.at[p, h, z, :, cut]

    def far(self, r):
        cut = self.cut(r)
        if r == 0:
            return lambda p, h: self.buf.at[p, h, :, :, cut]
        return lambda p, h: self.buf.at[:, h, p, :, cut]

    def ring(self, r, phase):
        x, y, z, c = self.here
        if (r + phase) % 2 == 0:
            return z, (x, y, lax.rem(z + 1, 4), c), (x, y, lax.rem(z + 3, 4), c)
        return y, (x, lax.rem(y + 1, 4), z, c), (x, lax.rem(y + 3, 4), z, c)

    def start(self):
        own = lax.div(self.here[0], 2)
        send(
            self.whole(own), self.whole(own), self.cross_sem.at[0], self.cross_sem.at[1], self.cross
        ).start()
        self.push(0, own)

    def push(self, phase, h):
        for r in range(2):
            pick = (self.near if phase == 0 else self.far)(r)
            pos, right, left = self.ring(r, phase)
            piece = pick(pos, h)
            for d, there in enumerate((right, left)):
                send(
                    piece,
                    piece,
                    self.send_sem.at[r, phase, d, h],
                    self.recv_sem.at[r, phase, d, h],
                    there,
                ).start()

    def first(self):
        own = lax.div(self.here[0], 2)
        arrived(self.whole(1 - own), self.cross_sem.at[1])
        self.push(0, 1 - own)
        self.forward(0)
        self.rest(0, None)

    def forward(self, phase):
        for d in range(2):
            for r in range(2):
                pick = (self.near if phase == 0 else self.far)(r)
                pos, right, left = self.ring(r, phase)
                arrived(pick(pos, d), self.recv_sem.at[r, phase, d, d])
                piece = pick(lax.rem(pos + (3 if d == 0 else 1), 4), d)
                send(
                    piece,
                    piece,
                    self.send_sem.at[r, phase, 2, d],
                    self.recv_sem.at[r, phase, 2, d],
                    right if d == 0 else left,
                ).start()

    def rest(self, phase, seen):
        for d, h in ((0, 1), (1, 0), (2, 0), (2, 1)):
            for r in range(2):
                pick = (self.near if phase == 0 else self.far)(r)
                pos, _, _ = self.ring(r, phase)
                arrived(pick(pos, h), self.recv_sem.at[r, phase, d, h])
                if seen is not None:
                    seen(r, d, h, pick(lax.rem(pos + (3, 1, 2)[d], 4), h))

    def second(self, seen=None):
        self.push(1, 0)
        self.push(1, 1)
        self.forward(1)
        if seen is not None:
            for d in range(2):
                for r in range(2):
                    pos, _, _ = self.ring(r, 1)
                    seen(r, d, d, self.far(r)(lax.rem(pos + (3, 1)[d], 4), d))
        self.rest(1, seen)

    def drain(self):
        arrived(self.whole(0), self.cross_sem.at[0])
        for r in range(2):
            for phase in range(2):
                pick = (self.near if phase == 0 else self.far)(r)
                for d in range(3):
                    for h in range(2):
                        arrived(pick(0, h), self.send_sem.at[r, phase, d, h])


def request_bounds(lengths_ref, row):
    ends = [lengths_ref[row, 0]]
    for r in range(1, 3):
        ends.append(ends[-1] + lengths_ref[row, r])
    return ends


def front_kernel(
    lengths_ref,
    hidden_ref,
    gain_ref,
    shard_ref,
    out_shard_ref,
    pool_ref,
    q_gain_ref,
    k_gain_ref,
    freq_ref,
    q_ref,
    kv_ref,
    cache_ref,
    w_out_ref,
    pages_ref,
    weight,
    qkv,
    normed_ref,
    w_sems,
    k_sems,
    o_sems,
    cross_sems,
    w_swap,
    o_swap,
    pool_sems,
    local_sem,
):
    f32, bf16 = jnp.float32, jnp.bfloat16
    here = place()
    x, y, z, c = here
    own = lax.div(x, 2)
    columns = weight.shape[-1]
    side = columns // 2
    partner = (x, y, z, 1 - c)
    even = 1 - lax.rem(x, 2)
    across = (lax.rem(x + 1 + 2 * even, 4), y, z, c)
    opposite = (lax.rem(x + 2, 4), y, z, c)
    upper = (lax.rem(x + 1, 4), y, z, c)
    lower = (lax.rem(x + 3, 4), y, z, c)
    barrier = pltpu.get_barrier_semaphore()
    peers = (
        partner,
        opposite,
        upper,
        lower,
        (x, lax.rem(y + 1, 4), z, c),
        (x, lax.rem(y + 3, 4), z, c),
        (x, y, lax.rem(z + 1, 4), c),
        (x, y, lax.rem(z + 3, 4), c),
    )
    for peer in peers:
        pl.semaphore_signal(barrier, inc=1, device_id=device(*peer), device_id_type=MESH_ID)
    out_side = w_out_ref.shape[-1] // 2
    mine = pl.ds(pl.multiple_of(c * side, 128), side)
    mine_out = pl.ds(pl.multiple_of(c * out_side, 128), out_side)
    held = pool_ref.shape[0]
    row = lax.rem(x, 2) * 2 + c
    seeds = (
        pltpu.make_async_copy(
            shard_ref.at[:, mine], weight.at[y, own, z, :, mine], local_sem.at[0]
        ),
        pltpu.make_async_copy(
            out_shard_ref.at[:, mine_out], w_out_ref.at[y, own, z, :, mine_out], local_sem.at[1]
        ),
        pltpu.make_async_copy(pool_ref, pages_ref.at[pl.ds(row * held, held)], local_sem.at[2]),
    )
    for seed in seeds:
        seed.start()
    seeds[0].wait()
    pl.semaphore_wait(barrier, len(peers))

    gather = Gather(
        weight,
        here,
        across,
        ((c * side, side // 2), (c * side + side // 2, side // 2)),
        (w_sems.at[0], w_sems.at[1], cross_sems.at[0]),
    )
    gather.start()
    seeds[1].wait()
    seeds[2].wait()
    project_out = Gather(
        w_out_ref,
        here,
        across,
        ((c * out_side, out_side // 2), (c * out_side + out_side // 2, out_side // 2)),
        (o_sems.at[0], o_sems.at[1], cross_sems.at[1]),
    )

    def pool_send(slot, first, count, there):
        piece = pages_ref.at[pl.ds(first, count)]
        copy = send(piece, piece, pool_sems.at[0, slot], pool_sems.at[1, slot], there)
        copy.start()
        return copy

    few = held // 2
    far_row = (1 - lax.rem(x, 2)) * 2 + c
    pool_copies = [
        pool_send(0, row * held, few, upper),
        pool_send(1, row * held + few, few, lower),
        pool_send(2, row * held, held, partner),
    ]

    value = hidden_ref[...].astype(f32)
    mean = jnp.mean(value * value, axis=-1, keepdims=True)
    normed_ref[...] = (value * lax.rsqrt(mean + eps) * gain_ref[...]).astype(bf16)

    gather.first()

    def swapper(sems, kept):
        def swap(r, slot, piece):
            copy = send(piece, piece, sems.at[0, r, slot], sems.at[1, r, slot], partner)
            copy.start()
            kept.append(copy)

        return swap

    def swap_near(target, ref, swap):
        for r in range(2):
            pos, _, _ = target.ring(r, 1)
            cut = target.cut(r)
            swap(r, 6, ref.at[pos, :, :, :, cut] if r == 0 else ref.at[:, :, pos, :, cut])

    def swap_forwarded(target, swap):
        for d in range(2):
            for r in range(2):
                pos, _, _ = target.ring(r, 1)
                swap(r, d * 2 + d, target.far(r)(lax.rem(pos + (3, 1)[d], 4), d))

    w_kept, o_kept = [], []
    w_pair = swapper(w_swap, w_kept)
    o_pair = swapper(o_swap, o_kept)
    gather.push(1, 0)
    gather.push(1, 1)
    swap_near(gather, weight, w_pair)
    project_out.start()
    gather.forward(1)
    swap_forwarded(gather, w_pair)
    gather.rest(1, lambda r, d, h, piece: w_pair(r, d * 2 + h, piece))
    project_out.first()
    project_out.push(1, 0)
    project_out.push(1, 1)
    for copy in w_kept:
        copy.wait_recv()
    swap_near(project_out, w_out_ref, o_pair)

    span = 2 * 4 * weight.shape[3]

    def project(tile, _):
        at = pl.multiple_of(tile * 512, 512)
        total = jnp.zeros((normed_ref.shape[0], 512), f32)
        for plane in range(4):
            block = weight[plane, :, :, :, pl.ds(at, 512)].reshape(span, 512)
            total += jnp.dot(
                normed_ref[:, plane * span : (plane + 1) * span],
                block,
                preferred_element_type=f32,
            )
        qkv[:, pl.ds(at, 512)] = total
        return 0

    tokens = hidden_ref.shape[0]
    index = (y * 8 + own * 4 + z) * tokens + lax.broadcasted_iota(jnp.int32, (tokens, 128), 0)
    start = jnp.zeros_like(index)
    for end in request_bounds(lengths_ref, row):
        start = jnp.where(index >= end, end, start)
    angles = (PREFIX_TOKENS + index - start).astype(f32) * freq_ref[...]
    cosine = jnp.cos(angles)
    sine = jnp.sin(angles)
    lane = lax.broadcasted_iota(jnp.int32, (tokens, 128), 1)
    sine = jnp.where(lane < 64, -sine, sine)
    heads = columns // 128

    def turned(head, gain):
        rows = qkv[:, pl.ds(pl.multiple_of(head * 128, 128), 128)]
        mean = jnp.mean(rows * rows, axis=-1, keepdims=True)
        rows = rows * lax.rsqrt(mean + eps) * gain
        return (rows * cosine + pltpu.roll(rows, 64, 1) * sine).astype(bf16)

    project(columns // 512 - 1, 0)
    for h in range(2):
        cache_ref[:, h * 128 : (h + 1) * 128] = turned(heads - 4 + h, k_gain_ref[...])
    cache_ref[:, 256:512] = qkv[:, columns - 256 :].astype(bf16)
    seed = pltpu.make_async_copy(cache_ref, kv_ref.at[y, own, z], local_sem.at[0])
    seed.start()
    seed.wait()
    spread = Gather(
        kv_ref,
        here,
        opposite,
        ((0, 256), (256, 256)),
        (k_sems.at[0], k_sems.at[1], cross_sems.at[2]),
    )
    spread.start()
    lax.fori_loop(0, columns // 512 - 1, project, 0)

    def query(head, _):
        at = pl.multiple_of(lax.rem(head, 8) * 128, 128)
        q_ref[lax.div(head, 8), pl.ds(at, 128), :] = turned(head, q_gain_ref[...])
        return 0

    spread.first()
    spread.push(1, 0)
    spread.push(1, 1)
    arrived(pages_ref.at[pl.ds(0, few)], pool_sems.at[1, 0])
    arrived(pages_ref.at[pl.ds(0, few)], pool_sems.at[1, 1])
    pool_copies.append(pool_send(3, far_row * held, held, partner))
    lax.fori_loop(0, heads - 4, query, 0)
    spread.forward(1)
    project_out.forward(1)
    swap_forwarded(project_out, o_pair)
    spread.rest(1, None)
    project_out.rest(1, lambda r, d, h, piece: o_pair(r, d * 2 + h, piece))
    for copy in o_kept:
        copy.wait_recv()
    for copy in pool_copies[2:]:
        copy.wait_recv()
    gather.drain()
    spread.drain()
    project_out.drain()
    for copy in w_kept + o_kept + pool_copies:
        copy.wait_send()


def front(lengths, hidden, gain, shard, out_shard, pool, q_gain, k_gain, freqs):
    tokens, width = hidden.shape
    rows, columns = shard.shape
    vmem = pl.BlockSpec(memory_space=pltpu.VMEM)
    smem = pl.BlockSpec(memory_space=pltpu.SMEM)
    hbm = pl.BlockSpec(memory_space=pl.ANY)
    ring = pltpu.SemaphoreType.DMA((2, 2, 2, 3, 2))
    swap = pltpu.SemaphoreType.DMA((2, 2, 7))
    return pl.pallas_call(
        front_kernel,
        out_shape=(
            jax.ShapeDtypeStruct((2, 8 * tokens, 128), jnp.bfloat16),
            jax.ShapeDtypeStruct((4, 2, 4, tokens, 512), jnp.bfloat16),
            jax.ShapeDtypeStruct((tokens, 512), jnp.bfloat16),
            jax.ShapeDtypeStruct((4, 2, 4) + out_shard.shape, jnp.bfloat16),
            jax.ShapeDtypeStruct((4 * pool.shape[0],) + pool.shape[1:], jnp.bfloat16),
        ),
        in_specs=[smem] + [vmem] * 8,
        out_specs=(vmem, hbm, vmem, hbm, hbm),
        scratch_shapes=[
            pltpu.VMEM((4, 2, 4, rows, columns), jnp.bfloat16),
            pltpu.VMEM((tokens, columns), jnp.float32),
            pltpu.VMEM((tokens, width), jnp.bfloat16),
            ring,
            ring,
            ring,
            pltpu.SemaphoreType.DMA((3, 2)),
            swap,
            swap,
            pltpu.SemaphoreType.DMA((2, 4)),
            pltpu.SemaphoreType.DMA((3,)),
        ],
        compiler_params=pltpu.CompilerParams(
            collective_id=1, has_side_effects=True, vmem_limit_bytes=56 * 1024 * 1024
        ),
        cost_estimate=pl.CostEstimate(
            flops=1_400_000_000, bytes_accessed=200_000_000, transcendentals=1_000_000
        ),
    )(lengths, hidden, gain, shard, out_shard, pool, q_gain, k_gain, freqs)


def attention_kernel(
    table,
    lengths_ref,
    groups_ref,
    q_ref,
    hidden_ref,
    gain_ref,
    kv_hbm,
    pool_hbm,
    w_out_hbm,
    mid_ref,
    moe_ref,
    kv_ref,
    pool_ref,
    w_out_ref,
    mixed,
    high,
    total,
    acc,
    sems,
):
    f32, bf16 = jnp.float32, jnp.bfloat16
    loads = (
        pltpu.make_async_copy(pool_hbm, pool_ref, sems.at[0]),
        pltpu.make_async_copy(kv_hbm, kv_ref, sems.at[1]),
        pltpu.make_async_copy(w_out_hbm, w_out_ref, sems.at[2]),
    )
    for load in loads:
        load.start()
    row = lax.axis_index("dp")
    first = lax.axis_index("expert") * hidden_ref.shape[0]
    last = first + hidden_ref.shape[0] - 1
    index = first + lax.broadcasted_iota(jnp.int32, (1, 128), 1)
    start = jnp.zeros_like(index)
    group_of = jnp.zeros_like(index) + groups_ref[row, 0]
    earliest, latest = jnp.int32(0), jnp.int32(0)
    begin = jnp.int32(0)
    counts = [jnp.int32(0), jnp.int32(0)]
    for r in range(4):
        end = begin + lengths_ref[row, r]
        of = groups_ref[row, r]
        if r > 0:
            start = jnp.where(index >= begin, begin, start)
            group_of = jnp.where(index >= begin, of, group_of)
            earliest = jnp.where(first >= begin, begin, earliest)
            latest = jnp.where(last >= begin, begin, latest)
        inside = jnp.maximum(jnp.minimum(end, last + 1) - jnp.maximum(begin, first), 0)
        counts[0] += jnp.where(of == 0, inside, 0)
        counts[1] += jnp.where(of == 1, inside, 0)
        begin = end
    everyone = last - first + 1
    factor = math.log2(math.e) / math.sqrt(128)
    high[...] = jnp.full_like(high, floor_value)
    total[...] = jnp.zeros_like(total)
    acc[...] = jnp.zeros_like(acc)

    def step(h, keys, values, seen):
        scores = lax.dot_general(
            keys, q_ref[h], (((1,), (1,)), ((), ())), preferred_element_type=f32
        )
        if seen is not None:
            scores = jnp.where(jnp.concatenate([seen] * 8, axis=1), scores, -jnp.inf)
        old = high[h]
        new = jnp.maximum(old, jnp.max(scores, axis=0, keepdims=True))
        weights = jnp.exp2((scores - new) * factor)
        shrink = jnp.exp2((old - new) * factor)
        high[h] = new
        total[h] = total[h] * shrink + jnp.sum(weights, axis=0, keepdims=True)
        acc[h] = acc[h] * shrink + lax.dot_general(
            values, weights.astype(bf16), (((0,), (0,)), ((), ())), preferred_element_type=f32
        )

    span = 4
    loads[0].wait()
    for group in range(2):

        def pages(seen, group=group):
            def body(j, _):
                picked = [table[group * 16 + j * span + i] for i in range(span)]
                for h in range(2):
                    keys = jnp.concatenate([pool_ref[p, 0, h] for p in picked], axis=0)
                    values = jnp.concatenate([pool_ref[p, 1, h] for p in picked], axis=0)
                    step(h, keys, values, seen)
                return 0

            lax.fori_loop(0, 16 // span, body, 0)

        @pl.when(counts[group] == everyone)
        def _():
            pages(None)

        @pl.when((counts[group] > 0) & (counts[group] < everyone))
        def _():
            pages(jnp.broadcast_to(group_of == group, (span * 128, 128)))

    loads[1].wait()
    size = 256

    def suffix(tile, masked):
        at = pl.multiple_of(tile * size, size)
        seen = None
        if masked:
            place_of = at + lax.broadcasted_iota(jnp.int32, (size, 128), 0)
            seen = (place_of >= start) & (place_of <= index)
        for h in range(2):
            keys = kv_ref[pl.ds(at, size), h * 128 : (h + 1) * 128]
            values = kv_ref[pl.ds(at, size), 256 + h * 128 : 256 + (h + 1) * 128]
            step(h, keys, values, seen)

    def tiles(tile, _):
        clear = (tile * size >= latest) & (tile * size + size <= first + 1)

        @pl.when(clear)
        def _():
            suffix(tile, False)

        @pl.when(jnp.logical_not(clear))
        def _():
            suffix(tile, True)

        return 0

    lax.fori_loop(lax.div(earliest, size), lax.div(last, size) + 1, tiles, 0)
    for h in range(2):
        done = acc[h] / total[h]
        for g in range(8):
            head = h * 8 + g
            mixed[:, head * 128 : (head + 1) * 128] = (
                done[:, g * 128 : (g + 1) * 128].T.astype(bf16)
            )


    loads[2].wait()

    def project(tile, square):
        at = pl.multiple_of(tile * 512, 512)
        part = jnp.dot(mixed[...], w_out_ref[:, pl.ds(at, 512)], preferred_element_type=f32)
        mid = (hidden_ref[:, pl.ds(at, 512)].astype(f32) + part).astype(bf16)
        mid_ref[:, pl.ds(at, 512)] = mid
        mid = mid.astype(f32)
        return square + jnp.sum(mid * mid, axis=-1, keepdims=True)

    width = hidden_ref.shape[1]
    square = lax.fori_loop(0, width // 512, project, jnp.zeros((hidden_ref.shape[0], 1), f32))
    factor_of = lax.rsqrt(square / width + eps)
    moe_ref[...] = (mid_ref[...].astype(f32) * factor_of * gain_ref[...]).astype(bf16)


def attention(table, lengths, groups, q, hidden, gain, kv, pool, w_out):
    vmem = pl.BlockSpec(memory_space=pltpu.VMEM)
    smem = pl.BlockSpec(memory_space=pltpu.SMEM)
    hbm = pl.BlockSpec(memory_space=pl.ANY)
    tokens, width = hidden.shape
    row = jax.ShapeDtypeStruct((tokens, width), jnp.bfloat16)
    return pl.pallas_call(
        attention_kernel,
        out_shape=(row, row),
        in_specs=[smem] * 3 + [vmem] * 3 + [hbm] * 3,
        out_specs=(vmem, vmem),
        scratch_shapes=[
            pltpu.VMEM(kv.shape, jnp.bfloat16),
            pltpu.VMEM(pool.shape, jnp.bfloat16),
            pltpu.VMEM(w_out.shape, jnp.bfloat16),
            pltpu.VMEM((tokens, width), jnp.bfloat16),
            pltpu.VMEM((2, 1, 8 * tokens), jnp.float32),
            pltpu.VMEM((2, 1, 8 * tokens), jnp.float32),
            pltpu.VMEM((2, 128, 8 * tokens), jnp.float32),
            pltpu.SemaphoreType.DMA((3,)),
        ],
        compiler_params=pltpu.CompilerParams(vmem_limit_bytes=56 * 1024 * 1024),
        cost_estimate=pl.CostEstimate(
            flops=5_000_000_000, bytes_accessed=10_000_000, transcendentals=10_000_000
        ),
    )(table, lengths, groups, q, hidden, gain, kv, pool, w_out)


def local(
    hidden_in,
    attn_gain,
    query_key_value_weight,
    q_gain,
    key_norm_gain,
    w_out,
    moe_gain,
    w_gate_up,
    w_down,
    kv_pool,
    page_table,
    suffix_lengths,
    request_group,
    expert_ids,
    gate_weights,
):
    tokens_here, width = hidden_in.shape
    half = q_gain.shape[0] // 2
    freqs = theta ** (-jnp.arange(half, dtype=jnp.float32) / half)
    q, kv, suffix_cache, w_out_all, pool = front(
        suffix_lengths,
        hidden_in,
        attn_gain[None],
        query_key_value_weight,
        w_out,
        kv_pool.transpose(0, 1, 3, 2, 4),
        q_gain[None],
        key_norm_gain[None],
        jnp.concatenate([freqs, freqs])[None],
    )
    mid, moe_in = attention(
        page_table,
        suffix_lengths,
        request_group,
        q,
        hidden_in,
        moe_gain[None],
        kv.reshape(32 * tokens_here, 512),
        pool,
        w_out_all.reshape(32 * w_out.shape[0], width),
    )
    hidden_out = experts(moe_in, mid, expert_ids, gate_weights, w_gate_up[0], w_down[0])
    return (hidden_out, suffix_cache)


def solution(mesh):
    return jax.shard_map(
        local,
        mesh=mesh,
        in_specs=(
            P(("dp", "expert"), None),
            P(),
            P("expert", None),
            P(),
            P(),
            P("expert", None),
            P(),
            P(("dp", "expert"), None, None),
            P(("dp", "expert"), None, None),
            P("dp", None, None, None, None),
            P(),
            P(),
            P(),
            P(("dp", "expert"), None),
            P(("dp", "expert"), None),
        ),
        out_specs=(P(("dp", "expert"), None), P(("dp", "expert"), None)),
        check_vma=False,
    )
```

```python
import math

import jax
import jax.numpy as jnp
from jax import lax
from jax.experimental import pallas as pl
from jax.experimental.pallas import tpu as pltpu
from jax.sharding import PartitionSpec as P

PREFIX_TOKENS = 2048


eps = 1e-06
theta = 1000000.0
floor_value = -1e30


MESH_ID = pl.DeviceIdType.MESH
STEP = 1
PARTS = (0, 640, 1280, 2048)


def place():
    dp = lax.axis_index("dp")
    ex = lax.axis_index("expert")
    x = lax.rem(lax.div(ex, 4), 2) * 2 + lax.div(dp, 2)
    return (x, lax.div(ex, 8), lax.rem(ex, 4), lax.rem(dp, 2))


def device(x, y, z, c):
    return {"dp": lax.rem(x, 2) * 2 + c, "expert": y * 8 + lax.div(x, 2) * 4 + z}


def number(x, y, z, c):
    return (lax.rem(x, 2) * 2 + c) * 32 + y * 8 + lax.div(x, 2) * 4 + z


def greet_all(here):
    barrier = pltpu.get_barrier_semaphore()
    x, y, z, c = here

    def tell(k, _):
        there = (
            lax.rem(x + lax.div(k, 32), 4),
            lax.rem(y + lax.rem(lax.div(k, 8), 4), 4),
            lax.rem(z + lax.rem(lax.div(k, 2), 4), 4),
            lax.rem(c + k, 2),
        )
        pl.semaphore_signal(barrier, inc=1, device_id=device(*there), device_id_type=MESH_ID)
        return 0

    lax.fori_loop(1, 128, tell, 0)
    return barrier


def send(src, dst, send_sem, recv_sem, where):
    return pltpu.make_async_remote_copy(
        src_ref=src,
        dst_ref=dst,
        send_sem=send_sem,
        recv_sem=recv_sem,
        device_id=device(*where),
        device_id_type=MESH_ID,
    )


def part_columns(p):
    return slice(PARTS[p], PARTS[p + 1])


def in_plane(p, here):
    x, y, z, c = here
    return ((y, z), (z, x), (y, x))[p]


def at_plane(p, here, a, b, c):
    x, y, z, _ = here
    return ((x, a, b, c), (b, y, a, c), (b, a, z, c))[p]


def on_line(p, here, d):
    moved = list(here)
    moved[p] = lax.rem(here[p] + d, 4)
    return tuple(moved)


def moe_kernel(
    x_ref,
    mid_ref,
    info_ref,
    gate_up_hbm,
    down_hbm,
    out_ref,
    line,
    infos,
    pack_a,
    pack_b,
    recv_a,
    recv_b,
    home_a,
    home_b,
    rows,
    acts,
    partial,
    inbox,
    ranks,
    gates,
    gate_up,
    down,
    weight_sem,
    line_send,
    line_recv,
    info_send,
    info_recv,
    out_sem,
    in_sem,
    back_sem,
    home_sem,
    sum_send,
    sum_recv,
):
    f32, bf16 = jnp.float32, jnp.bfloat16
    ff = down.shape[0]
    here = place()
    c = here[3]
    load_gate_up = pltpu.make_async_copy(gate_up_hbm, gate_up, weight_sem.at[0])
    load_down = pltpu.make_async_copy(down_hbm, down, weight_sem.at[1])
    load_gate_up.start()
    load_down.start()
    barrier = greet_all(here)
    pl.semaphore_wait(barrier, 127)

    for p in range(3):
        own = here[p]
        pltpu.make_async_copy(info_ref, infos.at[p, own], info_recv.at[p]).start()
        for d in (1, 3, 2):
            send(
                info_ref, infos.at[p, own], info_send.at[p], info_recv.at[p], on_line(p, here, d)
            ).start()
    for d in (1, 3, 2):
        for p in range(3):
            cut = part_columns(p)
            send(
                x_ref.at[:, cut],
                line.at[here[p], :, cut],
                line_send.at[p],
                line_recv.at[p],
                on_line(p, here, d),
            ).start()
    for p in range(3):
        cut = part_columns(p)
        pltpu.make_async_copy(
            x_ref.at[:, cut], line.at[here[p], :, cut], line_recv.at[p]
        ).start()

    local = lax.broadcasted_iota(jnp.int32, (32, 128), 0)
    before = jnp.where(
        lax.broadcasted_iota(jnp.int32, (128, 128), 0)
        < lax.broadcasted_iota(jnp.int32, (128, 128), 1),
        1.0,
        0.0,
    ).astype(bf16)
    for p in range(3):
        arrived(infos.at[p], info_recv.at[p])
        expert = number(
            *at_plane(
                p,
                here,
                lax.rem(lax.div(local, 4), 4),
                lax.rem(local, 4),
                lax.div(local, 16),
            )
        ).astype(f32)
        for q in range(4):
            named = jnp.zeros((32, 128), f32)
            gate = jnp.zeros((32, 128), f32)
            for k in range(8):
                hit = infos[p, q, k : k + 1, :] == expert
                named += jnp.where(hit, 1.0, 0.0)
                gate += jnp.where(hit, infos[p, q, 8 + k : 9 + k, :], 0.0)
            rank = jnp.dot(named.astype(bf16), before, preferred_element_type=f32)
            ranks[p, q] = jnp.where(named > 0.5, rank, 99.0)
            gates[p, q] = gate

    def choice(p, q, low, count):
        rank = ranks[p, q]
        wanted = (low + lax.broadcasted_iota(jnp.int32, (32, count, 128), 1)).astype(f32)
        return jnp.where(rank[:, None, :] == wanted, 1.0, 0.0)

    halves = ((0, 8, pack_a, recv_a, home_a), (8, 4, pack_b, recv_b, home_b))

    def pack(half):
        low, count, packed, _, _ = halves[half]

        def body(q, _):
            for p in range(3):
                cut = part_columns(p)
                chosen = choice(p, q, low, count).reshape(32 * count, 128).astype(bf16)
                value = jnp.dot(chosen, line[q, :, cut], preferred_element_type=f32)
                packed[q, :, :, cut] = value.astype(bf16).reshape(32, count, cut.stop - cut.start)
            return 0

        lax.fori_loop(0, 4, body, 0)

    def bundle(ref, a, b, core, p):
        return ref.at[:, core * 16 + a * 4 + b, :, part_columns(p)]

    def spread(ref, p, x, y, z, core):
        cut = part_columns(p)
        if p == 0:
            return ref.at[:, core, y, z, :, cut]
        if p == 1:
            return ref.at[x, core, :, z, :, cut]
        return ref.at[x, core, y, :, :, cut]

    def visit(step):
        sign = 1 - 2 * c

        def body(k, _):
            o = lax.rem(k * STEP, 32)
            for p in range(3):
                a, b = in_plane(p, here)
                to_a = lax.rem(a + sign * lax.rem(lax.div(o, 4), 4) + 4, 4)
                to_b = lax.rem(b + sign * lax.rem(o, 4) + 4, 4)
                to_c = lax.rem(c + lax.div(o, 16), 2)
                step(p, to_a, to_b, to_c)
            return 0

        lax.fori_loop(1, 32, body, 0)

    def dispatch(src, dst, send_sem, recv_sem):
        def step(p, a, b, core):
            send(
                bundle(src, a, b, core, p),
                spread(dst, p, *here),
                send_sem.at[p],
                recv_sem.at[p],
                at_plane(p, here, a, b, core),
            ).start()

        visit(step)
        for p in range(3):
            a, b = in_plane(p, here)
            pltpu.make_async_copy(
                bundle(src, a, b, c, p), spread(dst, p, *here), recv_sem.at[p]
            ).start()

    def give_back(src, dst, send_sem, recv_sem):
        def step(p, a, b, core):
            own_a, own_b = in_plane(p, here)
            there = at_plane(p, here, a, b, core)
            send(
                spread(src, p, *there),
                bundle(dst, own_a, own_b, c, p),
                send_sem.at[p],
                recv_sem.at[p],
                there,
            ).start()

        visit(step)
        for p in range(3):
            a, b = in_plane(p, here)
            pltpu.make_async_copy(
                spread(src, p, *here), bundle(dst, a, b, c, p), recv_sem.at[p]
            ).start()

    for p in range(3):
        cut = part_columns(p)
        arrived(line.at[:, :, cut], line_recv.at[p])
    for half in range(2):
        low, count, packed, received, _ = halves[half]
        pack(half)
        dispatch(packed, received, out_sem.at[half], in_sem.at[half])
    load_gate_up.wait()
    load_down.wait()

    def others(ref, p):
        return ref.at[:, pl.ds(0, 31), :, part_columns(p)]

    for half in range(2):
        low, count, packed, received, home = halves[half]
        total = 128 * count
        for p in range(3):
            whole = packed.at[:, :, :, part_columns(p)]
            arrived(whole, in_sem.at[half, p])
        rows[:total, :] = received[...].reshape(total, rows.shape[1])

        def up(tile, _):
            at = pl.multiple_of(tile * 256, 256)
            values = rows[:total, :]
            first = jnp.dot(values, gate_up[:, pl.ds(at, 256)], preferred_element_type=f32)
            second = jnp.dot(values, gate_up[:, pl.ds(ff + at, 256)], preferred_element_type=f32)
            acts[:total, pl.ds(at, 256)] = (jax.nn.silu(first) * second).astype(bf16)
            return 0

        lax.fori_loop(0, ff // 256, up, 0)

        def lower(tile, _):
            at = pl.multiple_of(tile * 256, 256)
            value = jnp.dot(
                acts[:total, :], down[:, pl.ds(at, 256)], preferred_element_type=f32
            ).astype(bf16)
            received[:, :, :, :, :, pl.ds(at, 256)] = value.reshape(4, 2, 4, 4, count, 256)
            return 0

        lax.fori_loop(0, rows.shape[1] // 256, lower, 0)
        give_back(received, home, back_sem.at[half], home_sem.at[half])

    over_rows = (((0,), (0,)), ((), ()))
    for half in range(2):
        low, count, packed, received, home = halves[half]
        for p in range(3):
            arrived(home.at[:, :, :, part_columns(p)], home_sem.at[half, p])

        def combine(d, _):
            for p in range(3):
                q = lax.rem(here[p] + d, 4)
                at = pl.ds(pl.multiple_of(q * 128, 128), 128)
                cut = part_columns(p)
                exact = choice(p, q, low, count) * gates[p, q][:, None, :]
                exact = exact.reshape(32 * count, 128)
                coarse = exact.astype(bf16)
                fine = (exact - coarse.astype(f32)).astype(bf16)
                values = home[q, :, :, cut].reshape(32 * count, cut.stop - cut.start)
                value = lax.dot_general(
                    coarse, values, over_rows, preferred_element_type=f32
                ) + lax.dot_general(fine, values, over_rows, preferred_element_type=f32)
                if half == 0:
                    partial[at, cut] = value
                else:
                    value += partial[at, cut]
                    partial[at, cut] = value
                    rows[at, cut] = value.astype(bf16)
            if half == 1:

                @pl.when(d < 4)
                def _():
                    for p in range(3):
                        cut = part_columns(p)
                        there = on_line(p, here, d)
                        send(
                            rows.at[pl.ds(pl.multiple_of(there[p] * 128, 128), 128), cut],
                            inbox.at[here[p], :, cut],
                            sum_send.at[p],
                            sum_recv.at[p],
                            there,
                        ).start()

            return 0

        lax.fori_loop(1, 5, combine, 0)

    for p in range(3):
        cut = part_columns(p)
        arrived(inbox.at[pl.ds(0, 3), :, cut], sum_recv.at[p])
        total = partial[pl.ds(pl.multiple_of(here[p] * 128, 128), 128), cut]
        for d in range(1, 4):
            total += inbox[lax.rem(here[p] + d, 4), :, cut].astype(f32)
        out_ref[:, cut] = (mid_ref[:, cut].astype(f32) + total).astype(bf16)

    for p in range(3):
        cut = part_columns(p)
        arrived(infos.at[p, pl.ds(0, 3)], info_send.at[p])
        arrived(inbox.at[pl.ds(0, 3), :, cut], line_send.at[p])
        arrived(inbox.at[pl.ds(0, 3), :, cut], sum_send.at[p])
        for half in range(2):
            arrived(others(halves[half][2], p), out_sem.at[half, p])
            arrived(others(halves[half][2], p), back_sem.at[half, p])


def experts(moe_in, mid, ids, gates, gate_up, down):
    tokens, width = moe_in.shape
    ff = down.shape[0]
    bf16 = jnp.bfloat16
    vmem = pl.BlockSpec(memory_space=pltpu.VMEM)
    hbm = pl.BlockSpec(memory_space=pl.ANY)
    flat_a, flat_b = (pltpu.VMEM((4, 32, n, width), bf16) for n in (8, 4))
    wide_a, wide_b = (pltpu.VMEM((4, 2, 4, 4, n, width), bf16) for n in (8, 4))
    three = pltpu.SemaphoreType.DMA((3,))
    six = pltpu.SemaphoreType.DMA((2, 3))
    info = jnp.concatenate([ids.T.astype(jnp.float32), gates.T], axis=0)
    return pl.pallas_call(
        moe_kernel,
        out_shape=jax.ShapeDtypeStruct((tokens, width), bf16),
        in_specs=[vmem] * 3 + [hbm] * 2,
        out_specs=vmem,
        scratch_shapes=[
            pltpu.VMEM((4, tokens, width), bf16),
            pltpu.VMEM((3, 4, 16, tokens), jnp.float32),
            flat_a,
            flat_b,
            wide_a,
            wide_b,
            flat_a,
            flat_b,
            pltpu.VMEM((1024, width), bf16),
            pltpu.VMEM((1024, ff), bf16),
            pltpu.VMEM((512, width), jnp.float32),
            pltpu.VMEM((4, tokens, width), bf16),
            pltpu.VMEM((3, 4, 32, tokens), jnp.float32),
            pltpu.VMEM((3, 4, 32, tokens), jnp.float32),
            pltpu.VMEM((width, 2 * ff), bf16),
            pltpu.VMEM((ff, width), bf16),
            pltpu.SemaphoreType.DMA((2,)),
            three,
            three,
            three,
            three,
            six,
            six,
            six,
            six,
            three,
            three,
        ],
        compiler_params=pltpu.CompilerParams(
            collective_id=3, has_side_effects=True, vmem_limit_bytes=63 * 1024 * 1024
        ),
        cost_estimate=pl.CostEstimate(
            flops=20_000_000_000, bytes_accessed=400_000_000, transcendentals=1_000_000
        ),
    )(moe_in, mid, info, gate_up, down)


def arrived(ref, sem):
    pltpu.make_async_copy(ref, ref, sem).wait()


class Gather:
    def __init__(self, buf, here, cross, columns, sems):
        self.buf, self.here, self.cross, self.columns = buf, here, cross, columns
        self.send_sem, self.recv_sem, self.cross_sem = sems

    def cut(self, r):
        start, size = self.columns[r]
        return pl.ds(pl.multiple_of(start, 128), size)

    def whole(self, h):
        x, y, z, c = self.here
        start, size = self.columns[0]
        return self.buf.at[y, h, z, :, pl.ds(pl.multiple_of(start, 128), size + self.columns[1][1])]

    def near(self, r):
        x, y, z, c = self.here
        cut = self.cut(r)
        if r == 0:
            return lambda p, h: self.buf.at[y, h, p, :, cut]
        return lambda p, h: self.buf.at[p, h, z, :, cut]

    def far(self, r):
        cut = self.cut(r)
        if r == 0:
            return lambda p, h: self.buf.at[p, h, :, :, cut]
        return lambda p, h: self.buf.at[:, h, p, :, cut]

    def ring(self, r, phase):
        x, y, z, c = self.here
        if (r + phase) % 2 == 0:
            return z, (x, y, lax.rem(z + 1, 4), c), (x, y, lax.rem(z + 3, 4), c)
        return y, (x, lax.rem(y + 1, 4), z, c), (x, lax.rem(y + 3, 4), z, c)

    def start(self):
        own = lax.div(self.here[0], 2)
        send(
            self.whole(own), self.whole(own), self.cross_sem.at[0], self.cross_sem.at[1], self.cross
        ).start()
        self.push(0, own)

    def push(self, phase, h):
        for r in range(2):
            pick = (self.near if phase == 0 else self.far)(r)
            pos, right, left = self.ring(r, phase)
            piece = pick(pos, h)
            for d, there in enumerate((right, left)):
                send(
                    piece,
                    piece,
                    self.send_sem.at[r, phase, d, h],
                    self.recv_sem.at[r, phase, d, h],
                    there,
                ).start()

    def first(self):
        own = lax.div(self.here[0], 2)
        arrived(self.whole(1 - own), self.cross_sem.at[1])
        self.push(0, 1 - own)
        self.forward(0)
        self.rest(0, None)

    def forward(self, phase):
        for d in range(2):
            for r in range(2):
                pick = (self.near if phase == 0 else self.far)(r)
                pos, right, left = self.ring(r, phase)
                arrived(pick(pos, d), self.recv_sem.at[r, phase, d, d])
                piece = pick(lax.rem(pos + (3 if d == 0 else 1), 4), d)
                send(
                    piece,
                    piece,
                    self.send_sem.at[r, phase, 2, d],
                    self.recv_sem.at[r, phase, 2, d],
                    right if d == 0 else left,
                ).start()

    def rest(self, phase, seen):
        for d, h in ((0, 1), (1, 0), (2, 0), (2, 1)):
            for r in range(2):
                pick = (self.near if phase == 0 else self.far)(r)
                pos, _, _ = self.ring(r, phase)
                arrived(pick(pos, h), self.recv_sem.at[r, phase, d, h])
                if seen is not None:
                    seen(r, d, h, pick(lax.rem(pos + (3, 1, 2)[d], 4), h))

    def second(self, seen=None):
        self.push(1, 0)
        self.push(1, 1)
        self.forward(1)
        if seen is not None:
            for d in range(2):
                for r in range(2):
                    pos, _, _ = self.ring(r, 1)
                    seen(r, d, d, self.far(r)(lax.rem(pos + (3, 1)[d], 4), d))
        self.rest(1, seen)

    def drain(self):
        arrived(self.whole(0), self.cross_sem.at[0])
        for r in range(2):
            for phase in range(2):
                pick = (self.near if phase == 0 else self.far)(r)
                for d in range(3):
                    for h in range(2):
                        arrived(pick(0, h), self.send_sem.at[r, phase, d, h])


def request_bounds(lengths_ref, row):
    ends = [lengths_ref[row, 0]]
    for r in range(1, 3):
        ends.append(ends[-1] + lengths_ref[row, r])
    return ends


def front_kernel(
    lengths_ref,
    hidden_ref,
    gain_ref,
    shard_ref,
    out_shard_ref,
    pool_ref,
    q_gain_ref,
    k_gain_ref,
    freq_ref,
    q_ref,
    kv_ref,
    cache_ref,
    w_out_ref,
    pages_ref,
    weight,
    qkv,
    normed_ref,
    w_sems,
    k_sems,
    o_sems,
    cross_sems,
    w_swap,
    o_swap,
    pool_sems,
    local_sem,
):
    f32, bf16 = jnp.float32, jnp.bfloat16
    here = place()
    x, y, z, c = here
    own = lax.div(x, 2)
    columns = weight.shape[-1]
    side = columns // 2
    partner = (x, y, z, 1 - c)
    even = 1 - lax.rem(x, 2)
    across = (lax.rem(x + 1 + 2 * even, 4), y, z, c)
    opposite = (lax.rem(x + 2, 4), y, z, c)
    upper = (lax.rem(x + 1, 4), y, z, c)
    lower = (lax.rem(x + 3, 4), y, z, c)
    barrier = pltpu.get_barrier_semaphore()
    peers = (
        partner,
        opposite,
        upper,
        lower,
        (x, lax.rem(y + 1, 4), z, c),
        (x, lax.rem(y + 3, 4), z, c),
        (x, y, lax.rem(z + 1, 4), c),
        (x, y, lax.rem(z + 3, 4), c),
    )
    for peer in peers:
        pl.semaphore_signal(barrier, inc=1, device_id=device(*peer), device_id_type=MESH_ID)
    out_side = w_out_ref.shape[-1] // 2
    mine = pl.ds(pl.multiple_of(c * side, 128), side)
    mine_out = pl.ds(pl.multiple_of(c * out_side, 128), out_side)
    held = pool_ref.shape[0]
    row = lax.rem(x, 2) * 2 + c
    seeds = (
        pltpu.make_async_copy(
            shard_ref.at[:, mine], weight.at[y, own, z, :, mine], local_sem.at[0]
        ),
        pltpu.make_async_copy(
            out_shard_ref.at[:, mine_out], w_out_ref.at[y, own, z, :, mine_out], local_sem.at[1]
        ),
        pltpu.make_async_copy(pool_ref, pages_ref.at[pl.ds(row * held, held)], local_sem.at[2]),
    )
    for seed in seeds:
        seed.start()
    seeds[0].wait()
    pl.semaphore_wait(barrier, len(peers))

    gather = Gather(
        weight,
        here,
        across,
        ((c * side, side // 2), (c * side + side // 2, side // 2)),
        (w_sems.at[0], w_sems.at[1], cross_sems.at[0]),
    )
    gather.start()
    seeds[1].wait()
    seeds[2].wait()
    project_out = Gather(
        w_out_ref,
        here,
        across,
        ((c * out_side, out_side // 2), (c * out_side + out_side // 2, out_side // 2)),
        (o_sems.at[0], o_sems.at[1], cross_sems.at[1]),
    )

    def pool_send(slot, first, count, there):
        piece = pages_ref.at[pl.ds(first, count)]
        copy = send(piece, piece, pool_sems.at[0, slot], pool_sems.at[1, slot], there)
        copy.start()
        return copy

    few = held // 2
    far_row = (1 - lax.rem(x, 2)) * 2 + c
    pool_copies = [
        pool_send(0, row * held, few, upper),
        pool_send(1, row * held + few, few, lower),
        pool_send(2, row * held, held, partner),
    ]

    value = hidden_ref[...].astype(f32)
    mean = jnp.mean(value * value, axis=-1, keepdims=True)
    normed_ref[...] = (value * lax.rsqrt(mean + eps) * gain_ref[...]).astype(bf16)

    gather.first()

    def swapper(sems, kept):
        def swap(r, slot, piece):
            copy = send(piece, piece, sems.at[0, r, slot], sems.at[1, r, slot], partner)
            copy.start()
            kept.append(copy)

        return swap

    def swap_near(target, ref, swap):
        for r in range(2):
            pos, _, _ = target.ring(r, 1)
            cut = target.cut(r)
            swap(r, 6, ref.at[pos, :, :, :, cut] if r == 0 else ref.at[:, :, pos, :, cut])

    def swap_forwarded(target, swap):
        for d in range(2):
            for r in range(2):
                pos, _, _ = target.ring(r, 1)
                swap(r, d * 2 + d, target.far(r)(lax.rem(pos + (3, 1)[d], 4), d))

    w_kept, o_kept = [], []
    w_pair = swapper(w_swap, w_kept)
    o_pair = swapper(o_swap, o_kept)
    gather.push(1, 0)
    gather.push(1, 1)
    swap_near(gather, weight, w_pair)
    project_out.start()
    gather.forward(1)
    swap_forwarded(gather, w_pair)
    gather.rest(1, lambda r, d, h, piece: w_pair(r, d * 2 + h, piece))
    project_out.first()
    project_out.push(1, 0)
    for copy in w_kept:
        copy.wait_recv()
    swap_near(project_out, w_out_ref, o_pair)

    span = 2 * 4 * weight.shape[3]

    def project(tile, _):
        at = pl.multiple_of(tile * 512, 512)
        total = jnp.zeros((normed_ref.shape[0], 512), f32)
        for plane in range(4):
            block = weight[plane, :, :, :, pl.ds(at, 512)].reshape(span, 512)
            total += jnp.dot(
                normed_ref[:, plane * span : (plane + 1) * span],
                block,
                preferred_element_type=f32,
            )
        qkv[:, pl.ds(at, 512)] = total
        return 0

    tokens = hidden_ref.shape[0]
    index = (y * 8 + own * 4 + z) * tokens + lax.broadcasted_iota(jnp.int32, (tokens, 128), 0)
    start = jnp.zeros_like(index)
    for end in request_bounds(lengths_ref, row):
        start = jnp.where(index >= end, end, start)
    angles = (PREFIX_TOKENS + index - start).astype(f32) * freq_ref[...]
    cosine = jnp.cos(angles)
    sine = jnp.sin(angles)
    lane = lax.broadcasted_iota(jnp.int32, (tokens, 128), 1)
    sine = jnp.where(lane < 64, -sine, sine)
    heads = columns // 128

    def turned(head, gain):
        rows = qkv[:, pl.ds(pl.multiple_of(head * 128, 128), 128)]
        mean = jnp.mean(rows * rows, axis=-1, keepdims=True)
        rows = rows * lax.rsqrt(mean + eps) * gain
        return (rows * cosine + pltpu.roll(rows, 64, 1) * sine).astype(bf16)

    project(columns // 512 - 1, 0)
    for h in range(2):
        cache_ref[:, h * 128 : (h + 1) * 128] = turned(heads - 4 + h, k_gain_ref[...])
    cache_ref[:, 256:512] = qkv[:, columns - 256 :].astype(bf16)
    seed = pltpu.make_async_copy(cache_ref, kv_ref.at[y, own, z], local_sem.at[0])
    seed.start()
    seed.wait()
    spread = Gather(
        kv_ref,
        here,
        opposite,
        ((0, 256), (256, 256)),
        (k_sems.at[0], k_sems.at[1], cross_sems.at[2]),
    )
    spread.start()
    lax.fori_loop(0, columns // 512 - 1, project, 0)

    def query(head, _):
        at = pl.multiple_of(lax.rem(head, 8) * 128, 128)
        q_ref[lax.div(head, 8), pl.ds(at, 128), :] = turned(head, q_gain_ref[...])
        return 0

    spread.first()
    spread.push(1, 0)
    spread.push(1, 1)
    project_out.push(1, 1)
    arrived(pages_ref.at[pl.ds(0, few)], pool_sems.at[1, 0])
    arrived(pages_ref.at[pl.ds(0, few)], pool_sems.at[1, 1])
    pool_copies.append(pool_send(3, far_row * held, held, partner))
    lax.fori_loop(0, heads - 4, query, 0)
    spread.forward(1)
    project_out.forward(1)
    swap_forwarded(project_out, o_pair)
    spread.rest(1, None)
    project_out.rest(1, lambda r, d, h, piece: o_pair(r, d * 2 + h, piece))
    for copy in o_kept:
        copy.wait_recv()
    for copy in pool_copies[2:]:
        copy.wait_recv()
    gather.drain()
    spread.drain()
    project_out.drain()
    for copy in w_kept + o_kept + pool_copies:
        copy.wait_send()


def front(lengths, hidden, gain, shard, out_shard, pool, q_gain, k_gain, freqs):
    tokens, width = hidden.shape
    rows, columns = shard.shape
    vmem = pl.BlockSpec(memory_space=pltpu.VMEM)
    smem = pl.BlockSpec(memory_space=pltpu.SMEM)
    hbm = pl.BlockSpec(memory_space=pl.ANY)
    ring = pltpu.SemaphoreType.DMA((2, 2, 2, 3, 2))
    swap = pltpu.SemaphoreType.DMA((2, 2, 7))
    return pl.pallas_call(
        front_kernel,
        out_shape=(
            jax.ShapeDtypeStruct((2, 8 * tokens, 128), jnp.bfloat16),
            jax.ShapeDtypeStruct((4, 2, 4, tokens, 512), jnp.bfloat16),
            jax.ShapeDtypeStruct((tokens, 512), jnp.bfloat16),
            jax.ShapeDtypeStruct((4, 2, 4) + out_shard.shape, jnp.bfloat16),
            jax.ShapeDtypeStruct((4 * pool.shape[0],) + pool.shape[1:], jnp.bfloat16),
        ),
        in_specs=[smem] + [vmem] * 8,
        out_specs=(vmem, hbm, vmem, hbm, hbm),
        scratch_shapes=[
            pltpu.VMEM((4, 2, 4, rows, columns), jnp.bfloat16),
            pltpu.VMEM((tokens, columns), jnp.float32),
            pltpu.VMEM((tokens, width), jnp.bfloat16),
            ring,
            ring,
            ring,
            pltpu.SemaphoreType.DMA((3, 2)),
            swap,
            swap,
            pltpu.SemaphoreType.DMA((2, 4)),
            pltpu.SemaphoreType.DMA((3,)),
        ],
        compiler_params=pltpu.CompilerParams(
            collective_id=1, has_side_effects=True, vmem_limit_bytes=56 * 1024 * 1024
        ),
        cost_estimate=pl.CostEstimate(
            flops=1_400_000_000, bytes_accessed=200_000_000, transcendentals=1_000_000
        ),
    )(lengths, hidden, gain, shard, out_shard, pool, q_gain, k_gain, freqs)


def attention_kernel(
    table,
    lengths_ref,
    groups_ref,
    q_ref,
    hidden_ref,
    gain_ref,
    kv_hbm,
    pool_hbm,
    w_out_hbm,
    mid_ref,
    moe_ref,
    kv_ref,
    pool_ref,
    w_out_ref,
    mixed,
    high,
    total,
    acc,
    sems,
):
    f32, bf16 = jnp.float32, jnp.bfloat16
    loads = (
        pltpu.make_async_copy(pool_hbm, pool_ref, sems.at[0]),
        pltpu.make_async_copy(kv_hbm, kv_ref, sems.at[1]),
        pltpu.make_async_copy(w_out_hbm, w_out_ref, sems.at[2]),
    )
    for load in loads:
        load.start()
    row = lax.axis_index("dp")
    first = lax.axis_index("expert") * hidden_ref.shape[0]
    last = first + hidden_ref.shape[0] - 1
    index = first + lax.broadcasted_iota(jnp.int32, (1, 128), 1)
    start = jnp.zeros_like(index)
    group_of = jnp.zeros_like(index) + groups_ref[row, 0]
    earliest, latest = jnp.int32(0), jnp.int32(0)
    begin = jnp.int32(0)
    counts = [jnp.int32(0), jnp.int32(0)]
    for r in range(4):
        end = begin + lengths_ref[row, r]
        of = groups_ref[row, r]
        if r > 0:
            start = jnp.where(index >= begin, begin, start)
            group_of = jnp.where(index >= begin, of, group_of)
            earliest = jnp.where(first >= begin, begin, earliest)
            latest = jnp.where(last >= begin, begin, latest)
        inside = jnp.maximum(jnp.minimum(end, last + 1) - jnp.maximum(begin, first), 0)
        counts[0] += jnp.where(of == 0, inside, 0)
        counts[1] += jnp.where(of == 1, inside, 0)
        begin = end
    everyone = last - first + 1
    factor = math.log2(math.e) / math.sqrt(128)
    high[...] = jnp.full_like(high, floor_value)
    total[...] = jnp.zeros_like(total)
    acc[...] = jnp.zeros_like(acc)

    def step(h, keys, values, seen):
        scores = lax.dot_general(
            keys, q_ref[h], (((1,), (1,)), ((), ())), preferred_element_type=f32
        )
        if seen is not None:
            scores = jnp.where(jnp.concatenate([seen] * 8, axis=1), scores, -jnp.inf)
        old = high[h]
        new = jnp.maximum(old, jnp.max(scores, axis=0, keepdims=True))
        weights = jnp.exp2((scores - new) * factor)
        shrink = jnp.exp2((old - new) * factor)
        high[h] = new
        total[h] = total[h] * shrink + jnp.sum(weights, axis=0, keepdims=True)
        acc[h] = acc[h] * shrink + lax.dot_general(
            values, weights.astype(bf16), (((0,), (0,)), ((), ())), preferred_element_type=f32
        )

    span = 4
    loads[0].wait()
    for group in range(2):

        def pages(seen, group=group):
            def body(j, _):
                picked = [table[group * 16 + j * span + i] for i in range(span)]
                for h in range(2):
                    keys = jnp.concatenate([pool_ref[p, 0, h] for p in picked], axis=0)
                    values = jnp.concatenate([pool_ref[p, 1, h] for p in picked], axis=0)
                    step(h, keys, values, seen)
                return 0

            lax.fori_loop(0, 16 // span, body, 0)

        @pl.when(counts[group] == everyone)
        def _():
            pages(None)

        @pl.when((counts[group] > 0) & (counts[group] < everyone))
        def _():
            pages(jnp.broadcast_to(group_of == group, (span * 128, 128)))

    loads[1].wait()
    size = 256

    def suffix(tile, masked):
        at = pl.multiple_of(tile * size, size)
        seen = None
        if masked:
            place_of = at + lax.broadcasted_iota(jnp.int32, (size, 128), 0)
            seen = (place_of >= start) & (place_of <= index)
        for h in range(2):
            keys = kv_ref[pl.ds(at, size), h * 128 : (h + 1) * 128]
            values = kv_ref[pl.ds(at, size), 256 + h * 128 : 256 + (h + 1) * 128]
            step(h, keys, values, seen)

    def tiles(tile, _):
        clear = (tile * size >= latest) & (tile * size + size <= first + 1)

        @pl.when(clear)
        def _():
            suffix(tile, False)

        @pl.when(jnp.logical_not(clear))
        def _():
            suffix(tile, True)

        return 0

    lax.fori_loop(lax.div(earliest, size), lax.div(last, size) + 1, tiles, 0)
    for h in range(2):
        done = acc[h] / total[h]
        for g in range(8):
            head = h * 8 + g
            mixed[:, head * 128 : (head + 1) * 128] = (
                done[:, g * 128 : (g + 1) * 128].T.astype(bf16)
            )


    loads[2].wait()

    def project(tile, square):
        at = pl.multiple_of(tile * 512, 512)
        part = jnp.dot(mixed[...], w_out_ref[:, pl.ds(at, 512)], preferred_element_type=f32)
        mid = (hidden_ref[:, pl.ds(at, 512)].astype(f32) + part).astype(bf16)
        mid_ref[:, pl.ds(at, 512)] = mid
        mid = mid.astype(f32)
        return square + jnp.sum(mid * mid, axis=-1, keepdims=True)

    width = hidden_ref.shape[1]
    square = lax.fori_loop(0, width // 512, project, jnp.zeros((hidden_ref.shape[0], 1), f32))
    factor_of = lax.rsqrt(square / width + eps)
    moe_ref[...] = (mid_ref[...].astype(f32) * factor_of * gain_ref[...]).astype(bf16)


def attention(table, lengths, groups, q, hidden, gain, kv, pool, w_out):
    vmem = pl.BlockSpec(memory_space=pltpu.VMEM)
    smem = pl.BlockSpec(memory_space=pltpu.SMEM)
    hbm = pl.BlockSpec(memory_space=pl.ANY)
    tokens, width = hidden.shape
    row = jax.ShapeDtypeStruct((tokens, width), jnp.bfloat16)
    return pl.pallas_call(
        attention_kernel,
        out_shape=(row, row),
        in_specs=[smem] * 3 + [vmem] * 3 + [hbm] * 3,
        out_specs=(vmem, vmem),
        scratch_shapes=[
            pltpu.VMEM(kv.shape, jnp.bfloat16),
            pltpu.VMEM(pool.shape, jnp.bfloat16),
            pltpu.VMEM(w_out.shape, jnp.bfloat16),
            pltpu.VMEM((tokens, width), jnp.bfloat16),
            pltpu.VMEM((2, 1, 8 * tokens), jnp.float32),
            pltpu.VMEM((2, 1, 8 * tokens), jnp.float32),
            pltpu.VMEM((2, 128, 8 * tokens), jnp.float32),
            pltpu.SemaphoreType.DMA((3,)),
        ],
        compiler_params=pltpu.CompilerParams(vmem_limit_bytes=56 * 1024 * 1024),
        cost_estimate=pl.CostEstimate(
            flops=5_000_000_000, bytes_accessed=10_000_000, transcendentals=10_000_000
        ),
    )(table, lengths, groups, q, hidden, gain, kv, pool, w_out)


def local(
    hidden_in,
    attn_gain,
    query_key_value_weight,
    q_gain,
    key_norm_gain,
    w_out,
    moe_gain,
    w_gate_up,
    w_down,
    kv_pool,
    page_table,
    suffix_lengths,
    request_group,
    expert_ids,
    gate_weights,
):
    tokens_here, width = hidden_in.shape
    half = q_gain.shape[0] // 2
    freqs = theta ** (-jnp.arange(half, dtype=jnp.float32) / half)
    q, kv, suffix_cache, w_out_all, pool = front(
        suffix_lengths,
        hidden_in,
        attn_gain[None],
        query_key_value_weight,
        w_out,
        kv_pool.transpose(0, 1, 3, 2, 4),
        q_gain[None],
        key_norm_gain[None],
        jnp.concatenate([freqs, freqs])[None],
    )
    mid, moe_in = attention(
        page_table,
        suffix_lengths,
        request_group,
        q,
        hidden_in,
        moe_gain[None],
        kv.reshape(32 * tokens_here, 512),
        pool,
        w_out_all.reshape(32 * w_out.shape[0], width),
    )
    hidden_out = experts(moe_in, mid, expert_ids, gate_weights, w_gate_up[0], w_down[0])
    return (hidden_out, suffix_cache)


def solution(mesh):
    return jax.shard_map(
        local,
        mesh=mesh,
        in_specs=(
            P(("dp", "expert"), None),
            P(),
            P("expert", None),
            P(),
            P(),
            P("expert", None),
            P(),
            P(("dp", "expert"), None, None),
            P(("dp", "expert"), None, None),
            P("dp", None, None, None, None),
            P(),
            P(),
            P(),
            P(("dp", "expert"), None),
            P(("dp", "expert"), None),
        ),
        out_specs=(P(("dp", "expert"), None), P(("dp", "expert"), None)),
        check_vma=False,
    )
```
